32 devices in a mesh: ctx: 8 (over z, x), ch: 4 (over y, core).
Axes of the slice: x: 2, y: 2, z: 4, core: 2. Of those that a mesh axis runs over, the one named last changes fastest.
Arguments:
- query_proj: bfloat16 [2, 2048, 4096], P(None, 'ctx', 'ch'), may hold values from -6 to 6
- key_proj: bfloat16 [2, 2048, 4096], P(None, 'ctx', 'ch'), may hold values from -6 to 6
- value_proj: bfloat16 [2, 2048, 4096], P(None, 'ctx', 'ch'), may hold values from -6 to 6
- filter_taps: float32 [2048, 4096], P('ctx', 'ch'), may hold values from -6 to 6
- skip_gain: float32 [4096], P('ch'), may hold values from -3 to 3
- out_weight: bfloat16 [4096, 4096], P('ch', 'ctx'), may hold values from -0.09375 to 0.09375
- drop_seed: int32 [1], replicated, may hold values from 0 to 16777215
- drop_step: int32 [1], replicated, may hold values from 0 to 16777215
- offsets: int32 [2, 2048], P(None, 'ctx'), may hold values from 0 to 16777215
Outputs:
- block_out: bfloat16 [2, 2048, 4096], P(None, 'ctx', 'ch')
The draws below stay inside these ranges and needn't reach their ends.
All inputs are finite; a program needn't handle non-finite values.
Results may differ from the reference program's by a relative error of at most 0.0064.
Values may be sent and summed in bfloat16 or wider, within the bound.
No kernel may reach another device: no remote copies, remote signals or barrier semaphores. Data moves between devices by JAX's collectives and lax.ppermute only.
A program may use at most 128 MiB of HBM per device.

```python
import math
import jax
import jax.numpy as jnp
from jax import lax

D = 4096
SEQS = 2
SEQ_LEN = 2048


def draw_filter_taps(key, part):
    noise_key, pick_key, fast_key, slow_key = jax.random.split(key, 4)
    noise_field = jnp.clip(jax.random.normal(noise_key, (SEQ_LEN, D), jnp.float32), -6.0, 6.0)
    slow_share = 0.5
    slow_flags = jax.random.uniform(pick_key, (D,), jnp.float32) < slow_share
    fast_rate = jnp.exp(-jax.random.uniform(fast_key, (D,), jnp.float32, math.log(30.0), math.log(50.0)))
    slow_rate = jax.random.uniform(slow_key, (D,), jnp.float32, 0.2, 2.0) / SEQ_LEN
    decay_rate = jnp.where(slow_flags, slow_rate, fast_rate)
    positions = jnp.arange(SEQ_LEN, dtype=jnp.float32)[:, None]
    envelope = jnp.exp(-positions * decay_rate[None, :])
    norm_factor = jnp.sqrt((1.0 - jnp.exp(-2.0 * decay_rate)) / (1.0 - jnp.exp(-2.0 * decay_rate * SEQ_LEN)))
    return noise_field * envelope * norm_factor[None, :]


def with_ends(values, rng, least, largest):
    place = [jax.random.randint(jax.random.fold_in(rng, axis), (), 0, length) for axis, length in enumerate(values.shape)]
    widest = values.shape.index(max(values.shape))
    next_to = place[:widest] + [(place[widest] + 1) % values.shape[widest]] + place[widest + 1:]
    return values.at[tuple(place)].set(least).at[tuple(next_to)].set(largest)


def block_scale(rng, shape, cuts, smallest, top_value):
    def one(position, shards_of):
        draws = jax.random.uniform(jax.random.fold_in(jax.random.fold_in(rng, 6), position), (shards_of,), jnp.float32, smallest / len(cuts), top_value / len(cuts))
        return jnp.repeat(jnp.exp(draws), shape[position] // shards_of).reshape((-1,) + (1,) * (len(shape) - position - 1))

    level = one(*cuts[0])
    for cut in cuts[1:]:
        level = level * one(*cut)
    return level


def scatter_about(rng, shape, width, limit, cuts=(), kind=jnp.bfloat16):
    values = width * jax.random.normal(rng, shape, jnp.float32)
    if cuts:
        values = values * block_scale(rng, shape, cuts, -0.22, 0.18)
    return jnp.clip(values, -limit, limit).astype(kind)


def setup_inputs(seed: int = 0) -> dict:
    keys = jax.random.split(jax.random.key(seed), 10)
    query_proj = scatter_about(keys[0], (SEQS, SEQ_LEN, D), 1.0, 6.0, ((1, 8), (2, 4)))
    key_proj = scatter_about(keys[1], (SEQS, SEQ_LEN, D), 1.0, 6.0, ((1, 8), (2, 4)))
    value_proj = scatter_about(keys[2], (SEQS, SEQ_LEN, D), 1.0, 6.0, ((1, 8), (2, 4)))
    filter_taps = draw_filter_taps(jax.random.fold_in(keys[9], 71), 0)
    skip_gain = scatter_about(keys[4], (D,), 1.0, 3.0, ((0, 4),), jnp.float32)
    out_weight = scatter_about(keys[5], (D, D), D ** -0.5, 0.09375, ((0, 4), (1, 8)))
    drop_seed = jax.random.randint(keys[6], (1,), 0, 16777216).astype(jnp.int32)
    drop_step = jax.random.randint(keys[7], (1,), 0, 16777216).astype(jnp.int32)
    offsets = with_ends(jax.random.randint(keys[8], (SEQS, SEQ_LEN), 0, 16777216), jax.random.fold_in(keys[8], 1), 0, 16777215).astype(jnp.int32)
    return {"query_proj": query_proj, "key_proj": key_proj, "value_proj": value_proj, "filter_taps": filter_taps, "skip_gain": skip_gain, "out_weight": out_weight, "drop_seed": drop_seed, "drop_step": drop_step, "offsets": offsets}


drop_level = 6554
keep_scale = 65536.0 / (65536.0 - 6554.0)


def mix_bits(hashed):
    hashed = hashed ^ lax.shift_right_logical(hashed, jnp.full_like(hashed, 16))
    hashed = hashed * jnp.int32(73244475)
    hashed = hashed ^ lax.shift_right_logical(hashed, jnp.full_like(hashed, 16))
    hashed = hashed * jnp.int32(73244475)
    hashed = hashed ^ lax.shift_right_logical(hashed, jnp.full_like(hashed, 16))
    return hashed


def keep_mask(drop_seed, drop_step, positions, channel_ids):
    seed_word = mix_bits(drop_seed[0] * jnp.int32(-1640531535) + drop_step[0])
    hashed = mix_bits(seed_word ^ mix_bits(positions))
    hashed = mix_bits(hashed ^ (channel_ids * jnp.int32(668265263)))
    low_bits = lax.shift_right_logical(hashed, jnp.full_like(hashed, 8)) & 65535
    return low_bits >= drop_level


def reference(query_proj, key_proj, value_proj, filter_taps, skip_gain, out_weight, drop_seed, drop_step, offsets):
    channel_ids = jnp.arange(D, dtype=jnp.int32)
    keep_flags = keep_mask(drop_seed, drop_step, offsets[:, :, None], channel_ids[None, None, :])
    gated = (key_proj.astype(jnp.float32) * value_proj.astype(jnp.float32) * jnp.where(keep_flags, keep_scale, 0.0)).astype(jnp.bfloat16)
    block_width = min(512, D)
    block_count = D // block_width
    taps_blocks = filter_taps.reshape(SEQ_LEN, block_count, block_width).transpose(1, 0, 2)
    gated_blocks = gated.reshape(SEQS, SEQ_LEN, block_count, block_width).transpose(2, 0, 1, 3)
    skip_blocks = skip_gain.reshape(block_count, block_width)

    def convolve(operands):
        taps_part, gated_part, skip_part = operands
        period = 2 * SEQ_LEN
        signal = gated_part.astype(jnp.float32)
        spectrum = jnp.fft.rfft(signal, n=period, axis=1) * jnp.fft.rfft(taps_part, n=period, axis=0)[None]
        convolved = jnp.fft.irfft(spectrum, n=period, axis=1)[:, :SEQ_LEN]
        return (convolved + skip_part * signal).astype(jnp.bfloat16)

    mixed = lax.map(convolve, (taps_blocks, gated_blocks, skip_blocks))
    mixed = mixed.transpose(1, 2, 0, 3).reshape(SEQS, SEQ_LEN, D)
    gate_out = (query_proj.astype(jnp.float32) * mixed.astype(jnp.float32)).astype(jnp.bfloat16)
    result = jnp.dot(gate_out.reshape(SEQS * SEQ_LEN, D), out_weight, preferred_element_type=jnp.float32)
    return result.astype(jnp.bfloat16).reshape(SEQS, SEQ_LEN, D)
```

```python
import functools
import math

import jax
import jax.numpy as jnp
from jax import lax
from jax.experimental import pallas as pl
from jax.experimental.pallas import tpu as pltpu
from jax.sharding import PartitionSpec as P

drop_level = 6554
keep_scale = 65536.0 / (65536.0 - 6554.0)


def mix_bits(hashed):
    hashed = hashed ^ lax.shift_right_logical(hashed, jnp.full_like(hashed, 16))
    hashed = hashed * jnp.int32(73244475)
    hashed = hashed ^ lax.shift_right_logical(hashed, jnp.full_like(hashed, 16))
    hashed = hashed * jnp.int32(73244475)
    hashed = hashed ^ lax.shift_right_logical(hashed, jnp.full_like(hashed, 16))
    return hashed


def keep_mask(drop_seed, drop_step, positions, channel_ids):
    seed_word = mix_bits(drop_seed[0] * jnp.int32(-1640531535) + drop_step[0])
    hashed = mix_bits(seed_word ^ mix_bits(positions))
    hashed = mix_bits(hashed ^ channel_ids * jnp.int32(668265263))
    low_bits = lax.shift_right_logical(hashed, jnp.full_like(hashed, 8)) & 65535
    return low_bits >= drop_level


def phase_table(count_rows, count_cols, period, direction):
    product = (
        jnp.arange(count_rows, dtype=jnp.int32)[:, None]
        * jnp.arange(count_cols, dtype=jnp.int32)[None, :]
        % period
    )
    angles = direction * 2.0 * math.pi * product.astype(jnp.float32) / period
    return (jnp.cos(angles), jnp.sin(angles))


def einsum_high(formula, left_part, right_part):
    return jnp.einsum(formula, left_part, right_part, precision=lax.Precision.HIGHEST)


def complex_einsum(formula, left_pair, right_pair):
    left_real, left_imag = left_pair
    right_real, right_imag = right_pair
    real_part = einsum_high(formula, left_real, right_real)
    imag_part = None
    if left_imag is not None and right_imag is not None:
        real_part = real_part - einsum_high(formula, left_imag, right_imag)
    if right_imag is not None:
        imag_part = einsum_high(formula, left_real, right_imag)
    cross_term = einsum_high(formula, left_imag, right_real)
    imag_part = cross_term if imag_part is None else imag_part + cross_term
    return (real_part, imag_part)


def complex_product(first_pair, second_pair):
    return (
        first_pair[0] * second_pair[0] - first_pair[1] * second_pair[1],
        first_pair[0] * second_pair[1] + first_pair[1] * second_pair[0],
    )


def grid_shape(length):
    columns = min(256, length)
    period = 2 * length
    return (columns, period // columns, period)


def forward_spectrum(signal_pair, length):
    columns, rows_all, period = grid_shape(length)
    half_rows = rows_all // 2
    shaped = tuple(
        (
            (
                None
                if part_item is None
                else part_item.reshape(part_item.shape[0], half_rows, columns, part_item.shape[2])
            )
            for part_item in signal_pair
        )
    )
    sectioned = complex_einsum(
        "kr,nrcd->ndkc", phase_table(rows_all, half_rows, rows_all, -1.0), shaped
    )
    sectioned = complex_product(sectioned, phase_table(rows_all, columns, period, -1.0))
    return complex_einsum("ndkc,cj->ndkj", sectioned, phase_table(columns, columns, columns, -1.0))


def inverse_signal(spectrum, length):
    columns, rows_all, period = grid_shape(length)
    half_rows = rows_all // 2
    sectioned = complex_einsum(
        "ndkj,jc->ndkc", spectrum, phase_table(columns, columns, columns, 1.0)
    )
    sectioned = complex_product(sectioned, phase_table(rows_all, columns, period, 1.0))
    last_table = phase_table(half_rows, rows_all, rows_all, 1.0)
    real_part = einsum_high("rk,ndkc->nrcd", last_table[0], sectioned[0]) - einsum_high(
        "rk,ndkc->nrcd", last_table[1], sectioned[1]
    )
    pieces_out = (real_part,)
    return tuple(
        (
            item_part.reshape(item_part.shape[0], length, item_part.shape[3]) / period
            for item_part in pieces_out
        )
    )


def convolve_plain(signal, filter_spec):
    length = signal.shape[1]
    spectrum = forward_spectrum((signal, None), length)
    product = complex_product(spectrum, filter_spec)
    return inverse_signal(product, length)[0]


def per_device_plain(
    query_proj,
    key_proj,
    value_proj,
    filter_taps,
    skip_gain,
    out_weight,
    drop_seed,
    drop_step,
    offsets,
):
    group_width = query_proj.shape[2]
    channel_ids = lax.axis_index("ch") * group_width + jnp.arange(group_width, dtype=jnp.int32)
    keep_flags = keep_mask(drop_seed, drop_step, offsets[:, :, None], channel_ids[None, None, :])
    gated = (
        key_proj.astype(jnp.float32)
        * value_proj.astype(jnp.float32)
        * jnp.where(keep_flags, keep_scale, 0.0)
    ).astype(jnp.bfloat16)
    tap_cols = lax.all_to_all(filter_taps, "ctx", split_axis=1, concat_axis=0, tiled=True)
    local_width = tap_cols.shape[1]
    skip_local = lax.dynamic_slice_in_dim(
        skip_gain, lax.axis_index("ctx") * local_width, local_width
    )
    filter_spec = forward_spectrum((tap_cols[None], None), tap_cols.shape[0])
    signal = lax.all_to_all(gated, "ctx", split_axis=2, concat_axis=1, tiled=True).astype(
        jnp.float32
    )
    convolved = convolve_plain(signal, filter_spec)
    mixed_cols = (convolved + skip_local * signal).astype(jnp.bfloat16)
    mixed = lax.all_to_all(mixed_cols, "ctx", split_axis=1, concat_axis=2, tiled=True)
    gate_out = (query_proj.astype(jnp.float32) * mixed.astype(jnp.float32)).astype(jnp.bfloat16)
    flat_rows = gate_out.reshape(-1, group_width)
    partial_value = jnp.dot(
        flat_rows,
        lax.all_gather(out_weight, "ctx", axis=1, tiled=True),
        preferred_element_type=jnp.float32,
    )
    summed = lax.psum_scatter(partial_value, "ch", scatter_dimension=1, tiled=True)
    return summed.astype(jnp.bfloat16).reshape(query_proj.shape)


SIDE = 64

def roots(number):
    value = jnp.cos(number.astype(jnp.float32) * (2.0 * math.pi / (SIDE * SIDE)))
    high = lax.reduce_precision(value, 8, 7)
    return high.astype(jnp.bfloat16), (value - high).astype(jnp.bfloat16)

def phases(row_half, col_half, angle, sign):
    quarter = SIDE * SIDE // 4
    turn = jnp.where(row_half == col_half, 0, jnp.where(row_half > col_half, -sign * quarter, sign * quarter))
    return (angle + turn) % (SIDE * SIDE)

def tables():
    half = SIDE // 2
    def grid(shape):
        return tuple(lax.broadcasted_iota(jnp.int32, shape, axis) for axis in range(len(shape)))
    n2, row, col = grid((SIDE, 2 * SIDE, 2 * half))
    first = phases(row // SIDE, col // half, (SIDE * (col % half) + n2) * (row % SIDE), -1)
    row, col = grid((2 * SIDE, 2 * SIDE))
    angle = SIDE * (row % SIDE) * (col % SIDE)
    second = phases(row // SIDE, col // SIDE, angle, -1)
    third = phases(row // SIDE, col // SIDE, angle, 1)
    n2, row, col = grid((SIDE, 2 * half, 2 * SIDE))
    last = phases(row // half, col // SIDE, (SIDE * (row % half) + n2) * (col % SIDE), 1)
    return tuple(jnp.concatenate(roots(t), axis=-1) for t in (first, second, third, last))

def conv_kernel(got_ref, skip_ref, first_ref, second_ref, third_ref, last_ref, out_ref, sig_s, tap_s, mids_s, midt_s, back_s, res_s, *, blocks, tokens):
    half = SIDE // 2
    length = blocks * tokens
    for d in range(blocks):
        for s in range(2):
            sig_s[pl.ds(s * length + d * tokens, tokens), :] = got_ref[d, s * tokens:(s + 1) * tokens, :].astype(jnp.float32)
        tap_s[pl.ds(d * tokens, tokens), :] = got_ref[d, 2 * tokens:3 * tokens, :].astype(jnp.float32)
    zero = jnp.zeros((half, 128), jnp.float32)

    UA = 4
    def stage_a(i, _):
        for u in range(UA):
            n2 = i * UA + u
            sig = sig_s[pl.ds(n2, 2 * half, stride=SIDE), :]
            tap = jnp.concatenate([tap_s[pl.ds(n2, half, stride=SIDE), :], zero], axis=0)
            rhs = jnp.concatenate([sig, tap], axis=1).astype(jnp.bfloat16)
            rhs = jnp.concatenate([rhs, rhs], axis=0)
            spec = jnp.dot(first_ref[n2], rhs, preferred_element_type=jnp.float32)
            rows = pl.ds(pl.multiple_of(n2 * 2 * SIDE, 128), 2 * SIDE)
            mids_s[rows, :] = spec[:, :128]
            midt_s[rows, :] = spec[:, 128:]
        return 0
    lax.fori_loop(0, SIDE // UA, stage_a, 0)

    skip = skip_ref[...]
    scale = 1.0 / (SIDE * SIDE)
    UB = 2
    def stage_b(i, _):
        ys = []
        for u in range(UB):
            k1 = i * UB + u
            both = [jnp.concatenate([ref[pl.ds(k1, SIDE, stride=2 * SIDE), :], ref[pl.ds(SIDE + k1, SIDE, stride=2 * SIDE), :]], axis=0) for ref in (mids_s, midt_s)]
            rhs = jnp.concatenate(both, axis=1).astype(jnp.bfloat16)
            rhs = jnp.concatenate([rhs, rhs], axis=0)
            spec = jnp.dot(second_ref[...], rhs, preferred_element_type=jnp.float32)
            zr, zi = spec[:SIDE, :128], spec[SIDE:, :128]
            hr, hi = (spec[:SIDE, 128:] + skip) * scale, spec[SIDE:, 128:] * scale
            ys.append(jnp.concatenate([zr * hr - zi * hi, zr * hi + zi * hr], axis=0).astype(jnp.bfloat16))
        rhs = jnp.concatenate(ys, axis=1)
        rhs = jnp.concatenate([rhs, rhs], axis=0)
        back = jnp.dot(third_ref[...], rhs, preferred_element_type=jnp.float32)
        for u in range(UB):
            k1 = i * UB + u
            back_s[pl.ds(pl.multiple_of(k1 * 2 * SIDE, 128), 2 * SIDE), :] = back[:, u * 128:(u + 1) * 128]
        return 0
    lax.fori_loop(0, SIDE // UB, stage_b, 0)

    UD = 4
    def stage_d(i, _):
        for u in range(UD):
            n2 = i * UD + u
            real = back_s[pl.ds(n2, SIDE, stride=2 * SIDE), :]
            imag = back_s[pl.ds(SIDE + n2, SIDE, stride=2 * SIDE), :]
            rhs = jnp.concatenate([real, imag], axis=0).astype(jnp.bfloat16)
            rhs = jnp.concatenate([rhs, rhs], axis=0)
            res_s[pl.ds(n2, SIDE, stride=SIDE), :] = jnp.dot(last_ref[n2], rhs, preferred_element_type=jnp.float32)
        return 0
    lax.fori_loop(0, SIDE // UD, stage_d, 0)
    for d in range(blocks):
        for s in range(2):
            out_ref[d, s * tokens:(s + 1) * tokens, :] = res_s[pl.ds(s * length + d * tokens, tokens), :].astype(jnp.bfloat16)

def conv(got, skip, tabs):
    blocks, rows, lanes = got.shape
    tokens = rows // 3
    length = blocks * tokens
    V = pl.BlockSpec(memory_space=pltpu.VMEM)
    return pl.pallas_call(
        functools.partial(conv_kernel, blocks=blocks, tokens=tokens),
        out_shape=jax.ShapeDtypeStruct((blocks, 2 * tokens, lanes), jnp.bfloat16),
        in_specs=[V] * 6, out_specs=V,
        scratch_shapes=[pltpu.VMEM((2 * length, lanes), jnp.float32), pltpu.VMEM((length, lanes), jnp.float32),
                        pltpu.VMEM((2 * SIDE * SIDE, lanes), jnp.float32), pltpu.VMEM((2 * SIDE * SIDE, lanes), jnp.float32), pltpu.VMEM((2 * SIDE * SIDE, lanes), jnp.float32),
                        pltpu.VMEM((2 * length, lanes), jnp.float32)],
        compiler_params=pltpu.CompilerParams(vmem_limit_bytes=48 << 20),
        name="long_conv",
    )(got, skip, *tabs)


VMEM = pl.BlockSpec(memory_space=pltpu.VMEM)
SMEM = pl.BlockSpec(memory_space=pltpu.SMEM)


def gate_kernel(word_ref, off_ref, key_ref, value_ref, taps_ref, out_ref, tok_s):
    tokens = off_ref.shape[1]
    block = pl.program_id(0)

    @pl.when(block == 0)
    def _():
        for s in range(2):
            row = mix_bits(off_ref[s : s + 1, :])
            row = mix_bits(row ^ word_ref[0])
            tok_s[s * tokens : (s + 1) * tokens, :] = jnp.broadcast_to(row, (128, tokens)).T

    channel = word_ref[1] + block * 128 + lax.broadcasted_iota(jnp.int32, (1, 128), 1)
    channel = channel * jnp.int32(668265263)
    for s in range(2):
        rows = slice(s * tokens, (s + 1) * tokens)
        hashed = mix_bits(tok_s[rows, :] ^ channel)
        low_bits = lax.shift_right_logical(hashed, jnp.full_like(hashed, 8)) & 65535
        keep = jnp.where(low_bits >= drop_level, jnp.float32(keep_scale), jnp.float32(0.0))
        product = key_ref[s].astype(jnp.float32) * value_ref[s].astype(jnp.float32)
        out_ref[0, rows, :] = (product * keep).astype(jnp.bfloat16)
    out_ref[0, 2 * tokens : 3 * tokens, :] = taps_ref[...].astype(jnp.bfloat16)


def gate_and_pack(words, offsets, key_proj, value_proj, taps):
    _, tokens, width = key_proj.shape
    blocks = width // 128
    part = pl.BlockSpec((2, tokens, 128), lambda d: (0, 0, d))
    return pl.pallas_call(
        gate_kernel,
        grid=(blocks,),
        out_shape=jax.ShapeDtypeStruct((blocks, 3 * tokens, 128), jnp.bfloat16),
        in_specs=[
            SMEM,
            pl.BlockSpec((2, tokens), lambda d: (0, 0)),
            part,
            part,
            pl.BlockSpec((tokens, 128), lambda d: (0, d)),
        ],
        out_specs=pl.BlockSpec((1, 3 * tokens, 128), lambda d: (d, 0, 0)),
        scratch_shapes=[pltpu.VMEM((2 * tokens, 128), jnp.int32)],
        name="gate_and_pack",
    )(words, offsets, key_proj, value_proj, taps)


def query_kernel(query_ref, mixed_ref, out_ref):
    tokens = query_ref.shape[1]
    for s in range(2):
        rows = slice(s * tokens, (s + 1) * tokens)
        mixed = mixed_ref[0, rows, :].astype(jnp.float32)
        out_ref[rows, :] = (query_ref[s].astype(jnp.float32) * mixed).astype(jnp.bfloat16)


def query_gate(query_proj, mixed):
    _, tokens, width = query_proj.shape
    return pl.pallas_call(
        query_kernel,
        grid=(width // 128,),
        out_shape=jax.ShapeDtypeStruct((2 * tokens, width), jnp.bfloat16),
        in_specs=[
            pl.BlockSpec((2, tokens, 128), lambda c: (0, 0, c)),
            pl.BlockSpec((1, 2 * tokens, 128), lambda c: (c, 0, 0)),
        ],
        out_specs=pl.BlockSpec((2 * tokens, 128), lambda c: (0, c)),
        name="query_gate",
    )(query_proj, mixed)


def pair_kernel(sel_ref, rows_ref, *refs):
    weights, (keep_ref, give_ref) = refs[:-2], refs[-2:]
    for index, weight in enumerate(weights):
        part = jnp.dot(rows_ref[...], weight[...], preferred_element_type=jnp.float32)
        half, slot = index // 2, index % 2

        @pl.when(sel_ref[0] == slot)
        def _():
            keep_ref[half] = part

        @pl.when(sel_ref[0] != slot)
        def _():
            give_ref[half] = part.astype(jnp.bfloat16)


def pair_products(sel, rows, *weights):
    shape = (len(weights) // 2, rows.shape[0], weights[0].shape[1])
    return pl.pallas_call(
        pair_kernel,
        out_shape=(
            jax.ShapeDtypeStruct(shape, jnp.float32),
            jax.ShapeDtypeStruct(shape, jnp.bfloat16),
        ),
        in_specs=[SMEM] + [VMEM] * (1 + len(weights)),
        out_specs=(VMEM, VMEM),
        compiler_params=pltpu.CompilerParams(vmem_limit_bytes=40 << 20),
        name="pair_products",
    )(sel, rows, *weights)


def per_device_mesh(
    query_proj,
    key_proj,
    value_proj,
    filter_taps,
    skip_gain,
    out_weight,
    drop_seed,
    drop_step,
    offsets,
):
    group_width = query_proj.shape[2]
    ctx, ch = lax.axis_index("ctx"), lax.axis_index("ch")
    z, x, y, core = ctx // 2, ctx % 2, ch // 2, ch % 2

    def along_z(value, pairs):
        return lax.ppermute(value, "ctx", [(2 * a + k, 2 * b + k) for a, b in pairs for k in (0, 1)])

    def across_x(value):
        return lax.ppermute(value, "ctx", [(i, i ^ 1) for i in range(8)])

    def to_sibling(value):
        return lax.ppermute(value, "ch", [(j, j ^ 1) for j in range(4)])

    def across_y(value, same):
        pairs = []
        for i in range(8):
            for k in range(2):
                root = (i // 4) ^ (0 if same else 1)
                pairs.append((i * 4 + (root ^ 1) * 2 + k, i * 4 + root * 2 + k))
        return lax.ppermute(value, ("ctx", "ch"), pairs)

    seed_word = mix_bits(drop_seed[0] * jnp.int32(-1640531535) + drop_step[0])
    words = jnp.stack([seed_word, ch * group_width])
    packed = gate_and_pack(words, offsets, key_proj, value_proj, filter_taps)
    got = lax.all_to_all(packed, "ctx", split_axis=0, concat_axis=0, tiled=True)

    own = out_weight
    near = along_z(own, [(0, 1), (1, 0), (2, 3), (3, 2)])
    middle = along_z(own, [(1, 2), (2, 1)])
    own_x = across_x(own)
    near, middle, own_x = lax.optimization_barrier((near, middle, own_x))
    far_ends = along_z(middle, [(1, 0), (2, 3)])
    far_mid = along_z(near, [(2, 1), (1, 2)])
    near_x = across_x(near)

    skip_local = lax.dynamic_slice_in_dim(skip_gain, ctx * 128, 128)
    mixed = conv(got, skip_local[None, :], tables())
    mixed, far_ends, far_mid, near_x = lax.optimization_barrier((mixed, far_ends, far_mid, near_x))
    inner = (z == 1) | (z == 2)
    two = jnp.where(inner, far_mid, far_ends)
    back = lax.all_to_all(mixed, "ctx", split_axis=0, concat_axis=0, tiled=True)
    three_ends = along_z(far_mid, [(1, 0), (2, 3)])
    two_x = across_x(two)
    three = jnp.where(inner, middle, three_ends)
    two_x, three = lax.optimization_barrier((two_x, three))
    three_x = across_x(three)

    rows = query_gate(query_proj, back)
    sel = ((z + core) % 2).astype(jnp.int32)[None]

    def half_sums(keep, give):
        return keep + to_sibling(give).astype(jnp.float32)

    near_sum = half_sums(*pair_products(sel, rows, own, near, own_x, near_x))
    near_got = across_y(near_sum.astype(jnp.bfloat16), True)
    far_sum = half_sums(*pair_products(sel, rows, two, three))
    far_got = across_y(far_sum.astype(jnp.bfloat16), False)
    last_sum = half_sums(*pair_products(sel, rows, two_x, three_x))
    last_got = across_y(last_sum.astype(jnp.bfloat16), False)

    home = y == z // 2
    total_near = near_sum + near_got.astype(jnp.float32)
    here = jnp.where(home, total_near[0], far_sum[0] + far_got[0].astype(jnp.float32)).astype(jnp.bfloat16)
    there = jnp.where(home, total_near[1], last_sum[0] + last_got[0].astype(jnp.float32)).astype(jnp.bfloat16)
    left = jnp.where(x == 0, here, there)
    right = jnp.where(x == 0, there, here)
    return jnp.concatenate([left, right], axis=1).reshape(query_proj.shape)


def solution(mesh):
    sizes = dict(mesh.shape)

    def per_device(query_proj, *rest):
        width = query_proj.shape[2]
        length = query_proj.shape[1] * sizes["ctx"]
        fits = sizes["ctx"] == 8 and sizes["ch"] == 4 and width == 1024 and length == 2048
        return (per_device_mesh if fits else per_device_plain)(query_proj, *rest)

    return jax.shard_map(
        per_device,
        mesh=mesh,
        in_specs=(
            P(None, "ctx", "ch"),
            P(None, "ctx", "ch"),
            P(None, "ctx", "ch"),
            P("ctx", "ch"),
            P("ch"),
            P("ch", "ctx"),
            P(),
            P(),
            P(None, "ctx"),
        ),
        out_specs=P(None, "ctx", "ch"),
        check_vma=False,
    )
```

```python
import functools
import math

import jax
import jax.numpy as jnp
from jax import lax
from jax.experimental import pallas as pl
from jax.experimental.pallas import tpu as pltpu
from jax.sharding import PartitionSpec as P

drop_level = 6554
keep_scale = 65536.0 / (65536.0 - 6554.0)


def mix_bits(hashed):
    hashed = hashed ^ lax.shift_right_logical(hashed, jnp.full_like(hashed, 16))
    hashed = hashed * jnp.int32(73244475)
    hashed = hashed ^ lax.shift_right_logical(hashed, jnp.full_like(hashed, 16))
    hashed = hashed * jnp.int32(73244475)
    hashed = hashed ^ lax.shift_right_logical(hashed, jnp.full_like(hashed, 16))
    return hashed


def keep_mask(drop_seed, drop_step, positions, channel_ids):
    seed_word = mix_bits(drop_seed[0] * jnp.int32(-1640531535) + drop_step[0])
    hashed = mix_bits(seed_word ^ mix_bits(positions))
    hashed = mix_bits(hashed ^ channel_ids * jnp.int32(668265263))
    low_bits = lax.shift_right_logical(hashed, jnp.full_like(hashed, 8)) & 65535
    return low_bits >= drop_level


def phase_table(count_rows, count_cols, period, direction):
    product = (
        jnp.arange(count_rows, dtype=jnp.int32)[:, None]
        * jnp.arange(count_cols, dtype=jnp.int32)[None, :]
        % period
    )
    angles = direction * 2.0 * math.pi * product.astype(jnp.float32) / period
    return (jnp.cos(angles), jnp.sin(angles))


def einsum_high(formula, left_part, right_part):
    return jnp.einsum(formula, left_part, right_part, precision=lax.Precision.HIGHEST)


def complex_einsum(formula, left_pair, right_pair):
    left_real, left_imag = left_pair
    right_real, right_imag = right_pair
    real_part = einsum_high(formula, left_real, right_real)
    imag_part = None
    if left_imag is not None and right_imag is not None:
        real_part = real_part - einsum_high(formula, left_imag, right_imag)
    if right_imag is not None:
        imag_part = einsum_high(formula, left_real, right_imag)
    cross_term = einsum_high(formula, left_imag, right_real)
    imag_part = cross_term if imag_part is None else imag_part + cross_term
    return (real_part, imag_part)


def complex_product(first_pair, second_pair):
    return (
        first_pair[0] * second_pair[0] - first_pair[1] * second_pair[1],
        first_pair[0] * second_pair[1] + first_pair[1] * second_pair[0],
    )


def grid_shape(length):
    columns = min(256, length)
    period = 2 * length
    return (columns, period // columns, period)


def forward_spectrum(signal_pair, length):
    columns, rows_all, period = grid_shape(length)
    half_rows = rows_all // 2
    shaped = tuple(
        (
            (
                None
                if part_item is None
                else part_item.reshape(part_item.shape[0], half_rows, columns, part_item.shape[2])
            )
            for part_item in signal_pair
        )
    )
    sectioned = complex_einsum(
        "kr,nrcd->ndkc", phase_table(rows_all, half_rows, rows_all, -1.0), shaped
    )
    sectioned = complex_product(sectioned, phase_table(rows_all, columns, period, -1.0))
    return complex_einsum("ndkc,cj->ndkj", sectioned, phase_table(columns, columns, columns, -1.0))


def inverse_signal(spectrum, length):
    columns, rows_all, period = grid_shape(length)
    half_rows = rows_all // 2
    sectioned = complex_einsum(
        "ndkj,jc->ndkc", spectrum, phase_table(columns, columns, columns, 1.0)
    )
    sectioned = complex_product(sectioned, phase_table(rows_all, columns, period, 1.0))
    last_table = phase_table(half_rows, rows_all, rows_all, 1.0)
    real_part = einsum_high("rk,ndkc->nrcd", last_table[0], sectioned[0]) - einsum_high(
        "rk,ndkc->nrcd", last_table[1], sectioned[1]
    )
    pieces_out = (real_part,)
    return tuple(
        (
            item_part.reshape(item_part.shape[0], length, item_part.shape[3]) / period
            for item_part in pieces_out
        )
    )


def convolve_plain(signal, filter_spec):
    length = signal.shape[1]
    spectrum = forward_spectrum((signal, None), length)
    product = complex_product(spectrum, filter_spec)
    return inverse_signal(product, length)[0]


def per_device_plain(
    query_proj,
    key_proj,
    value_proj,
    filter_taps,
    skip_gain,
    out_weight,
    drop_seed,
    drop_step,
    offsets,
):
    group_width = query_proj.shape[2]
    channel_ids = lax.axis_index("ch") * group_width + jnp.arange(group_width, dtype=jnp.int32)
    keep_flags = keep_mask(drop_seed, drop_step, offsets[:, :, None], channel_ids[None, None, :])
    gated = (
        key_proj.astype(jnp.float32)
        * value_proj.astype(jnp.float32)
        * jnp.where(keep_flags, keep_scale, 0.0)
    ).astype(jnp.bfloat16)
    tap_cols = lax.all_to_all(filter_taps, "ctx", split_axis=1, concat_axis=0, tiled=True)
    local_width = tap_cols.shape[1]
    skip_local = lax.dynamic_slice_in_dim(
        skip_gain, lax.axis_index("ctx") * local_width, local_width
    )
    filter_spec = forward_spectrum((tap_cols[None], None), tap_cols.shape[0])
    signal = lax.all_to_all(gated, "ctx", split_axis=2, concat_axis=1, tiled=True).astype(
        jnp.float32
    )
    convolved = convolve_plain(signal, filter_spec)
    mixed_cols = (convolved + skip_local * signal).astype(jnp.bfloat16)
    mixed = lax.all_to_all(mixed_cols, "ctx", split_axis=1, concat_axis=2, tiled=True)
    gate_out = (query_proj.astype(jnp.float32) * mixed.astype(jnp.float32)).astype(jnp.bfloat16)
    flat_rows = gate_out.reshape(-1, group_width)
    partial_value = jnp.dot(
        flat_rows,
        lax.all_gather(out_weight, "ctx", axis=1, tiled=True),
        preferred_element_type=jnp.float32,
    )
    summed = lax.psum_scatter(partial_value, "ch", scatter_dimension=1, tiled=True)
    return summed.astype(jnp.bfloat16).reshape(query_proj.shape)


SIDE = 64
WIDE = 2 * SIDE + 8
NARROW = SIDE + 8


def numbers(shape):
    return tuple(lax.broadcasted_iota(jnp.int32, shape, axis) for axis in range(len(shape)))


def waves(steps):
    angle = (steps % (SIDE * SIDE)).astype(jnp.float32) * (2.0 * math.pi / (SIDE * SIDE))
    return jnp.cos(angle), jnp.sin(angle)


def turn(row_part, col_part, sign):
    return (row_part - col_part) * (sign * SIDE * SIDE // 4)


def high_low(value, low):
    high = lax.reduce_precision(value, 8, 7)
    return jnp.where(low, value - high, high).astype(jnp.bfloat16)


def small_waves():
    half = SIDE // 2
    row, col = numbers((2 * SIDE, 4 * half))
    first = waves(SIDE * (col % half) * (row % SIDE) + turn(row // SIDE, col // half % 2, 1))
    n2, row = numbers((SIDE, 2 * SIDE))
    first_shift = waves(n2 * (row % SIDE))
    row, col = numbers((2 * SIDE, 4 * SIDE))
    steps = SIDE * (row % SIDE) * (col % SIDE)
    second = waves(steps + turn(row // SIDE, col // SIDE % 2, 1))[0]
    third = waves(steps + turn(row // SIDE, col // SIDE % 2, -1))[0]
    row, col = numbers((2 * half, 4 * SIDE))
    last = waves(SIDE * (row % half) * (col % SIDE) + turn(row // half, col // SIDE % 2, -1))
    n2, col = numbers((SIDE, 4 * SIDE))
    last_shift = waves(n2 * (col % SIDE))
    return first, first_shift, second, third, last, last_shift


def tables(small):
    first, first_shift, second, third, last, last_shift = small
    value = first[0][None] * first_shift[0][:, :, None] - first[1][None] * first_shift[1][:, :, None]
    first_table = high_low(value, numbers(value.shape)[2] >= SIDE)
    value = last[0][None] * last_shift[0][:, None, :] - last[1][None] * last_shift[1][:, None, :]
    last_table = high_low(value, numbers(value.shape)[2] >= 2 * SIDE)
    low = numbers(second.shape)[1] >= 2 * SIDE
    return first_table, high_low(second, low), high_low(third, low), last_table


def conv_kernel(
    got_ref, skip_ref, first_ref, second_ref, third_ref, last_ref, out_ref,
    sig_s, tap_s, mids_s, midt_s, back_s, res_s, *, blocks, tokens
):
    half = SIDE // 2
    parts = tokens // SIDE
    for d in range(blocks):
        for a in range(parts):
            n1 = d * parts + a
            for s in range(3):
                ref, row = (tap_s, n1) if s == 2 else (sig_s, s * half + n1)
                begin = s * tokens + a * SIDE
                ref[row * NARROW : row * NARROW + SIDE, :] = got_ref[d, begin : begin + SIDE, :].astype(jnp.float32)
    zero = jnp.zeros((half, 128), jnp.float32)

    def stage_first(i, carry):
        for u in range(16):
            n2 = i * 16 + u
            sig = sig_s[pl.ds(n2, 2 * half, stride=NARROW), :]
            tap = jnp.concatenate([tap_s[pl.ds(n2, half, stride=NARROW), :], zero], axis=0)
            right = jnp.concatenate([sig, tap], axis=1).astype(jnp.bfloat16)
            right = jnp.concatenate([right, right], axis=0)
            spec = jnp.dot(first_ref[n2], right, preferred_element_type=jnp.float32)
            rows = pl.ds(pl.multiple_of(n2 * WIDE, 8), 2 * SIDE)
            mids_s[rows, :] = spec[:, :128]
            midt_s[rows, :] = spec[:, 128:]
        return carry

    lax.fori_loop(0, SIDE // 16, stage_first, 0)
    skip = skip_ref[...]
    scale = 1.0 / (SIDE * SIDE)

    def column(ref, k):
        real = ref[pl.ds(k, SIDE, stride=WIDE), :]
        return jnp.concatenate([real, ref[pl.ds(SIDE + k, SIDE, stride=WIDE), :]], axis=0)

    def stage_spectrum(i, carry):
        for v in range(4):
            products = []
            for u in range(2):
                k1 = i * 8 + v * 2 + u
                right = jnp.concatenate([column(mids_s, k1), column(midt_s, k1)], axis=1).astype(jnp.bfloat16)
                right = jnp.concatenate([right, right], axis=0)
                spec = jnp.dot(second_ref[...], right, preferred_element_type=jnp.float32)
                sig_r, sig_i = spec[:SIDE, :128], spec[SIDE:, :128]
                tap_r, tap_i = (spec[:SIDE, 128:] + skip) * scale, spec[SIDE:, 128:] * scale
                pair = [sig_r * tap_r - sig_i * tap_i, sig_r * tap_i + sig_i * tap_r]
                products.append(jnp.concatenate(pair, axis=0).astype(jnp.bfloat16))
            right = jnp.concatenate(products, axis=1)
            right = jnp.concatenate([right, right], axis=0)
            back = jnp.dot(third_ref[...], right, preferred_element_type=jnp.float32)
            for u in range(2):
                k1 = i * 8 + v * 2 + u
                back_s[pl.ds(pl.multiple_of(k1 * WIDE, 8), 2 * SIDE), :] = back[:, u * 128 : (u + 1) * 128]
        return carry

    lax.fori_loop(0, SIDE // 8, stage_spectrum, 0)

    def stage_last(i, carry):
        for u in range(16):
            n2 = i * 16 + u
            right = column(back_s, n2).astype(jnp.bfloat16)
            right = jnp.concatenate([right, right], axis=0)
            res_s[pl.ds(n2, 2 * half, stride=NARROW), :] = jnp.dot(
                last_ref[n2], right, preferred_element_type=jnp.float32
            )
        return carry

    lax.fori_loop(0, SIDE // 16, stage_last, 0)
    for d in range(blocks):
        for a in range(parts):
            for s in range(2):
                row = (s * half + d * parts + a) * NARROW
                begin = s * tokens + a * SIDE
                out_ref[d, begin : begin + SIDE, :] = res_s[row : row + SIDE, :].astype(jnp.bfloat16)


def conv(got, skip, tabs):
    blocks, rows, lanes = got.shape
    tokens = rows // 3
    full = pl.BlockSpec(memory_space=pltpu.VMEM)
    return pl.pallas_call(
        functools.partial(conv_kernel, blocks=blocks, tokens=tokens),
        out_shape=jax.ShapeDtypeStruct((blocks, 2 * tokens, lanes), jnp.bfloat16),
        in_specs=[full] * 6,
        out_specs=full,
        scratch_shapes=[
            pltpu.VMEM((SIDE * NARROW, lanes), jnp.float32),
            pltpu.VMEM((SIDE // 2 * NARROW, lanes), jnp.float32),
            pltpu.VMEM((SIDE * WIDE, lanes), jnp.float32),
            pltpu.VMEM((SIDE * WIDE, lanes), jnp.float32),
            pltpu.VMEM((SIDE * WIDE, lanes), jnp.float32),
            pltpu.VMEM((SIDE * NARROW, lanes), jnp.float32),
        ],
        compiler_params=pltpu.CompilerParams(vmem_limit_bytes=32 << 20),
        cost_estimate=pl.CostEstimate(flops=16_000_000_000, bytes_accessed=8 << 20, transcendentals=0),
        name="long_conv",
    )(got, skip, *tabs)


VMEM = pl.BlockSpec(memory_space=pltpu.VMEM)
SMEM = pl.BlockSpec(memory_space=pltpu.SMEM)


def gate_kernel(word_ref, off_ref, key_ref, value_ref, taps_ref, out_ref, tok_s):
    tokens = off_ref.shape[1]
    block = pl.program_id(0)

    @pl.when(block == 0)
    def _():
        for s in range(2):
            row = mix_bits(off_ref[s : s + 1, :])
            row = mix_bits(row ^ word_ref[0])
            tok_s[s * tokens : (s + 1) * tokens, :] = jnp.broadcast_to(row, (128, tokens)).T

    count = out_ref.shape[0]
    for c in range(count):
        lanes = slice(c * 128, (c + 1) * 128)
        channel = word_ref[1] + (block * count + c) * 128 + lax.broadcasted_iota(jnp.int32, (1, 128), 1)
        channel = channel * jnp.int32(668265263)
        for s in range(2):
            rows = slice(s * tokens, (s + 1) * tokens)
            hashed = mix_bits(tok_s[rows, :] ^ channel)
            low_bits = lax.shift_right_logical(hashed, jnp.full_like(hashed, 8)) & 65535
            keep = jnp.where(low_bits >= drop_level, jnp.float32(keep_scale), jnp.float32(0.0))
            product = key_ref[s, :, lanes].astype(jnp.float32) * value_ref[s, :, lanes].astype(jnp.float32)
            out_ref[c, rows, :] = (product * keep).astype(jnp.bfloat16)
        out_ref[c, 2 * tokens : 3 * tokens, :] = taps_ref[:, lanes].astype(jnp.bfloat16)


def gate_and_pack(words, offsets, key_proj, value_proj, taps):
    _, tokens, width = key_proj.shape
    blocks = width // 128
    count = 4
    part = pl.BlockSpec((2, tokens, count * 128), lambda d: (0, 0, d))
    return pl.pallas_call(
        gate_kernel,
        grid=(blocks // count,),
        out_shape=jax.ShapeDtypeStruct((blocks, 3 * tokens, 128), jnp.bfloat16),
        in_specs=[
            SMEM,
            pl.BlockSpec((2, tokens), lambda d: (0, 0)),
            part,
            part,
            pl.BlockSpec((tokens, count * 128), lambda d: (0, d)),
        ],
        out_specs=pl.BlockSpec((count, 3 * tokens, 128), lambda d: (d, 0, 0)),
        scratch_shapes=[pltpu.VMEM((2 * tokens, 128), jnp.int32)],
        name="gate_and_pack",
    )(words, offsets, key_proj, value_proj, taps)


def gate_rows(query_ref, mixed_ref, rows_ref):
    tokens = query_ref.shape[1]
    for c in range(mixed_ref.shape[0]):
        lanes = slice(c * 128, (c + 1) * 128)
        for s in range(2):
            rows = slice(s * tokens, (s + 1) * tokens)
            mixed = mixed_ref[c, rows, :].astype(jnp.float32)
            rows_ref[rows, lanes] = (query_ref[s, :, lanes].astype(jnp.float32) * mixed).astype(jnp.bfloat16)


def place_products(sel_ref, rows_ref, weights, keep_ref, give_ref):
    for index, weight in enumerate(weights):
        part = jnp.dot(rows_ref[...], weight[...], preferred_element_type=jnp.float32)
        home = jnp.where(sel_ref[1] == index // 2, 1, 0)

        @pl.when(sel_ref[0] == index % 2)
        def _():
            keep_ref[home] = part

        @pl.when(sel_ref[0] != index % 2)
        def _():
            give_ref[home] = part.astype(jnp.bfloat16)


def first_products_kernel(sel_ref, query_ref, mixed_ref, *refs):
    weights, (rows_ref, keep_ref, give_ref) = refs[:4], refs[4:]
    gate_rows(query_ref, mixed_ref, rows_ref)
    place_products(sel_ref, rows_ref, weights, keep_ref, give_ref)


def products_kernel(sel_ref, rows_ref, *refs):
    place_products(sel_ref, rows_ref, refs[:4], *refs[4:])


def products(kernel, sel, left, weights, extra=()):
    rows, width = left[-1].shape[-2], weights[0].shape[1]
    return pl.pallas_call(
        kernel,
        out_shape=tuple(extra)
        + (
            jax.ShapeDtypeStruct((2, rows, width), jnp.float32),
            jax.ShapeDtypeStruct((2, rows, width), jnp.bfloat16),
        ),
        in_specs=[SMEM] + [VMEM] * (len(left) + 4),
        out_specs=(VMEM,) * (2 + len(extra)),
        compiler_params=pltpu.CompilerParams(vmem_limit_bytes=24 << 20),
        cost_estimate=pl.CostEstimate(flops=2 * 4 * 512 * 1024 * 512, bytes_accessed=8 << 20, transcendentals=0),
        name="products",
    )(sel, *left, *weights)


def per_device_mesh(
    query_proj,
    key_proj,
    value_proj,
    filter_taps,
    skip_gain,
    out_weight,
    drop_seed,
    drop_step,
    offsets,
):
    group_width = query_proj.shape[2]
    ctx, ch = lax.axis_index("ctx"), lax.axis_index("ch")
    z, x, y, core = ctx // 2, ctx % 2, ch // 2, ch % 2

    def along_z(value, pairs):
        return lax.ppermute(value, "ctx", [(2 * a + k, 2 * b + k) for a, b in pairs for k in (0, 1)])

    def across_x(value):
        return lax.ppermute(value, "ctx", [(i, i ^ 1) for i in range(8)])

    def to_sibling(value):
        return lax.ppermute(value, "ch", [(j, j ^ 1) for j in range(4)])

    def across_y(value):
        return lax.ppermute(value, "ch", [(j, j ^ 2) for j in range(4)])

    own = out_weight
    near = along_z(own, [(0, 1), (1, 0), (2, 3), (3, 2)])
    middle = along_z(own, [(1, 2), (2, 1)])
    own_x = across_x(own)

    seed_word = mix_bits(drop_seed[0] * jnp.int32(-1640531535) + drop_step[0])
    words = jnp.stack([seed_word, ch * group_width])
    packed = gate_and_pack(words, offsets, key_proj, value_proj, filter_taps)
    got = lax.all_to_all(packed, "ctx", split_axis=0, concat_axis=0, tiled=True)

    near, middle, own_x, small = lax.optimization_barrier((near, middle, own_x, small_waves()))
    far_ends = along_z(middle, [(1, 0), (2, 3)])
    far_mid = along_z(near, [(2, 1), (1, 2)])
    near_x = across_x(near)
    tabs = tables(small)
    inner = (z == 1) | (z == 2)
    got, far_ends, far_mid, near_x, tabs = lax.optimization_barrier((got, far_ends, far_mid, near_x, tabs))
    two = jnp.where(inner, far_mid, far_ends)

    three_ends = along_z(far_mid, [(1, 0), (2, 3)])
    two_x = across_x(two)
    skip_local = lax.dynamic_slice_in_dim(skip_gain, ctx * 128, 128)
    mixed = conv(got, skip_local[None, :], tabs)
    mixed, three_ends, two_x = lax.optimization_barrier((mixed, three_ends, two_x))
    three = jnp.where(inner, middle, three_ends)

    back = lax.all_to_all(mixed, "ctx", split_axis=0, concat_axis=0, tiled=True)
    three_x = across_x(three)

    sel = jnp.stack([(z + core) % 2, (z // 2 + y) % 2]).astype(jnp.int32)

    def away_sum(keep, give):
        given = to_sibling(give).astype(jnp.float32)
        return (keep[0] + given[0]).astype(jnp.bfloat16), keep[1] + given[1]

    rows_type = jax.ShapeDtypeStruct((2 * query_proj.shape[1], group_width), jnp.bfloat16)
    rows, keep, give = products(
        first_products_kernel, sel, (query_proj, back), (own, near, two, three), (rows_type,)
    )
    away, home = away_sum(keep, give)
    here = across_y(away)
    keep, give = products(products_kernel, sel, (rows,), (own_x, near_x, two_x, three_x))
    away_x, home_x = away_sum(keep, give)
    there = across_y(away_x)

    here = (home + here.astype(jnp.float32)).astype(jnp.bfloat16)
    there = (home_x + there.astype(jnp.float32)).astype(jnp.bfloat16)
    left = jnp.where(x == 0, here, there)
    right = jnp.where(x == 0, there, here)
    return jnp.concatenate([left, right], axis=1).reshape(query_proj.shape)


def solution(mesh):
    sizes = dict(mesh.shape)

    def per_device(query_proj, *rest):
        width = query_proj.shape[2]
        length = query_proj.shape[1] * sizes["ctx"]
        fits = sizes["ctx"] == 8 and sizes["ch"] == 4 and width == 1024 and length == 2048
        return (per_device_mesh if fits else per_device_plain)(query_proj, *rest)

    return jax.shard_map(
        per_device,
        mesh=mesh,
        in_specs=(
            P(None, "ctx", "ch"),
            P(None, "ctx", "ch"),
            P(None, "ctx", "ch"),
            P("ctx", "ch"),
            P("ch"),
            P("ch", "ctx"),
            P(),
            P(),
            P(None, "ctx"),
        ),
        out_specs=P(None, "ctx", "ch"),
        check_vma=False,
    )
```

```python
import functools
import math

import jax
import jax.numpy as jnp
from jax import lax
from jax.experimental import pallas as pl
from jax.experimental.pallas import tpu as pltpu
from jax.sharding import PartitionSpec as P

drop_level = 6554
keep_scale = 65536.0 / (65536.0 - 6554.0)


def mix_bits(hashed):
    hashed = hashed ^ lax.shift_right_logical(hashed, jnp.full_like(hashed, 16))
    hashed = hashed * jnp.int32(73244475)
    hashed = hashed ^ lax.shift_right_logical(hashed, jnp.full_like(hashed, 16))
    hashed = hashed * jnp.int32(73244475)
    hashed = hashed ^ lax.shift_right_logical(hashed, jnp.full_like(hashed, 16))
    return hashed


def keep_mask(drop_seed, drop_step, positions, channel_ids):
    seed_word = mix_bits(drop_seed[0] * jnp.int32(-1640531535) + drop_step[0])
    hashed = mix_bits(seed_word ^ mix_bits(positions))
    hashed = mix_bits(hashed ^ channel_ids * jnp.int32(668265263))
    low_bits = lax.shift_right_logical(hashed, jnp.full_like(hashed, 8)) & 65535
    return low_bits >= drop_level


def phase_table(count_rows, count_cols, period, direction):
    product = (
        jnp.arange(count_rows, dtype=jnp.int32)[:, None]
        * jnp.arange(count_cols, dtype=jnp.int32)[None, :]
        % period
    )
    angles = direction * 2.0 * math.pi * product.astype(jnp.float32) / period
    return (jnp.cos(angles), jnp.sin(angles))


def einsum_high(formula, left_part, right_part):
    return jnp.einsum(formula, left_part, right_part, precision=lax.Precision.HIGHEST)


def complex_einsum(formula, left_pair, right_pair):
    left_real, left_imag = left_pair
    right_real, right_imag = right_pair
    real_part = einsum_high(formula, left_real, right_real)
    imag_part = None
    if left_imag is not None and right_imag is not None:
        real_part = real_part - einsum_high(formula, left_imag, right_imag)
    if right_imag is not None:
        imag_part = einsum_high(formula, left_real, right_imag)
    cross_term = einsum_high(formula, left_imag, right_real)
    imag_part = cross_term if imag_part is None else imag_part + cross_term
    return (real_part, imag_part)


def complex_product(first_pair, second_pair):
    return (
        first_pair[0] * second_pair[0] - first_pair[1] * second_pair[1],
        first_pair[0] * second_pair[1] + first_pair[1] * second_pair[0],
    )


def grid_shape(length):
    columns = min(256, length)
    period = 2 * length
    return (columns, period // columns, period)


def forward_spectrum(signal_pair, length):
    columns, rows_all, period = grid_shape(length)
    half_rows = rows_all // 2
    shaped = tuple(
        (
            (
                None
                if part_item is None
                else part_item.reshape(part_item.shape[0], half_rows, columns, part_item.shape[2])
            )
            for part_item in signal_pair
        )
    )
    sectioned = complex_einsum(
        "kr,nrcd->ndkc", phase_table(rows_all, half_rows, rows_all, -1.0), shaped
    )
    sectioned = complex_product(sectioned, phase_table(rows_all, columns, period, -1.0))
    return complex_einsum("ndkc,cj->ndkj", sectioned, phase_table(columns, columns, columns, -1.0))


def inverse_signal(spectrum, length):
    columns, rows_all, period = grid_shape(length)
    half_rows = rows_all // 2
    sectioned = complex_einsum(
        "ndkj,jc->ndkc", spectrum, phase_table(columns, columns, columns, 1.0)
    )
    sectioned = complex_product(sectioned, phase_table(rows_all, columns, period, 1.0))
    last_table = phase_table(half_rows, rows_all, rows_all, 1.0)
    real_part = einsum_high("rk,ndkc->nrcd", last_table[0], sectioned[0]) - einsum_high(
        "rk,ndkc->nrcd", last_table[1], sectioned[1]
    )
    pieces_out = (real_part,)
    return tuple(
        (
            item_part.reshape(item_part.shape[0], length, item_part.shape[3]) / period
            for item_part in pieces_out
        )
    )


def convolve_plain(signal, filter_spec):
    length = signal.shape[1]
    spectrum = forward_spectrum((signal, None), length)
    product = complex_product(spectrum, filter_spec)
    return inverse_signal(product, length)[0]


def per_device_plain(
    query_proj,
    key_proj,
    value_proj,
    filter_taps,
    skip_gain,
    out_weight,
    drop_seed,
    drop_step,
    offsets,
):
    group_width = query_proj.shape[2]
    channel_ids = lax.axis_index("ch") * group_width + jnp.arange(group_width, dtype=jnp.int32)
    keep_flags = keep_mask(drop_seed, drop_step, offsets[:, :, None], channel_ids[None, None, :])
    gated = (
        key_proj.astype(jnp.float32)
        * value_proj.astype(jnp.float32)
        * jnp.where(keep_flags, keep_scale, 0.0)
    ).astype(jnp.bfloat16)
    tap_cols = lax.all_to_all(filter_taps, "ctx", split_axis=1, concat_axis=0, tiled=True)
    local_width = tap_cols.shape[1]
    skip_local = lax.dynamic_slice_in_dim(
        skip_gain, lax.axis_index("ctx") * local_width, local_width
    )
    filter_spec = forward_spectrum((tap_cols[None], None), tap_cols.shape[0])
    signal = lax.all_to_all(gated, "ctx", split_axis=2, concat_axis=1, tiled=True).astype(
        jnp.float32
    )
    convolved = convolve_plain(signal, filter_spec)
    mixed_cols = (convolved + skip_local * signal).astype(jnp.bfloat16)
    mixed = lax.all_to_all(mixed_cols, "ctx", split_axis=1, concat_axis=2, tiled=True)
    gate_out = (query_proj.astype(jnp.float32) * mixed.astype(jnp.float32)).astype(jnp.bfloat16)
    flat_rows = gate_out.reshape(-1, group_width)
    partial_value = jnp.dot(
        flat_rows,
        lax.all_gather(out_weight, "ctx", axis=1, tiled=True),
        preferred_element_type=jnp.float32,
    )
    summed = lax.psum_scatter(partial_value, "ch", scatter_dimension=1, tiled=True)
    return summed.astype(jnp.bfloat16).reshape(query_proj.shape)


SIDE = 64
WIDE = 2 * SIDE + 8
NARROW = SIDE + 8


def numbers(shape):
    return tuple(lax.broadcasted_iota(jnp.int32, shape, axis) for axis in range(len(shape)))


def waves(steps):
    angle = (steps % (SIDE * SIDE)).astype(jnp.float32) * (2.0 * math.pi / (SIDE * SIDE))
    return jnp.cos(angle), jnp.sin(angle)


def turn(row_part, col_part, sign):
    return (row_part - col_part) * (sign * SIDE * SIDE // 4)


def high_low(value, low):
    high = lax.reduce_precision(value, 8, 7)
    return jnp.where(low, value - high, high).astype(jnp.bfloat16)


def small_waves():
    half = SIDE // 2
    row, col = numbers((2 * SIDE, 4 * half))
    first = waves(SIDE * (col % half) * (row % SIDE) + turn(row // SIDE, col // half % 2, 1))
    n2, row = numbers((SIDE, 2 * SIDE))
    first_shift = waves(n2 * (row % SIDE))
    row, col = numbers((2 * SIDE, 4 * SIDE))
    steps = SIDE * (row % SIDE) * (col % SIDE)
    second = waves(steps + turn(row // SIDE, col // SIDE % 2, 1))[0]
    third = waves(steps + turn(row // SIDE, col // SIDE % 2, -1))[0]
    row, col = numbers((2 * half, 4 * SIDE))
    last = waves(SIDE * (row % half) * (col % SIDE) + turn(row // half, col // SIDE % 2, -1))
    n2, col = numbers((SIDE, 4 * SIDE))
    last_shift = waves(n2 * (col % SIDE))
    return first, first_shift, second, third, last, last_shift


def tables(small):
    first, first_shift, second, third, last, last_shift = small
    value = first[0][None] * first_shift[0][:, :, None] - first[1][None] * first_shift[1][:, :, None]
    first_table = high_low(value, numbers(value.shape)[2] >= SIDE)
    value = last[0][None] * last_shift[0][:, None, :] - last[1][None] * last_shift[1][:, None, :]
    last_table = high_low(value, numbers(value.shape)[2] >= 2 * SIDE)
    low = numbers(second.shape)[1] >= 2 * SIDE
    return first_table, high_low(second, low), high_low(third, low), last_table


def conv_kernel(
    got_ref, skip_ref, first_ref, second_ref, third_ref, last_ref, out_ref,
    sig_s, tap_s, mids_s, midt_s, back_s, res_s, *, blocks, tokens
):
    half = SIDE // 2
    parts = tokens // SIDE
    for d in range(blocks):
        for a in range(parts):
            n1 = d * parts + a
            for s in range(3):
                ref, row = (tap_s, n1) if s == 2 else (sig_s, s * half + n1)
                begin = s * tokens + a * SIDE
                ref[row * NARROW : row * NARROW + SIDE, :] = got_ref[d, begin : begin + SIDE, :].astype(jnp.float32)
    zero = jnp.zeros((half, 128), jnp.float32)

    def stage_first(i, carry):
        for u in range(16):
            n2 = i * 16 + u
            sig = sig_s[pl.ds(n2, 2 * half, stride=NARROW), :]
            tap = jnp.concatenate([tap_s[pl.ds(n2, half, stride=NARROW), :], zero], axis=0)
            right = jnp.concatenate([sig, tap], axis=1).astype(jnp.bfloat16)
            right = jnp.concatenate([right, right], axis=0)
            spec = jnp.dot(first_ref[n2], right, preferred_element_type=jnp.float32)
            rows = pl.ds(pl.multiple_of(n2 * WIDE, 8), 2 * SIDE)
            mids_s[rows, :] = spec[:, :128]
            midt_s[rows, :] = spec[:, 128:]
        return carry

    lax.fori_loop(0, SIDE // 16, stage_first, 0)
    skip = skip_ref[...]
    scale = 1.0 / (SIDE * SIDE)

    def column(ref, k):
        real = ref[pl.ds(k, SIDE, stride=WIDE), :]
        return jnp.concatenate([real, ref[pl.ds(SIDE + k, SIDE, stride=WIDE), :]], axis=0)

    def stage_spectrum(i, carry):
        for v in range(4):
            products = []
            for u in range(2):
                k1 = i * 8 + v * 2 + u
                right = jnp.concatenate([column(mids_s, k1), column(midt_s, k1)], axis=1).astype(jnp.bfloat16)
                right = jnp.concatenate([right, right], axis=0)
                spec = jnp.dot(second_ref[...], right, preferred_element_type=jnp.float32)
                sig_r, sig_i = spec[:SIDE, :128], spec[SIDE:, :128]
                tap_r, tap_i = (spec[:SIDE, 128:] + skip) * scale, spec[SIDE:, 128:] * scale
                pair = [sig_r * tap_r - sig_i * tap_i, sig_r * tap_i + sig_i * tap_r]
                products.append(jnp.concatenate(pair, axis=0).astype(jnp.bfloat16))
            right = jnp.concatenate(products, axis=1)
            right = jnp.concatenate([right, right], axis=0)
            back = jnp.dot(third_ref[...], right, preferred_element_type=jnp.float32)
            for u in range(2):
                k1 = i * 8 + v * 2 + u
                back_s[pl.ds(pl.multiple_of(k1 * WIDE, 8), 2 * SIDE), :] = back[:, u * 128 : (u + 1) * 128]
        return carry

    lax.fori_loop(0, SIDE // 8, stage_spectrum, 0)

    def stage_last(i, carry):
        for u in range(16):
            n2 = i * 16 + u
            right = column(back_s, n2).astype(jnp.bfloat16)
            right = jnp.concatenate([right, right], axis=0)
            res_s[pl.ds(n2, 2 * half, stride=NARROW), :] = jnp.dot(
                last_ref[n2], right, preferred_element_type=jnp.float32
            )
        return carry

    lax.fori_loop(0, SIDE // 16, stage_last, 0)
    for d in range(blocks):
        for a in range(parts):
            for s in range(2):
                row = (s * half + d * parts + a) * NARROW
                begin = s * tokens + a * SIDE
                out_ref[d, begin : begin + SIDE, :] = res_s[row : row + SIDE, :].astype(jnp.bfloat16)


def conv(got, skip, tabs):
    blocks, rows, lanes = got.shape
    tokens = rows // 3
    full = pl.BlockSpec(memory_space=pltpu.VMEM)
    return pl.pallas_call(
        functools.partial(conv_kernel, blocks=blocks, tokens=tokens),
        out_shape=jax.ShapeDtypeStruct((blocks, 2 * tokens, lanes), jnp.bfloat16),
        in_specs=[full] * 6,
        out_specs=full,
        scratch_shapes=[
            pltpu.VMEM((SIDE * NARROW, lanes), jnp.float32),
            pltpu.VMEM((SIDE // 2 * NARROW, lanes), jnp.float32),
            pltpu.VMEM((SIDE * WIDE, lanes), jnp.float32),
            pltpu.VMEM((SIDE * WIDE, lanes), jnp.float32),
            pltpu.VMEM((SIDE * WIDE, lanes), jnp.float32),
            pltpu.VMEM((SIDE * NARROW, lanes), jnp.float32),
        ],
        compiler_params=pltpu.CompilerParams(vmem_limit_bytes=32 << 20),
        cost_estimate=pl.CostEstimate(flops=16_000_000_000, bytes_accessed=8 << 20, transcendentals=0),
        name="long_conv",
    )(got, skip, *tabs)


VMEM = pl.BlockSpec(memory_space=pltpu.VMEM)
SMEM = pl.BlockSpec(memory_space=pltpu.SMEM)


def gate_kernel(word_ref, off_ref, key_ref, value_ref, taps_ref, out_ref, tok_s):
    tokens = off_ref.shape[1]
    block = pl.program_id(0)

    @pl.when(block == 0)
    def _():
        for s in range(2):
            row = mix_bits(off_ref[s : s + 1, :])
            row = mix_bits(row ^ word_ref[0])
            tok_s[s * tokens : (s + 1) * tokens, :] = jnp.broadcast_to(row, (128, tokens)).T

    count = out_ref.shape[0]
    for c in range(count):
        lanes = slice(c * 128, (c + 1) * 128)
        channel = word_ref[1] + (block * count + c) * 128 + lax.broadcasted_iota(jnp.int32, (1, 128), 1)
        channel = channel * jnp.int32(668265263)
        for s in range(2):
            rows = slice(s * tokens, (s + 1) * tokens)
            hashed = mix_bits(tok_s[rows, :] ^ channel)
            low_bits = lax.shift_right_logical(hashed, jnp.full_like(hashed, 8)) & 65535
            keep = jnp.where(low_bits >= drop_level, jnp.float32(keep_scale), jnp.float32(0.0))
            product = key_ref[s, :, lanes].astype(jnp.float32) * value_ref[s, :, lanes].astype(jnp.float32)
            out_ref[c, rows, :] = (product * keep).astype(jnp.bfloat16)
        out_ref[c, 2 * tokens : 3 * tokens, :] = taps_ref[:, lanes].astype(jnp.bfloat16)


def gate_and_pack(words, offsets, key_proj, value_proj, taps):
    _, tokens, width = key_proj.shape
    blocks = width // 128
    count = 4
    part = pl.BlockSpec((2, tokens, count * 128), lambda d: (0, 0, d))
    return pl.pallas_call(
        gate_kernel,
        grid=(blocks // count,),
        out_shape=jax.ShapeDtypeStruct((blocks, 3 * tokens, 128), jnp.bfloat16),
        in_specs=[
            SMEM,
            pl.BlockSpec((2, tokens), lambda d: (0, 0)),
            part,
            part,
            pl.BlockSpec((tokens, count * 128), lambda d: (0, d)),
        ],
        out_specs=pl.BlockSpec((count, 3 * tokens, 128), lambda d: (d, 0, 0)),
        scratch_shapes=[pltpu.VMEM((2 * tokens, 128), jnp.int32)],
        name="gate_and_pack",
    )(words, offsets, key_proj, value_proj, taps)


def gate_rows(query_ref, mixed_ref, rows_ref):
    tokens = query_ref.shape[1]
    for c in range(mixed_ref.shape[0]):
        lanes = slice(c * 128, (c + 1) * 128)
        for s in range(2):
            rows = slice(s * tokens, (s + 1) * tokens)
            mixed = mixed_ref[c, rows, :].astype(jnp.float32)
            rows_ref[rows, lanes] = (query_ref[s, :, lanes].astype(jnp.float32) * mixed).astype(jnp.bfloat16)


def fetch(sources, held, sems):
    copies = [pltpu.make_async_copy(source, held.at[i], sems.at[i]) for i, source in enumerate(sources)]
    for copy in copies:
        copy.start()
    return copies


def half_products(sel_ref, rows_ref, held, give_ref, keep_ref):
    away, home, mine = 2 - 2 * sel_ref[1], 2 * sel_ref[1], sel_ref[0]
    for place, index in enumerate((away + 1 - mine, home + 1 - mine)):
        part = jnp.dot(rows_ref[...], held[index], preferred_element_type=jnp.float32)
        give_ref[place] = part.astype(give_ref.dtype)
    keep_ref[...] = jnp.dot(rows_ref[...], held[away + mine], preferred_element_type=jnp.float32)


def line_kernel(sel_ref, query_ref, mixed_ref, *refs):
    sources, (rows_ref, give_ref, keep_ref, held, sems) = refs[:4], refs[4:]
    copies = fetch(sources, held, sems)
    gate_rows(query_ref, mixed_ref, rows_ref)
    for copy in copies:
        copy.wait()
    half_products(sel_ref, rows_ref, held, give_ref, keep_ref)


def across_kernel(sel_ref, rows_ref, *refs):
    sources, (give_ref, keep_ref, held, sems) = refs[:4], refs[4:]
    for copy in fetch(sources, held, sems):
        copy.wait()
    half_products(sel_ref, rows_ref, held, give_ref, keep_ref)


def home_kernel(sel_ref, rows_ref, given_ref, given_x_ref, *refs):
    sources, (out_ref, held, sems) = refs[:8], refs[8:]
    copies = fetch(sources, held, sems)
    for half in range(2):
        for copy in copies[4 * half : 4 * half + 4]:
            copy.wait()
        part = jnp.dot(
            rows_ref[...], held[4 * half + 2 * sel_ref[1] + sel_ref[0]], preferred_element_type=jnp.float32
        )
        given = (given_ref, given_x_ref)[half][1]
        out_ref[half] = part + given.astype(jnp.float32)


def products(kernel, outs, sel, left, weights, dots):
    rows, (depth, width) = left[-1].shape[-2], weights[0].shape
    return pl.pallas_call(
        kernel,
        out_shape=outs,
        in_specs=[SMEM] + [VMEM] * len(left) + [pl.BlockSpec(memory_space=pl.ANY)] * len(weights),
        out_specs=(VMEM,) * len(outs),
        scratch_shapes=[
            pltpu.VMEM((len(weights), depth, width), jnp.bfloat16),
            pltpu.SemaphoreType.DMA((len(weights),)),
        ],
        compiler_params=pltpu.CompilerParams(vmem_limit_bytes=56 << 20),
        cost_estimate=pl.CostEstimate(
            flops=2 * dots * rows * depth * width, bytes_accessed=8 << 20, transcendentals=0
        ),
        name="products",
    )(sel, *left, *weights)


def finish_kernel(x_ref, home_ref, here_ref, there_ref, out_ref):
    width = here_ref.shape[1]
    for half, away_ref in enumerate((here_ref, there_ref)):
        total = (home_ref[half] + away_ref[...].astype(jnp.float32)).astype(jnp.bfloat16)

        @pl.when(x_ref[0] == half)
        def _():
            out_ref[:, :width] = total

        @pl.when(x_ref[0] != half)
        def _():
            out_ref[:, width:] = total


def finish(x, home, here, there):
    rows, width = here.shape
    return pl.pallas_call(
        finish_kernel,
        out_shape=jax.ShapeDtypeStruct((rows, 2 * width), jnp.bfloat16),
        in_specs=[SMEM, VMEM, VMEM, VMEM],
        out_specs=VMEM,
        compiler_params=pltpu.CompilerParams(vmem_limit_bytes=16 << 20),
        name="finish",
    )(x, home, here, there)


def per_device_mesh(
    query_proj,
    key_proj,
    value_proj,
    filter_taps,
    skip_gain,
    out_weight,
    drop_seed,
    drop_step,
    offsets,
):
    group_width = query_proj.shape[2]
    ctx, ch = lax.axis_index("ctx"), lax.axis_index("ch")
    z, x, y, core = ctx // 2, ctx % 2, ch // 2, ch % 2

    def along_z(value, pairs):
        return lax.ppermute(value, "ctx", [(2 * a + k, 2 * b + k) for a, b in pairs for k in (0, 1)])

    def across_x(value):
        return lax.ppermute(value, "ctx", [(i, i ^ 1) for i in range(8)])

    def to_sibling(value):
        return lax.ppermute(value, "ch", [(j, j ^ 1) for j in range(4)])

    def across_y(value):
        return lax.ppermute(value, "ch", [(j, j ^ 2) for j in range(4)])

    own = out_weight
    near = along_z(own, [(0, 1), (1, 0), (2, 3), (3, 2)])
    middle = along_z(own, [(1, 2), (2, 1)])
    own_x = across_x(own)

    seed_word = mix_bits(drop_seed[0] * jnp.int32(-1640531535) + drop_step[0])
    words = jnp.stack([seed_word, ch * group_width])
    packed = gate_and_pack(words, offsets, key_proj, value_proj, filter_taps)
    got = lax.all_to_all(packed, "ctx", split_axis=0, concat_axis=0, tiled=True)

    near, middle, own_x, small = lax.optimization_barrier((near, middle, own_x, small_waves()))
    near_x = across_x(near)
    tabs = tables(small)
    got, near_x, near, middle, tabs = lax.optimization_barrier((got, near_x, near, middle, tabs))
    far_ends = along_z(middle, [(1, 0), (2, 3)])
    far_mid = along_z(near, [(2, 1), (1, 2)])
    skip_local = lax.dynamic_slice_in_dim(skip_gain, ctx * 128, 128)
    mixed = conv(got, skip_local[None, :], tabs)
    back = lax.all_to_all(mixed, "ctx", split_axis=0, concat_axis=0, tiled=True)
    far_ends, far_mid, mixed = lax.optimization_barrier((far_ends, far_mid, mixed))
    inner = (z == 1) | (z == 2)
    two = jnp.where(inner, far_mid, far_ends)
    three_ends = along_z(far_mid, [(1, 0), (2, 3)])
    two_x = across_x(two)
    two_x, three_ends = lax.optimization_barrier((two_x, three_ends))
    three = jnp.where(inner, middle, three_ends)
    three_x = across_x(three)

    sel = jnp.stack([(z + core) % 2, (z // 2 + y) % 2]).astype(jnp.int32)
    line, line_x = (own, near, two, three), (own_x, near_x, two_x, three_x)
    row_count, half_width = 2 * query_proj.shape[1], own.shape[1]

    def out(dtype, *shape):
        return jax.ShapeDtypeStruct(shape + (row_count, half_width), dtype)

    halves = (out(jnp.bfloat16, 2), out(jnp.float32))
    rows_type = jax.ShapeDtypeStruct((row_count, group_width), jnp.bfloat16)
    rows, give, keep = products(line_kernel, (rows_type,) + halves, sel, (query_proj, back), line, 3)
    given = to_sibling(give)
    here = across_y((keep + given[0].astype(jnp.float32)).astype(jnp.bfloat16))
    rows, here = lax.optimization_barrier((rows, here))
    give, keep = products(across_kernel, halves, sel, (rows,), line_x, 3)
    given_x = to_sibling(give)
    there = across_y((keep + given_x[0].astype(jnp.float32)).astype(jnp.bfloat16))
    (home,) = products(home_kernel, (out(jnp.float32, 2),), sel, (rows, given, given_x), line + line_x, 2)
    return finish(x.astype(jnp.int32)[None], home, here, there).reshape(query_proj.shape)


def solution(mesh):
    sizes = dict(mesh.shape)

    def per_device(query_proj, *rest):
        width = query_proj.shape[2]
        length = query_proj.shape[1] * sizes["ctx"]
        fits = sizes["ctx"] == 8 and sizes["ch"] == 4 and width == 1024 and length == 2048
        return (per_device_mesh if fits else per_device_plain)(query_proj, *rest)

    return jax.shard_map(
        per_device,
        mesh=mesh,
        in_specs=(
            P(None, "ctx", "ch"),
            P(None, "ctx", "ch"),
            P(None, "ctx", "ch"),
            P("ctx", "ch"),
            P("ch"),
            P("ch", "ctx"),
            P(),
            P(),
            P(None, "ctx"),
        ),
        out_specs=P(None, "ctx", "ch"),
        check_vma=False,
    )
```

```python
import functools
import math

import jax
import jax.numpy as jnp
from jax import lax
from jax.experimental import pallas as pl
from jax.experimental.pallas import tpu as pltpu
from jax.sharding import PartitionSpec as P

drop_level = 6554
keep_scale = 65536.0 / (65536.0 - 6554.0)


def mix_bits(hashed):
    hashed = hashed ^ lax.shift_right_logical(hashed, jnp.full_like(hashed, 16))
    hashed = hashed * jnp.int32(73244475)
    hashed = hashed ^ lax.shift_right_logical(hashed, jnp.full_like(hashed, 16))
    hashed = hashed * jnp.int32(73244475)
    hashed = hashed ^ lax.shift_right_logical(hashed, jnp.full_like(hashed, 16))
    return hashed


def keep_mask(drop_seed, drop_step, positions, channel_ids):
    seed_word = mix_bits(drop_seed[0] * jnp.int32(-1640531535) + drop_step[0])
    hashed = mix_bits(seed_word ^ mix_bits(positions))
    hashed = mix_bits(hashed ^ channel_ids * jnp.int32(668265263))
    low_bits = lax.shift_right_logical(hashed, jnp.full_like(hashed, 8)) & 65535
    return low_bits >= drop_level


def phase_table(count_rows, count_cols, period, direction):
    product = (
        jnp.arange(count_rows, dtype=jnp.int32)[:, None]
        * jnp.arange(count_cols, dtype=jnp.int32)[None, :]
        % period
    )
    angles = direction * 2.0 * math.pi * product.astype(jnp.float32) / period
    return (jnp.cos(angles), jnp.sin(angles))


def einsum_high(formula, left_part, right_part):
    return jnp.einsum(formula, left_part, right_part, precision=lax.Precision.HIGHEST)


def complex_einsum(formula, left_pair, right_pair):
    left_real, left_imag = left_pair
    right_real, right_imag = right_pair
    real_part = einsum_high(formula, left_real, right_real)
    imag_part = None
    if left_imag is not None and right_imag is not None:
        real_part = real_part - einsum_high(formula, left_imag, right_imag)
    if right_imag is not None:
        imag_part = einsum_high(formula, left_real, right_imag)
    cross_term = einsum_high(formula, left_imag, right_real)
    imag_part = cross_term if imag_part is None else imag_part + cross_term
    return (real_part, imag_part)


def complex_product(first_pair, second_pair):
    return (
        first_pair[0] * second_pair[0] - first_pair[1] * second_pair[1],
        first_pair[0] * second_pair[1] + first_pair[1] * second_pair[0],
    )


def grid_shape(length):
    columns = min(256, length)
    period = 2 * length
    return (columns, period // columns, period)


def forward_spectrum(signal_pair, length):
    columns, rows_all, period = grid_shape(length)
    half_rows = rows_all // 2
    shaped = tuple(
        (
            (
                None
                if part_item is None
                else part_item.reshape(part_item.shape[0], half_rows, columns, part_item.shape[2])
            )
            for part_item in signal_pair
        )
    )
    sectioned = complex_einsum(
        "kr,nrcd->ndkc", phase_table(rows_all, half_rows, rows_all, -1.0), shaped
    )
    sectioned = complex_product(sectioned, phase_table(rows_all, columns, period, -1.0))
    return complex_einsum("ndkc,cj->ndkj", sectioned, phase_table(columns, columns, columns, -1.0))


def inverse_signal(spectrum, length):
    columns, rows_all, period = grid_shape(length)
    half_rows = rows_all // 2
    sectioned = complex_einsum(
        "ndkj,jc->ndkc", spectrum, phase_table(columns, columns, columns, 1.0)
    )
    sectioned = complex_product(sectioned, phase_table(rows_all, columns, period, 1.0))
    last_table = phase_table(half_rows, rows_all, rows_all, 1.0)
    real_part = einsum_high("rk,ndkc->nrcd", last_table[0], sectioned[0]) - einsum_high(
        "rk,ndkc->nrcd", last_table[1], sectioned[1]
    )
    pieces_out = (real_part,)
    return tuple(
        (
            item_part.reshape(item_part.shape[0], length, item_part.shape[3]) / period
            for item_part in pieces_out
        )
    )


def convolve_plain(signal, filter_spec):
    length = signal.shape[1]
    spectrum = forward_spectrum((signal, None), length)
    product = complex_product(spectrum, filter_spec)
    return inverse_signal(product, length)[0]


def per_device_plain(
    query_proj,
    key_proj,
    value_proj,
    filter_taps,
    skip_gain,
    out_weight,
    drop_seed,
    drop_step,
    offsets,
):
    group_width = query_proj.shape[2]
    channel_ids = lax.axis_index("ch") * group_width + jnp.arange(group_width, dtype=jnp.int32)
    keep_flags = keep_mask(drop_seed, drop_step, offsets[:, :, None], channel_ids[None, None, :])
    gated = (
        key_proj.astype(jnp.float32)
        * value_proj.astype(jnp.float32)
        * jnp.where(keep_flags, keep_scale, 0.0)
    ).astype(jnp.bfloat16)
    tap_cols = lax.all_to_all(filter_taps, "ctx", split_axis=1, concat_axis=0, tiled=True)
    local_width = tap_cols.shape[1]
    skip_local = lax.dynamic_slice_in_dim(
        skip_gain, lax.axis_index("ctx") * local_width, local_width
    )
    filter_spec = forward_spectrum((tap_cols[None], None), tap_cols.shape[0])
    signal = lax.all_to_all(gated, "ctx", split_axis=2, concat_axis=1, tiled=True).astype(
        jnp.float32
    )
    convolved = convolve_plain(signal, filter_spec)
    mixed_cols = (convolved + skip_local * signal).astype(jnp.bfloat16)
    mixed = lax.all_to_all(mixed_cols, "ctx", split_axis=1, concat_axis=2, tiled=True)
    gate_out = (query_proj.astype(jnp.float32) * mixed.astype(jnp.float32)).astype(jnp.bfloat16)
    flat_rows = gate_out.reshape(-1, group_width)
    partial_value = jnp.dot(
        flat_rows,
        lax.all_gather(out_weight, "ctx", axis=1, tiled=True),
        preferred_element_type=jnp.float32,
    )
    summed = lax.psum_scatter(partial_value, "ch", scatter_dimension=1, tiled=True)
    return summed.astype(jnp.bfloat16).reshape(query_proj.shape)


SIDE = 64
WIDE = 2 * SIDE + 8
NARROW = SIDE + 8


def numbers(shape):
    return tuple(lax.broadcasted_iota(jnp.int32, shape, axis) for axis in range(len(shape)))


def waves(steps):
    angle = (steps % (SIDE * SIDE)).astype(jnp.float32) * (2.0 * math.pi / (SIDE * SIDE))
    return jnp.cos(angle), jnp.sin(angle)


def turn(row_part, col_part, sign):
    return (row_part - col_part) * (sign * SIDE * SIDE // 4)


def high_low(value, low):
    high = lax.reduce_precision(value, 8, 7)
    return jnp.where(low, value - high, high).astype(jnp.bfloat16)


def small_waves():
    half = SIDE // 2
    row, col = numbers((2 * SIDE, 4 * half))
    first = waves(SIDE * (col % half) * (row % SIDE) + turn(row // SIDE, col // half % 2, 1))
    n2, row = numbers((SIDE, 2 * SIDE))
    first_shift = waves(n2 * (row % SIDE))
    row, col = numbers((2 * SIDE, 4 * SIDE))
    steps = SIDE * (row % SIDE) * (col % SIDE)
    second = waves(steps + turn(row // SIDE, col // SIDE % 2, 1))[0]
    third = waves(steps + turn(row // SIDE, col // SIDE % 2, -1))[0]
    row, col = numbers((2 * half, 4 * SIDE))
    last = waves(SIDE * (row % half) * (col % SIDE) + turn(row // half, col // SIDE % 2, -1))
    n2, col = numbers((SIDE, 4 * SIDE))
    last_shift = waves(n2 * (col % SIDE))
    return first, first_shift, second, third, last, last_shift


def tables(small):
    first, first_shift, second, third, last, last_shift = small
    value = first[0][None] * first_shift[0][:, :, None] - first[1][None] * first_shift[1][:, :, None]
    first_table = high_low(value, numbers(value.shape)[2] >= SIDE)
    value = last[0][None] * last_shift[0][:, None, :] - last[1][None] * last_shift[1][:, None, :]
    last_table = high_low(value, numbers(value.shape)[2] >= 2 * SIDE)
    low = numbers(second.shape)[1] >= 2 * SIDE
    return first_table, high_low(second, low), high_low(third, low), last_table


def conv_kernel(
    got_ref, skip_ref, first_ref, second_ref, third_ref, last_ref, out_ref,
    sig_s, tap_s, mids_s, midt_s, back_s, res_s, *, blocks, tokens
):
    half = SIDE // 2
    parts = tokens // SIDE
    for d in range(blocks):
        for a in range(parts):
            n1 = d * parts + a
            for s in range(3):
                ref, row = (tap_s, n1) if s == 2 else (sig_s, s * half + n1)
                begin = s * tokens + a * SIDE
                ref[row * NARROW : row * NARROW + SIDE, :] = got_ref[d, begin : begin + SIDE, :].astype(jnp.float32)
    zero = jnp.zeros((half, 128), jnp.float32)

    def stage_first(i, carry):
        for u in range(16):
            n2 = i * 16 + u
            sig = sig_s[pl.ds(n2, 2 * half, stride=NARROW), :]
            tap = jnp.concatenate([tap_s[pl.ds(n2, half, stride=NARROW), :], zero], axis=0)
            right = jnp.concatenate([sig, tap], axis=1).astype(jnp.bfloat16)
            right = jnp.concatenate([right, right], axis=0)
            spec = jnp.dot(first_ref[n2], right, preferred_element_type=jnp.float32)
            rows = pl.ds(pl.multiple_of(n2 * WIDE, 8), 2 * SIDE)
            mids_s[rows, :] = spec[:, :128]
            midt_s[rows, :] = spec[:, 128:]
        return carry

    lax.fori_loop(0, SIDE // 16, stage_first, 0)
    skip = skip_ref[...]
    scale = 1.0 / (SIDE * SIDE)

    def column(ref, k):
        real = ref[pl.ds(k, SIDE, stride=WIDE), :]
        return jnp.concatenate([real, ref[pl.ds(SIDE + k, SIDE, stride=WIDE), :]], axis=0)

    def stage_spectrum(i, carry):
        for v in range(4):
            products = []
            for u in range(2):
                k1 = i * 8 + v * 2 + u
                right = jnp.concatenate([column(mids_s, k1), column(midt_s, k1)], axis=1).astype(jnp.bfloat16)
                right = jnp.concatenate([right, right], axis=0)
                spec = jnp.dot(second_ref[...], right, preferred_element_type=jnp.float32)
                sig_r, sig_i = spec[:SIDE, :128], spec[SIDE:, :128]
                tap_r, tap_i = (spec[:SIDE, 128:] + skip) * scale, spec[SIDE:, 128:] * scale
                pair = [sig_r * tap_r - sig_i * tap_i, sig_r * tap_i + sig_i * tap_r]
                products.append(jnp.concatenate(pair, axis=0).astype(jnp.bfloat16))
            right = jnp.concatenate(products, axis=1)
            right = jnp.concatenate([right, right], axis=0)
            back = jnp.dot(third_ref[...], right, preferred_element_type=jnp.float32)
            for u in range(2):
                k1 = i * 8 + v * 2 + u
                back_s[pl.ds(pl.multiple_of(k1 * WIDE, 8), 2 * SIDE), :] = back[:, u * 128 : (u + 1) * 128]
        return carry

    lax.fori_loop(0, SIDE // 8, stage_spectrum, 0)

    def stage_last(i, carry):
        for u in range(16):
            n2 = i * 16 + u
            right = column(back_s, n2).astype(jnp.bfloat16)
            right = jnp.concatenate([right, right], axis=0)
            res_s[pl.ds(n2, 2 * half, stride=NARROW), :] = jnp.dot(
                last_ref[n2], right, preferred_element_type=jnp.float32
            )
        return carry

    lax.fori_loop(0, SIDE // 16, stage_last, 0)
    for d in range(blocks):
        for a in range(parts):
            for s in range(2):
                row = (s * half + d * parts + a) * NARROW
                begin = s * tokens + a * SIDE
                out_ref[d, begin : begin + SIDE, :] = res_s[row : row + SIDE, :].astype(jnp.bfloat16)


def conv(got, skip, tabs):
    blocks, rows, lanes = got.shape
    tokens = rows // 3
    full = pl.BlockSpec(memory_space=pltpu.VMEM)
    return pl.pallas_call(
        functools.partial(conv_kernel, blocks=blocks, tokens=tokens),
        out_shape=jax.ShapeDtypeStruct((blocks, 2 * tokens, lanes), jnp.bfloat16),
        in_specs=[full] * 6,
        out_specs=full,
        scratch_shapes=[
            pltpu.VMEM((SIDE * NARROW, lanes), jnp.float32),
            pltpu.VMEM((SIDE // 2 * NARROW, lanes), jnp.float32),
            pltpu.VMEM((SIDE * WIDE, lanes), jnp.float32),
            pltpu.VMEM((SIDE * WIDE, lanes), jnp.float32),
            pltpu.VMEM((SIDE * WIDE, lanes), jnp.float32),
            pltpu.VMEM((SIDE * NARROW, lanes), jnp.float32),
        ],
        compiler_params=pltpu.CompilerParams(vmem_limit_bytes=32 << 20),
        cost_estimate=pl.CostEstimate(flops=1_000_000_000, bytes_accessed=1 << 20, transcendentals=0),
        name="long_conv",
    )(got, skip, *tabs)


VMEM = pl.BlockSpec(memory_space=pltpu.VMEM)
SMEM = pl.BlockSpec(memory_space=pltpu.SMEM)


def gate_kernel(word_ref, off_ref, key_ref, value_ref, taps_ref, out_ref, tok_s):
    tokens = off_ref.shape[1]
    block = pl.program_id(0)

    @pl.when(block == 0)
    def _():
        for s in range(2):
            row = mix_bits(off_ref[s : s + 1, :])
            row = mix_bits(row ^ word_ref[0])
            tok_s[s * tokens : (s + 1) * tokens, :] = jnp.broadcast_to(row, (128, tokens)).T

    count = out_ref.shape[0]
    for c in range(count):
        lanes = slice(c * 128, (c + 1) * 128)
        channel = word_ref[1] + (block * count + c) * 128 + lax.broadcasted_iota(jnp.int32, (1, 128), 1)
        channel = channel * jnp.int32(668265263)
        for s in range(2):
            rows = slice(s * tokens, (s + 1) * tokens)
            hashed = mix_bits(tok_s[rows, :] ^ channel)
            low_bits = lax.shift_right_logical(hashed, jnp.full_like(hashed, 8)) & 65535
            keep = jnp.where(low_bits >= drop_level, jnp.float32(keep_scale), jnp.float32(0.0))
            product = key_ref[s, :, lanes].astype(jnp.float32) * value_ref[s, :, lanes].astype(jnp.float32)
            out_ref[c, rows, :] = (product * keep).astype(jnp.bfloat16)
        out_ref[c, 2 * tokens : 3 * tokens, :] = taps_ref[:, lanes].astype(jnp.bfloat16)


def gate_and_pack(words, offsets, key_proj, value_proj, taps):
    _, tokens, width = key_proj.shape
    blocks = width // 128
    count = 4
    part = pl.BlockSpec((2, tokens, count * 128), lambda d: (0, 0, d))
    return pl.pallas_call(
        gate_kernel,
        grid=(blocks // count,),
        out_shape=jax.ShapeDtypeStruct((blocks, 3 * tokens, 128), jnp.bfloat16),
        in_specs=[
            SMEM,
            pl.BlockSpec((2, tokens), lambda d: (0, 0)),
            part,
            part,
            pl.BlockSpec((tokens, count * 128), lambda d: (0, d)),
        ],
        out_specs=pl.BlockSpec((count, 3 * tokens, 128), lambda d: (d, 0, 0)),
        scratch_shapes=[pltpu.VMEM((2 * tokens, 128), jnp.int32)],
        name="gate_and_pack",
    )(words, offsets, key_proj, value_proj, taps)


def gate_rows(query_ref, mixed_ref, rows_ref):
    tokens = query_ref.shape[1]
    for c in range(mixed_ref.shape[0]):
        lanes = slice(c * 128, (c + 1) * 128)
        for s in range(2):
            rows = slice(s * tokens, (s + 1) * tokens)
            mixed = mixed_ref[c, rows, :].astype(jnp.float32)
            rows_ref[rows, lanes] = (query_ref[s, :, lanes].astype(jnp.float32) * mixed).astype(jnp.bfloat16)


def fetch(sources, index, held, sem):
    for place, source in enumerate(sources):

        @pl.when(index == place)
        def _():
            pltpu.make_async_copy(source, held, sem).start()


def arrived(sources, held, sem):
    pltpu.make_async_copy(sources[0], held, sem).wait()


def place_of(sel_ref, pair, mine):
    kept = jnp.where(pair == 0, sel_ref[0], sel_ref[1])
    return 2 * pair + (kept if mine else 1 - kept)


def half_products(sel_ref, rows_ref, sources, give_ref, keep_ref, held, sems, before):
    home, away = sel_ref[2], 1 - sel_ref[2]
    for i, (pair, mine) in enumerate(((away, False), (home, False), (away, True))):
        fetch(sources, place_of(sel_ref, pair, mine), held.at[i], sems.at[i])
    before()
    for i in range(3):
        arrived(sources, held.at[i], sems.at[i])
        part = jnp.dot(rows_ref[...], held[i], preferred_element_type=jnp.float32)
        if i < 2:
            give_ref[i] = part.astype(give_ref.dtype)
        else:
            keep_ref[...] = part


def line_kernel(sel_ref, query_ref, mixed_ref, *refs):
    sources, (rows_ref, give_ref, keep_ref, held, sems) = refs[:4], refs[4:]
    before = functools.partial(gate_rows, query_ref, mixed_ref, rows_ref)
    half_products(sel_ref, rows_ref, sources, give_ref, keep_ref, held, sems, before)


def across_kernel(sel_ref, rows_ref, *refs):
    sources, (give_ref, keep_ref, held, sems) = refs[:4], refs[4:]
    half_products(sel_ref, rows_ref, sources, give_ref, keep_ref, held, sems, lambda: None)


def home_kernel(sel_ref, rows_ref, given_ref, given_x_ref, *refs):
    sources, (out_ref, held, sems) = (refs[:4], refs[4:8]), refs[8:]
    for half in range(2):
        fetch(sources[half], place_of(sel_ref, sel_ref[2], True), held.at[half], sems.at[half])
    for half in range(2):
        arrived(sources[half], held.at[half], sems.at[half])
        part = jnp.dot(rows_ref[...], held[half], preferred_element_type=jnp.float32)
        given = (given_ref, given_x_ref)[half][1]
        out_ref[half] = part + given.astype(jnp.float32)


def products(kernel, outs, sel, left, weights, dots):
    rows, (depth, width) = left[-1].shape[-2], weights[0].shape
    return pl.pallas_call(
        kernel,
        out_shape=outs,
        in_specs=[SMEM] + [VMEM] * len(left) + [pl.BlockSpec(memory_space=pl.ANY)] * len(weights),
        out_specs=(VMEM,) * len(outs),
        scratch_shapes=[
            pltpu.VMEM((dots, depth, width), jnp.bfloat16),
            pltpu.SemaphoreType.DMA((dots,)),
        ],
        compiler_params=pltpu.CompilerParams(vmem_limit_bytes=56 << 20),
        cost_estimate=pl.CostEstimate(
            flops=2 * dots * rows * depth * width, bytes_accessed=8 << 20, transcendentals=0
        ),
        name="products",
    )(sel, *left, *weights)


def finish_kernel(x_ref, home_ref, here_ref, there_ref, out_ref):
    width = here_ref.shape[1]
    for half, away_ref in enumerate((here_ref, there_ref)):
        total = (home_ref[half] + away_ref[...].astype(jnp.float32)).astype(jnp.bfloat16)

        @pl.when(x_ref[0] == half)
        def _():
            out_ref[:, :width] = total

        @pl.when(x_ref[0] != half)
        def _():
            out_ref[:, width:] = total


def finish(x, home, here, there):
    rows, width = here.shape
    return pl.pallas_call(
        finish_kernel,
        out_shape=jax.ShapeDtypeStruct((rows, 2 * width), jnp.bfloat16),
        in_specs=[SMEM, VMEM, VMEM, VMEM],
        out_specs=VMEM,
        compiler_params=pltpu.CompilerParams(vmem_limit_bytes=16 << 20),
        name="finish",
    )(x, home, here, there)


def per_device_mesh(
    query_proj,
    key_proj,
    value_proj,
    filter_taps,
    skip_gain,
    out_weight,
    drop_seed,
    drop_step,
    offsets,
):
    group_width = query_proj.shape[2]
    ctx, ch = lax.axis_index("ctx"), lax.axis_index("ch")
    z, x, y, core = ctx // 2, ctx % 2, ch // 2, ch % 2

    def along_z(value, pairs):
        return lax.ppermute(value, "ctx", [(2 * a + k, 2 * b + k) for a, b in pairs for k in (0, 1)])

    def across_x(value):
        return lax.ppermute(value, "ctx", [(i, i ^ 1) for i in range(8)])

    def to_sibling(value):
        return lax.ppermute(value, "ch", [(j, j ^ 1) for j in range(4)])

    def across_y(value):
        return lax.ppermute(value, "ch", [(j, j ^ 2) for j in range(4)])

    own = out_weight
    near = along_z(own, [(0, 1), (1, 0), (2, 3), (3, 2)])
    middle = along_z(own, [(1, 2), (2, 1)])
    own_x = across_x(own)

    seed_word = mix_bits(drop_seed[0] * jnp.int32(-1640531535) + drop_step[0])
    words = jnp.stack([seed_word, ch * group_width])
    packed = gate_and_pack(words, offsets, key_proj, value_proj, filter_taps)
    got = lax.all_to_all(packed, "ctx", split_axis=0, concat_axis=0, tiled=True)

    near, middle, own_x, small = lax.optimization_barrier((near, middle, own_x, small_waves()))
    near_x = across_x(near)
    far_ends = along_z(middle, [(1, 0), (2, 3)])
    tabs = tables(small)
    got, near, tabs = lax.optimization_barrier((got, near, tabs))
    far_mid = along_z(near, [(2, 1), (1, 2)])
    skip_local = lax.dynamic_slice_in_dim(skip_gain, ctx * 128, 128)
    mixed = conv(got, skip_local[None, :], tabs)
    back = lax.all_to_all(mixed, "ctx", split_axis=0, concat_axis=0, tiled=True)
    far_mid, far_ends, near_x, mixed = lax.optimization_barrier((far_mid, far_ends, near_x, mixed))
    inner = (z == 1) | (z == 2)
    three_ends = along_z(far_mid, [(1, 0), (2, 3)])
    third = jnp.where(inner, middle, far_ends)
    third_x = across_x(third)
    three_ends, third_x = lax.optimization_barrier((three_ends, third_x))
    fourth = jnp.where(inner, far_mid, three_ends)
    fourth_x = across_x(fourth)

    near_kept = (z + core) % 2
    sel = jnp.stack([near_kept, (near_kept + inner) % 2, (z // 2 + y) % 2]).astype(jnp.int32)
    line, line_x = (own, near, third, fourth), (own_x, near_x, third_x, fourth_x)
    row_count, half_width = 2 * query_proj.shape[1], own.shape[1]

    def out(dtype, *shape):
        return jax.ShapeDtypeStruct(shape + (row_count, half_width), dtype)

    halves = (out(jnp.bfloat16, 2), out(jnp.float32))
    rows_type = jax.ShapeDtypeStruct((row_count, group_width), jnp.bfloat16)
    rows, give, keep = products(line_kernel, (rows_type,) + halves, sel, (query_proj, back), line, 3)
    given = to_sibling(give)
    here = across_y((keep + given[0].astype(jnp.float32)).astype(jnp.bfloat16))
    rows, here = lax.optimization_barrier((rows, here))
    give, keep = products(across_kernel, halves, sel, (rows,), line_x, 3)
    given_x = to_sibling(give)
    there = across_y((keep + given_x[0].astype(jnp.float32)).astype(jnp.bfloat16))
    (home,) = products(home_kernel, (out(jnp.float32, 2),), sel, (rows, given, given_x), line + line_x, 2)
    return finish(x.astype(jnp.int32)[None], home, here, there).reshape(query_proj.shape)


def solution(mesh):
    sizes = dict(mesh.shape)

    def per_device(query_proj, *rest):
        width = query_proj.shape[2]
        length = query_proj.shape[1] * sizes["ctx"]
        fits = sizes["ctx"] == 8 and sizes["ch"] == 4 and width == 1024 and length == 2048
        return (per_device_mesh if fits else per_device_plain)(query_proj, *rest)

    return jax.shard_map(
        per_device,
        mesh=mesh,
        in_specs=(
            P(None, "ctx", "ch"),
            P(None, "ctx", "ch"),
            P(None, "ctx", "ch"),
            P("ctx", "ch"),
            P("ch"),
            P("ch", "ctx"),
            P(),
            P(),
            P(None, "ctx"),
        ),
        out_specs=P(None, "ctx", "ch"),
        check_vma=False,
    )
```

```python
import functools
import math

import jax
import jax.numpy as jnp
from jax import lax
from jax.experimental import pallas as pl
from jax.experimental.pallas import tpu as pltpu
from jax.sharding import PartitionSpec as P

drop_level = 6554
keep_scale = 65536.0 / (65536.0 - 6554.0)


def mix_bits(hashed):
    hashed = hashed ^ lax.shift_right_logical(hashed, jnp.full_like(hashed, 16))
    hashed = hashed * jnp.int32(73244475)
    hashed = hashed ^ lax.shift_right_logical(hashed, jnp.full_like(hashed, 16))
    hashed = hashed * jnp.int32(73244475)
    hashed = hashed ^ lax.shift_right_logical(hashed, jnp.full_like(hashed, 16))
    return hashed


def keep_mask(drop_seed, drop_step, positions, channel_ids):
    seed_word = mix_bits(drop_seed[0] * jnp.int32(-1640531535) + drop_step[0])
    hashed = mix_bits(seed_word ^ mix_bits(positions))
    hashed = mix_bits(hashed ^ channel_ids * jnp.int32(668265263))
    low_bits = lax.shift_right_logical(hashed, jnp.full_like(hashed, 8)) & 65535
    return low_bits >= drop_level


def phase_table(count_rows, count_cols, period, direction):
    product = (
        jnp.arange(count_rows, dtype=jnp.int32)[:, None]
        * jnp.arange(count_cols, dtype=jnp.int32)[None, :]
        % period
    )
    angles = direction * 2.0 * math.pi * product.astype(jnp.float32) / period
    return (jnp.cos(angles), jnp.sin(angles))


def einsum_high(formula, left_part, right_part):
    return jnp.einsum(formula, left_part, right_part, precision=lax.Precision.HIGHEST)


def complex_einsum(formula, left_pair, right_pair):
    left_real, left_imag = left_pair
    right_real, right_imag = right_pair
    real_part = einsum_high(formula, left_real, right_real)
    imag_part = None
    if left_imag is not None and right_imag is not None:
        real_part = real_part - einsum_high(formula, left_imag, right_imag)
    if right_imag is not None:
        imag_part = einsum_high(formula, left_real, right_imag)
    cross_term = einsum_high(formula, left_imag, right_real)
    imag_part = cross_term if imag_part is None else imag_part + cross_term
    return (real_part, imag_part)


def complex_product(first_pair, second_pair):
    return (
        first_pair[0] * second_pair[0] - first_pair[1] * second_pair[1],
        first_pair[0] * second_pair[1] + first_pair[1] * second_pair[0],
    )


def grid_shape(length):
    columns = min(256, length)
    period = 2 * length
    return (columns, period // columns, period)


def forward_spectrum(signal_pair, length):
    columns, rows_all, period = grid_shape(length)
    half_rows = rows_all // 2
    shaped = tuple(
        (
            (
                None
                if part_item is None
                else part_item.reshape(part_item.shape[0], half_rows, columns, part_item.shape[2])
            )
            for part_item in signal_pair
        )
    )
    sectioned = complex_einsum(
        "kr,nrcd->ndkc", phase_table(rows_all, half_rows, rows_all, -1.0), shaped
    )
    sectioned = complex_product(sectioned, phase_table(rows_all, columns, period, -1.0))
    return complex_einsum("ndkc,cj->ndkj", sectioned, phase_table(columns, columns, columns, -1.0))


def inverse_signal(spectrum, length):
    columns, rows_all, period = grid_shape(length)
    half_rows = rows_all // 2
    sectioned = complex_einsum(
        "ndkj,jc->ndkc", spectrum, phase_table(columns, columns, columns, 1.0)
    )
    sectioned = complex_product(sectioned, phase_table(rows_all, columns, period, 1.0))
    last_table = phase_table(half_rows, rows_all, rows_all, 1.0)
    real_part = einsum_high("rk,ndkc->nrcd", last_table[0], sectioned[0]) - einsum_high(
        "rk,ndkc->nrcd", last_table[1], sectioned[1]
    )
    pieces_out = (real_part,)
    return tuple(
        (
            item_part.reshape(item_part.shape[0], length, item_part.shape[3]) / period
            for item_part in pieces_out
        )
    )


def convolve_plain(signal, filter_spec):
    length = signal.shape[1]
    spectrum = forward_spectrum((signal, None), length)
    product = complex_product(spectrum, filter_spec)
    return inverse_signal(product, length)[0]


def per_device_plain(
    query_proj,
    key_proj,
    value_proj,
    filter_taps,
    skip_gain,
    out_weight,
    drop_seed,
    drop_step,
    offsets,
):
    group_width = query_proj.shape[2]
    channel_ids = lax.axis_index("ch") * group_width + jnp.arange(group_width, dtype=jnp.int32)
    keep_flags = keep_mask(drop_seed, drop_step, offsets[:, :, None], channel_ids[None, None, :])
    gated = (
        key_proj.astype(jnp.float32)
        * value_proj.astype(jnp.float32)
        * jnp.where(keep_flags, keep_scale, 0.0)
    ).astype(jnp.bfloat16)
    tap_cols = lax.all_to_all(filter_taps, "ctx", split_axis=1, concat_axis=0, tiled=True)
    local_width = tap_cols.shape[1]
    skip_local = lax.dynamic_slice_in_dim(
        skip_gain, lax.axis_index("ctx") * local_width, local_width
    )
    filter_spec = forward_spectrum((tap_cols[None], None), tap_cols.shape[0])
    signal = lax.all_to_all(gated, "ctx", split_axis=2, concat_axis=1, tiled=True).astype(
        jnp.float32
    )
    convolved = convolve_plain(signal, filter_spec)
    mixed_cols = (convolved + skip_local * signal).astype(jnp.bfloat16)
    mixed = lax.all_to_all(mixed_cols, "ctx", split_axis=1, concat_axis=2, tiled=True)
    gate_out = (query_proj.astype(jnp.float32) * mixed.astype(jnp.float32)).astype(jnp.bfloat16)
    flat_rows = gate_out.reshape(-1, group_width)
    partial_value = jnp.dot(
        flat_rows,
        lax.all_gather(out_weight, "ctx", axis=1, tiled=True),
        preferred_element_type=jnp.float32,
    )
    summed = lax.psum_scatter(partial_value, "ch", scatter_dimension=1, tiled=True)
    return summed.astype(jnp.bfloat16).reshape(query_proj.shape)


SIDE = 64
WIDE = 2 * SIDE + 8
NARROW = SIDE + 8


def numbers(shape):
    return tuple(lax.broadcasted_iota(jnp.int32, shape, axis) for axis in range(len(shape)))


def waves(steps):
    angle = (steps % (SIDE * SIDE)).astype(jnp.float32) * (2.0 * math.pi / (SIDE * SIDE))
    return jnp.cos(angle), jnp.sin(angle)


def turn(row_part, col_part, sign):
    return (row_part - col_part) * (sign * SIDE * SIDE // 4)


def high_low(value, low):
    high = lax.reduce_precision(value, 8, 7)
    return jnp.where(low, value - high, high).astype(jnp.bfloat16)


def small_waves():
    half = SIDE // 2
    row, col = numbers((2 * SIDE, 4 * half))
    first = waves(SIDE * (col % half) * (row % SIDE) + turn(row // SIDE, col // half % 2, 1))
    n2, row = numbers((SIDE, 2 * SIDE))
    first_shift = waves(n2 * (row % SIDE))
    row, col = numbers((2 * SIDE, 4 * SIDE))
    steps = SIDE * (row % SIDE) * (col % SIDE)
    second = waves(steps + turn(row // SIDE, col // SIDE % 2, 1))[0]
    third = waves(steps + turn(row // SIDE, col // SIDE % 2, -1))[0]
    row, col = numbers((2 * half, 4 * SIDE))
    last = waves(SIDE * (row % half) * (col % SIDE) + turn(row // half, col // SIDE % 2, -1))
    n2, col = numbers((SIDE, 4 * SIDE))
    last_shift = waves(n2 * (col % SIDE))
    return first, first_shift, second, third, last, last_shift


def tables(small):
    first, first_shift, second, third, last, last_shift = small
    value = first[0][None] * first_shift[0][:, :, None] - first[1][None] * first_shift[1][:, :, None]
    first_table = high_low(value, numbers(value.shape)[2] >= SIDE)
    value = last[0][None] * last_shift[0][:, None, :] - last[1][None] * last_shift[1][:, None, :]
    last_table = high_low(value, numbers(value.shape)[2] >= 2 * SIDE)
    low = numbers(second.shape)[1] >= 2 * SIDE
    return first_table, high_low(second, low), high_low(third, low), last_table


def conv_kernel(
    got_ref, skip_ref, first_ref, second_ref, third_ref, last_ref, out_ref,
    sig_s, tap_s, mids_s, midt_s, back_s, res_s, *, blocks, tokens
):
    half = SIDE // 2
    parts = tokens // SIDE
    for d in range(blocks):
        for a in range(parts):
            n1 = d * parts + a
            for s in range(3):
                ref, row = (tap_s, n1) if s == 2 else (sig_s, s * half + n1)
                begin = s * tokens + a * SIDE
                ref[row * NARROW : row * NARROW + SIDE, :] = got_ref[d, begin : begin + SIDE, :].astype(jnp.float32)
    zero = jnp.zeros((half, 128), jnp.float32)

    def stage_first(i, carry):
        for u in range(16):
            n2 = i * 16 + u
            sig = sig_s[pl.ds(n2, 2 * half, stride=NARROW), :]
            tap = jnp.concatenate([tap_s[pl.ds(n2, half, stride=NARROW), :], zero], axis=0)
            right = jnp.concatenate([sig, tap], axis=1).astype(jnp.bfloat16)
            right = jnp.concatenate([right, right], axis=0)
            spec = jnp.dot(first_ref[n2], right, preferred_element_type=jnp.float32)
            rows = pl.ds(pl.multiple_of(n2 * WIDE, 8), 2 * SIDE)
            mids_s[rows, :] = spec[:, :128]
            midt_s[rows, :] = spec[:, 128:]
        return carry

    lax.fori_loop(0, SIDE // 16, stage_first, 0)
    skip = skip_ref[...]
    scale = 1.0 / (SIDE * SIDE)

    def column(ref, k):
        real = ref[pl.ds(k, SIDE, stride=WIDE), :]
        return jnp.concatenate([real, ref[pl.ds(SIDE + k, SIDE, stride=WIDE), :]], axis=0)

    def stage_spectrum(i, carry):
        for v in range(4):
            products = []
            for u in range(2):
                k1 = i * 8 + v * 2 + u
                right = jnp.concatenate([column(mids_s, k1), column(midt_s, k1)], axis=1).astype(jnp.bfloat16)
                right = jnp.concatenate([right, right], axis=0)
                spec = jnp.dot(second_ref[...], right, preferred_element_type=jnp.float32)
                sig_r, sig_i = spec[:SIDE, :128], spec[SIDE:, :128]
                tap_r, tap_i = (spec[:SIDE, 128:] + skip) * scale, spec[SIDE:, 128:] * scale
                pair = [sig_r * tap_r - sig_i * tap_i, sig_r * tap_i + sig_i * tap_r]
                products.append(jnp.concatenate(pair, axis=0).astype(jnp.bfloat16))
            right = jnp.concatenate(products, axis=1)
            right = jnp.concatenate([right, right], axis=0)
            back = jnp.dot(third_ref[...], right, preferred_element_type=jnp.float32)
            for u in range(2):
                k1 = i * 8 + v * 2 + u
                back_s[pl.ds(pl.multiple_of(k1 * WIDE, 8), 2 * SIDE), :] = back[:, u * 128 : (u + 1) * 128]
        return carry

    lax.fori_loop(0, SIDE // 8, stage_spectrum, 0)

    def stage_last(i, carry):
        for u in range(16):
            n2 = i * 16 + u
            right = column(back_s, n2).astype(jnp.bfloat16)
            right = jnp.concatenate([right, right], axis=0)
            res_s[pl.ds(n2, 2 * half, stride=NARROW), :] = jnp.dot(
                last_ref[n2], right, preferred_element_type=jnp.float32
            )
        return carry

    lax.fori_loop(0, SIDE // 16, stage_last, 0)
    for d in range(blocks):
        for a in range(parts):
            for s in range(2):
                row = (s * half + d * parts + a) * NARROW
                begin = s * tokens + a * SIDE
                out_ref[d, begin : begin + SIDE, :] = res_s[row : row + SIDE, :].astype(jnp.bfloat16)


def conv(got, skip, tabs):
    blocks, rows, lanes = got.shape
    tokens = rows // 3
    full = pl.BlockSpec(memory_space=pltpu.VMEM)
    return pl.pallas_call(
        functools.partial(conv_kernel, blocks=blocks, tokens=tokens),
        out_shape=jax.ShapeDtypeStruct((blocks, 2 * tokens, lanes), jnp.bfloat16),
        in_specs=[full] * 6,
        out_specs=full,
        scratch_shapes=[
            pltpu.VMEM((SIDE * NARROW, lanes), jnp.float32),
            pltpu.VMEM((SIDE // 2 * NARROW, lanes), jnp.float32),
            pltpu.VMEM((SIDE * WIDE, lanes), jnp.float32),
            pltpu.VMEM((SIDE * WIDE, lanes), jnp.float32),
            pltpu.VMEM((SIDE * WIDE, lanes), jnp.float32),
            pltpu.VMEM((SIDE * NARROW, lanes), jnp.float32),
        ],
        compiler_params=pltpu.CompilerParams(vmem_limit_bytes=32 << 20),
        cost_estimate=pl.CostEstimate(flops=1_000_000_000, bytes_accessed=1 << 20, transcendentals=0),
        name="long_conv",
    )(got, skip, *tabs)


VMEM = pl.BlockSpec(memory_space=pltpu.VMEM)
SMEM = pl.BlockSpec(memory_space=pltpu.SMEM)


def gate_kernel(word_ref, off_ref, key_ref, value_ref, taps_ref, out_ref, tok_s):
    tokens = off_ref.shape[1]
    block = pl.program_id(0)

    @pl.when(block == 0)
    def _():
        for s in range(2):
            row = mix_bits(off_ref[s : s + 1, :])
            row = mix_bits(row ^ word_ref[0])
            tok_s[s * tokens : (s + 1) * tokens, :] = jnp.broadcast_to(row, (128, tokens)).T

    count = out_ref.shape[0]
    for c in range(count):
        lanes = slice(c * 128, (c + 1) * 128)
        channel = word_ref[1] + (block * count + c) * 128 + lax.broadcasted_iota(jnp.int32, (1, 128), 1)
        channel = channel * jnp.int32(668265263)
        for s in range(2):
            rows = slice(s * tokens, (s + 1) * tokens)
            hashed = mix_bits(tok_s[rows, :] ^ channel)
            low_bits = lax.shift_right_logical(hashed, jnp.full_like(hashed, 8)) & 65535
            keep = jnp.where(low_bits >= drop_level, jnp.float32(keep_scale), jnp.float32(0.0))
            product = key_ref[s, :, lanes].astype(jnp.float32) * value_ref[s, :, lanes].astype(jnp.float32)
            out_ref[c, rows, :] = (product * keep).astype(jnp.bfloat16)
        out_ref[c, 2 * tokens : 3 * tokens, :] = taps_ref[:, lanes].astype(jnp.bfloat16)


def gate_and_pack(words, offsets, key_proj, value_proj, taps):
    _, tokens, width = key_proj.shape
    blocks = width // 128
    count = 4
    part = pl.BlockSpec((2, tokens, count * 128), lambda d: (0, 0, d))
    return pl.pallas_call(
        gate_kernel,
        grid=(blocks // count,),
        out_shape=jax.ShapeDtypeStruct((blocks, 3 * tokens, 128), jnp.bfloat16),
        in_specs=[
            SMEM,
            pl.BlockSpec((2, tokens), lambda d: (0, 0)),
            part,
            part,
            pl.BlockSpec((tokens, count * 128), lambda d: (0, d)),
        ],
        out_specs=pl.BlockSpec((count, 3 * tokens, 128), lambda d: (d, 0, 0)),
        scratch_shapes=[pltpu.VMEM((2 * tokens, 128), jnp.int32)],
        name="gate_and_pack",
    )(words, offsets, key_proj, value_proj, taps)


def gate_rows(query_ref, mixed_ref, rows_ref):
    tokens = query_ref.shape[1]
    for c in range(mixed_ref.shape[0]):
        lanes = slice(c * 128, (c + 1) * 128)
        for s in range(2):
            rows = slice(s * tokens, (s + 1) * tokens)
            mixed = mixed_ref[c, rows, :].astype(jnp.float32)
            rows_ref[rows, lanes] = (query_ref[s, :, lanes].astype(jnp.float32) * mixed).astype(jnp.bfloat16)


def fetch(sources, index, held, sem):
    for place, source in enumerate(sources):

        @pl.when(index == place)
        def _():
            pltpu.make_async_copy(source, held, sem).start()


def arrived(sources, held, sem):
    pltpu.make_async_copy(sources[0], held, sem).wait()


def place_of(sel_ref, pair, mine):
    kept = jnp.where(pair == 0, sel_ref[0], sel_ref[1])
    return 2 * pair + (kept if mine else 1 - kept)


def dots_into(rows_ref, sources, wanted, held, sems, store, before=lambda: None):
    for i, (side, place) in enumerate(wanted):
        fetch(sources[4 * side : 4 * side + 4], place, held.at[i], sems.at[i])
    before()
    for i in range(len(wanted)):
        arrived(sources, held.at[i], sems.at[i])
        store(i, jnp.dot(rows_ref[...], held[i], preferred_element_type=jnp.float32))


def away_kernel(sel_ref, query_ref, mixed_ref, *refs):
    sources, (rows_ref, give_ref, keep_ref, held, sems) = refs[:8], refs[8:]
    away = 1 - sel_ref[2]
    wanted = [(side, place_of(sel_ref, away, mine)) for mine in (False, True) for side in (0, 1)]

    def store(i, part):
        if i < 2:
            give_ref[i] = part.astype(give_ref.dtype)
        else:
            keep_ref[i - 2] = part

    before = functools.partial(gate_rows, query_ref, mixed_ref, rows_ref)
    dots_into(rows_ref, sources, wanted, held, sems, store, before)


def give_kernel(sel_ref, rows_ref, *refs):
    sources, (give_ref, held, sems) = refs[:8], refs[8:]
    wanted = [(side, place_of(sel_ref, sel_ref[2], False)) for side in (0, 1)]

    def store(i, part):
        give_ref[i] = part.astype(give_ref.dtype)

    dots_into(rows_ref, sources, wanted, held, sems, store)


def home_kernel(sel_ref, rows_ref, given_ref, *refs):
    sources, (out_ref, held, sems) = refs[:8], refs[8:]
    wanted = [(side, place_of(sel_ref, sel_ref[2], True)) for side in (0, 1)]

    def store(i, part):
        out_ref[i] = part + given_ref[i].astype(jnp.float32)

    dots_into(rows_ref, sources, wanted, held, sems, store)


def products(kernel, outs, sel, left, weights, dots):
    rows, (depth, width) = outs[-1].shape[-2], weights[0].shape
    return pl.pallas_call(
        kernel,
        out_shape=outs,
        in_specs=[SMEM] + [VMEM] * len(left) + [pl.BlockSpec(memory_space=pl.ANY)] * len(weights),
        out_specs=(VMEM,) * len(outs),
        scratch_shapes=[
            pltpu.VMEM((dots, depth, width), jnp.bfloat16),
            pltpu.SemaphoreType.DMA((dots,)),
        ],
        compiler_params=pltpu.CompilerParams(vmem_limit_bytes=56 << 20),
        cost_estimate=pl.CostEstimate(
            flops=2 * dots * rows * depth * width, bytes_accessed=8 << 20, transcendentals=0
        ),
        name="products",
    )(sel, *left, *weights)


def finish_kernel(x_ref, home_ref, away_ref, out_ref):
    width = home_ref.shape[2]
    for half in range(2):
        total = (home_ref[half] + away_ref[half].astype(jnp.float32)).astype(jnp.bfloat16)

        @pl.when(x_ref[0] == half)
        def _():
            out_ref[:, :width] = total

        @pl.when(x_ref[0] != half)
        def _():
            out_ref[:, width:] = total


def finish(x, home, away):
    _, rows, width = home.shape
    return pl.pallas_call(
        finish_kernel,
        out_shape=jax.ShapeDtypeStruct((rows, 2 * width), jnp.bfloat16),
        in_specs=[SMEM, VMEM, VMEM],
        out_specs=VMEM,
        compiler_params=pltpu.CompilerParams(vmem_limit_bytes=16 << 20),
        name="finish",
    )(x, home, away)


def per_device_mesh(
    query_proj,
    key_proj,
    value_proj,
    filter_taps,
    skip_gain,
    out_weight,
    drop_seed,
    drop_step,
    offsets,
):
    group_width = query_proj.shape[2]
    ctx, ch = lax.axis_index("ctx"), lax.axis_index("ch")
    z, x, y, core = ctx // 2, ctx % 2, ch // 2, ch % 2

    def along_z(value, pairs):
        return lax.ppermute(value, "ctx", [(2 * a + k, 2 * b + k) for a, b in pairs for k in (0, 1)])

    def across_x(value):
        return lax.ppermute(value, "ctx", [(i, i ^ 1) for i in range(8)])

    def to_sibling(value):
        return lax.ppermute(value, "ch", [(j, j ^ 1) for j in range(4)])

    def across_y(value):
        return lax.ppermute(value, "ch", [(j, j ^ 2) for j in range(4)])

    own = out_weight
    middle = along_z(own, [(1, 2), (2, 1)])
    seed_word = mix_bits(drop_seed[0] * jnp.int32(-1640531535) + drop_step[0])
    words = jnp.stack([seed_word, ch * group_width])
    packed = gate_and_pack(words, offsets, key_proj, value_proj, filter_taps)
    near = along_z(own, [(0, 1), (1, 0), (2, 3), (3, 2)])
    own_x = across_x(own)
    got = lax.all_to_all(packed, "ctx", split_axis=0, concat_axis=0, tiled=True)

    near, middle, small = lax.optimization_barrier((near, middle, small_waves()))
    far_mid = along_z(near, [(2, 1), (1, 2)])
    far_ends = along_z(middle, [(1, 0), (2, 3)])
    near, own_x = lax.optimization_barrier((near, own_x))
    near_x = across_x(near)
    tabs = tables(small)
    inner = (z == 1) | (z == 2)
    third = jnp.where(inner, middle, far_ends)
    got, third, far_mid, tabs = lax.optimization_barrier((got, third, far_mid, tabs))
    three_ends = along_z(far_mid, [(1, 0), (2, 3)])
    third, near_x = lax.optimization_barrier((third, near_x))
    third_x = across_x(third)
    skip_local = lax.dynamic_slice_in_dim(skip_gain, ctx * 128, 128)
    mixed = conv(got, skip_local[None, :], tabs)
    back = lax.all_to_all(mixed, "ctx", split_axis=0, concat_axis=0, tiled=True)
    three_ends, third_x, mixed = lax.optimization_barrier((three_ends, third_x, mixed))
    fourth = jnp.where(inner, far_mid, three_ends)
    fourth_x = across_x(fourth)

    near_kept = (z + core) % 2
    sel = jnp.stack([near_kept, (near_kept + inner) % 2, (z // 2 + y) % 2]).astype(jnp.int32)
    weights = (own, near, third, fourth, own_x, near_x, third_x, fourth_x)
    row_count, half_width = 2 * query_proj.shape[1], own.shape[1]

    def halves(dtype):
        return jax.ShapeDtypeStruct((2, row_count, half_width), dtype)

    outs = (jax.ShapeDtypeStruct((row_count, group_width), jnp.bfloat16), halves(jnp.bfloat16), halves(jnp.float32))
    rows, give, keep = products(away_kernel, outs, sel, (query_proj, back), weights, 4)
    away = across_y((keep + to_sibling(give).astype(jnp.float32)).astype(jnp.bfloat16))
    (give,) = products(give_kernel, (halves(jnp.bfloat16),), sel, (rows,), weights, 2)
    (home,) = products(home_kernel, (halves(jnp.float32),), sel, (rows, to_sibling(give)), weights, 2)
    return finish(x.astype(jnp.int32)[None], home, away).reshape(query_proj.shape)


def solution(mesh):
    sizes = dict(mesh.shape)

    def per_device(query_proj, *rest):
        width = query_proj.shape[2]
        length = query_proj.shape[1] * sizes["ctx"]
        fits = sizes["ctx"] == 8 and sizes["ch"] == 4 and width == 1024 and length == 2048
        return (per_device_mesh if fits else per_device_plain)(query_proj, *rest)

    return jax.shard_map(
        per_device,
        mesh=mesh,
        in_specs=(
            P(None, "ctx", "ch"),
            P(None, "ctx", "ch"),
            P(None, "ctx", "ch"),
            P("ctx", "ch"),
            P("ch"),
            P("ch", "ctx"),
            P(),
            P(),
            P(None, "ctx"),
        ),
        out_specs=P(None, "ctx", "ch"),
        check_vma=False,
    )
```

```python
import functools
import math

import jax
import jax.numpy as jnp
from jax import lax
from jax.experimental import pallas as pl
from jax.experimental.pallas import tpu as pltpu
from jax.sharding import PartitionSpec as P

drop_level = 6554
keep_scale = 65536.0 / (65536.0 - 6554.0)


def mix_bits(hashed):
    hashed = hashed ^ lax.shift_right_logical(hashed, jnp.full_like(hashed, 16))
    hashed = hashed * jnp.int32(73244475)
    hashed = hashed ^ lax.shift_right_logical(hashed, jnp.full_like(hashed, 16))
    hashed = hashed * jnp.int32(73244475)
    hashed = hashed ^ lax.shift_right_logical(hashed, jnp.full_like(hashed, 16))
    return hashed


def keep_mask(drop_seed, drop_step, positions, channel_ids):
    seed_word = mix_bits(drop_seed[0] * jnp.int32(-1640531535) + drop_step[0])
    hashed = mix_bits(seed_word ^ mix_bits(positions))
    hashed = mix_bits(hashed ^ channel_ids * jnp.int32(668265263))
    low_bits = lax.shift_right_logical(hashed, jnp.full_like(hashed, 8)) & 65535
    return low_bits >= drop_level


def phase_table(count_rows, count_cols, period, direction):
    product = (
        jnp.arange(count_rows, dtype=jnp.int32)[:, None]
        * jnp.arange(count_cols, dtype=jnp.int32)[None, :]
        % period
    )
    angles = direction * 2.0 * math.pi * product.astype(jnp.float32) / period
    return (jnp.cos(angles), jnp.sin(angles))


def einsum_high(formula, left_part, right_part):
    return jnp.einsum(formula, left_part, right_part, precision=lax.Precision.HIGHEST)


def complex_einsum(formula, left_pair, right_pair):
    left_real, left_imag = left_pair
    right_real, right_imag = right_pair
    real_part = einsum_high(formula, left_real, right_real)
    imag_part = None
    if left_imag is not None and right_imag is not None:
        real_part = real_part - einsum_high(formula, left_imag, right_imag)
    if right_imag is not None:
        imag_part = einsum_high(formula, left_real, right_imag)
    cross_term = einsum_high(formula, left_imag, right_real)
    imag_part = cross_term if imag_part is None else imag_part + cross_term
    return (real_part, imag_part)


def complex_product(first_pair, second_pair):
    return (
        first_pair[0] * second_pair[0] - first_pair[1] * second_pair[1],
        first_pair[0] * second_pair[1] + first_pair[1] * second_pair[0],
    )


def grid_shape(length):
    columns = min(256, length)
    period = 2 * length
    return (columns, period // columns, period)


def forward_spectrum(signal_pair, length):
    columns, rows_all, period = grid_shape(length)
    half_rows = rows_all // 2
    shaped = tuple(
        (
            (
                None
                if part_item is None
                else part_item.reshape(part_item.shape[0], half_rows, columns, part_item.shape[2])
            )
            for part_item in signal_pair
        )
    )
    sectioned = complex_einsum(
        "kr,nrcd->ndkc", phase_table(rows_all, half_rows, rows_all, -1.0), shaped
    )
    sectioned = complex_product(sectioned, phase_table(rows_all, columns, period, -1.0))
    return complex_einsum("ndkc,cj->ndkj", sectioned, phase_table(columns, columns, columns, -1.0))


def inverse_signal(spectrum, length):
    columns, rows_all, period = grid_shape(length)
    half_rows = rows_all // 2
    sectioned = complex_einsum(
        "ndkj,jc->ndkc", spectrum, phase_table(columns, columns, columns, 1.0)
    )
    sectioned = complex_product(sectioned, phase_table(rows_all, columns, period, 1.0))
    last_table = phase_table(half_rows, rows_all, rows_all, 1.0)
    real_part = einsum_high("rk,ndkc->nrcd", last_table[0], sectioned[0]) - einsum_high(
        "rk,ndkc->nrcd", last_table[1], sectioned[1]
    )
    pieces_out = (real_part,)
    return tuple(
        (
            item_part.reshape(item_part.shape[0], length, item_part.shape[3]) / period
            for item_part in pieces_out
        )
    )


def convolve_plain(signal, filter_spec):
    length = signal.shape[1]
    spectrum = forward_spectrum((signal, None), length)
    product = complex_product(spectrum, filter_spec)
    return inverse_signal(product, length)[0]


def per_device_plain(
    query_proj,
    key_proj,
    value_proj,
    filter_taps,
    skip_gain,
    out_weight,
    drop_seed,
    drop_step,
    offsets,
):
    group_width = query_proj.shape[2]
    channel_ids = lax.axis_index("ch") * group_width + jnp.arange(group_width, dtype=jnp.int32)
    keep_flags = keep_mask(drop_seed, drop_step, offsets[:, :, None], channel_ids[None, None, :])
    gated = (
        key_proj.astype(jnp.float32)
        * value_proj.astype(jnp.float32)
        * jnp.where(keep_flags, keep_scale, 0.0)
    ).astype(jnp.bfloat16)
    tap_cols = lax.all_to_all(filter_taps, "ctx", split_axis=1, concat_axis=0, tiled=True)
    local_width = tap_cols.shape[1]
    skip_local = lax.dynamic_slice_in_dim(
        skip_gain, lax.axis_index("ctx") * local_width, local_width
    )
    filter_spec = forward_spectrum((tap_cols[None], None), tap_cols.shape[0])
    signal = lax.all_to_all(gated, "ctx", split_axis=2, concat_axis=1, tiled=True).astype(
        jnp.float32
    )
    convolved = convolve_plain(signal, filter_spec)
    mixed_cols = (convolved + skip_local * signal).astype(jnp.bfloat16)
    mixed = lax.all_to_all(mixed_cols, "ctx", split_axis=1, concat_axis=2, tiled=True)
    gate_out = (query_proj.astype(jnp.float32) * mixed.astype(jnp.float32)).astype(jnp.bfloat16)
    flat_rows = gate_out.reshape(-1, group_width)
    partial_value = jnp.dot(
        flat_rows,
        lax.all_gather(out_weight, "ctx", axis=1, tiled=True),
        preferred_element_type=jnp.float32,
    )
    summed = lax.psum_scatter(partial_value, "ch", scatter_dimension=1, tiled=True)
    return summed.astype(jnp.bfloat16).reshape(query_proj.shape)


SIDE = 64
WIDE = 2 * SIDE + 8
NARROW = SIDE + 8


def numbers(shape):
    return tuple(lax.broadcasted_iota(jnp.int32, shape, axis) for axis in range(len(shape)))


def waves(steps):
    angle = (steps % (SIDE * SIDE)).astype(jnp.float32) * (2.0 * math.pi / (SIDE * SIDE))
    return jnp.cos(angle), jnp.sin(angle)


def turn(row_part, col_part, sign):
    return (row_part - col_part) * (sign * SIDE * SIDE // 4)


def high_low(value, low):
    high = lax.reduce_precision(value, 8, 7)
    return jnp.where(low, value - high, high).astype(jnp.bfloat16)


def small_waves():
    half = SIDE // 2
    row, col = numbers((2 * SIDE, 4 * half))
    first = waves(SIDE * (col % half) * (row % SIDE) + turn(row // SIDE, col // half % 2, 1))
    n2, row = numbers((SIDE, 2 * SIDE))
    first_shift = waves(n2 * (row % SIDE))
    row, col = numbers((2 * SIDE, 4 * SIDE))
    steps = SIDE * (row % SIDE) * (col % SIDE)
    second = waves(steps + turn(row // SIDE, col // SIDE % 2, 1))[0]
    third = waves(steps + turn(row // SIDE, col // SIDE % 2, -1))[0]
    row, col = numbers((2 * half, 4 * SIDE))
    last = waves(SIDE * (row % half) * (col % SIDE) + turn(row // half, col // SIDE % 2, -1))
    n2, col = numbers((SIDE, 4 * SIDE))
    last_shift = waves(n2 * (col % SIDE))
    return first, first_shift, second, third, last, last_shift


def tables(small):
    first, first_shift, second, third, last, last_shift = small
    value = first[0][None] * first_shift[0][:, :, None] - first[1][None] * first_shift[1][:, :, None]
    first_table = high_low(value, numbers(value.shape)[2] >= SIDE)
    value = last[0][None] * last_shift[0][:, None, :] - last[1][None] * last_shift[1][:, None, :]
    last_table = high_low(value, numbers(value.shape)[2] >= 2 * SIDE)
    low = numbers(second.shape)[1] >= 2 * SIDE
    return first_table, high_low(second, low), high_low(third, low), last_table


def conv_kernel(
    got_ref, skip_ref, source_ref, second_ref, third_ref, last_ref, out_ref,
    sig_s, tap_s, mids_s, midt_s, back_s, res_s, first_ref, sem, *, blocks, tokens
):
    half = SIDE // 2
    copy = pltpu.make_async_copy(source_ref, first_ref, sem)
    copy.start()
    parts = tokens // SIDE
    for d in range(blocks):
        for a in range(parts):
            n1 = d * parts + a
            for s in range(3):
                ref, row = (tap_s, n1) if s == 2 else (sig_s, s * half + n1)
                begin = s * tokens + a * SIDE
                ref[row * NARROW : row * NARROW + SIDE, :] = got_ref[d, begin : begin + SIDE, :].astype(jnp.float32)
    zero = jnp.zeros((half, 128), jnp.float32)
    copy.wait()

    def stage_first(i, carry):
        for u in range(16):
            n2 = i * 16 + u
            sig = sig_s[pl.ds(n2, 2 * half, stride=NARROW), :]
            tap = jnp.concatenate([tap_s[pl.ds(n2, half, stride=NARROW), :], zero], axis=0)
            right = jnp.concatenate([sig, tap], axis=1).astype(jnp.bfloat16)
            right = jnp.concatenate([right, right], axis=0)
            spec = jnp.dot(first_ref[n2], right, preferred_element_type=jnp.float32)
            rows = pl.ds(pl.multiple_of(n2 * WIDE, 8), 2 * SIDE)
            mids_s[rows, :] = spec[:, :128]
            midt_s[rows, :] = spec[:, 128:]
        return carry

    lax.fori_loop(0, SIDE // 16, stage_first, 0)
    skip = skip_ref[...]
    scale = 1.0 / (SIDE * SIDE)

    def column(ref, k):
        real = ref[pl.ds(k, SIDE, stride=WIDE), :]
        return jnp.concatenate([real, ref[pl.ds(SIDE + k, SIDE, stride=WIDE), :]], axis=0)

    def stage_spectrum(i, carry):
        for v in range(4):
            products = []
            for u in range(2):
                k1 = i * 8 + v * 2 + u
                right = jnp.concatenate([column(mids_s, k1), column(midt_s, k1)], axis=1).astype(jnp.bfloat16)
                right = jnp.concatenate([right, right], axis=0)
                spec = jnp.dot(second_ref[...], right, preferred_element_type=jnp.float32)
                sig_r, sig_i = spec[:SIDE, :128], spec[SIDE:, :128]
                tap_r, tap_i = (spec[:SIDE, 128:] + skip) * scale, spec[SIDE:, 128:] * scale
                pair = [sig_r * tap_r - sig_i * tap_i, sig_r * tap_i + sig_i * tap_r]
                products.append(jnp.concatenate(pair, axis=0).astype(jnp.bfloat16))
            right = jnp.concatenate(products, axis=1)
            right = jnp.concatenate([right, right], axis=0)
            back = jnp.dot(third_ref[...], right, preferred_element_type=jnp.float32)
            for u in range(2):
                k1 = i * 8 + v * 2 + u
                back_s[pl.ds(pl.multiple_of(k1 * WIDE, 8), 2 * SIDE), :] = back[:, u * 128 : (u + 1) * 128]
        return carry

    lax.fori_loop(0, SIDE // 8, stage_spectrum, 0)

    def stage_last(i, carry):
        for u in range(16):
            n2 = i * 16 + u
            right = column(back_s, n2).astype(jnp.bfloat16)
            right = jnp.concatenate([right, right], axis=0)
            res_s[pl.ds(n2, 2 * half, stride=NARROW), :] = jnp.dot(
                last_ref[n2], right, preferred_element_type=jnp.float32
            )
        return carry

    lax.fori_loop(0, SIDE // 16, stage_last, 0)
    for d in range(blocks):
        for a in range(parts):
            for s in range(2):
                row = (s * half + d * parts + a) * NARROW
                begin = s * tokens + a * SIDE
                out_ref[d, begin : begin + SIDE, :] = res_s[row : row + SIDE, :].astype(jnp.bfloat16)


def conv(got, skip, tabs):
    blocks, rows, lanes = got.shape
    tokens = rows // 3
    full = pl.BlockSpec(memory_space=pltpu.VMEM)
    return pl.pallas_call(
        functools.partial(conv_kernel, blocks=blocks, tokens=tokens),
        out_shape=jax.ShapeDtypeStruct((blocks, 2 * tokens, lanes), jnp.bfloat16),
        in_specs=[full] * 2 + [pl.BlockSpec(memory_space=pl.ANY)] + [full] * 3,
        out_specs=full,
        scratch_shapes=[
            pltpu.VMEM((SIDE * NARROW, lanes), jnp.float32),
            pltpu.VMEM((SIDE // 2 * NARROW, lanes), jnp.float32),
            pltpu.VMEM((SIDE * WIDE, lanes), jnp.float32),
            pltpu.VMEM((SIDE * WIDE, lanes), jnp.float32),
            pltpu.VMEM((SIDE * WIDE, lanes), jnp.float32),
            pltpu.VMEM((SIDE * NARROW, lanes), jnp.float32),
            pltpu.VMEM(tabs[0].shape, jnp.bfloat16),
            pltpu.SemaphoreType.DMA,
        ],
        compiler_params=pltpu.CompilerParams(vmem_limit_bytes=32 << 20),
        cost_estimate=pl.CostEstimate(flops=1_000_000_000, bytes_accessed=1 << 20, transcendentals=0),
        name="long_conv",
    )(got, skip, *tabs)


VMEM = pl.BlockSpec(memory_space=pltpu.VMEM)
SMEM = pl.BlockSpec(memory_space=pltpu.SMEM)


def gate_kernel(word_ref, off_ref, key_ref, value_ref, taps_ref, out_ref, tok_s):
    tokens = off_ref.shape[1]
    block = pl.program_id(0)

    @pl.when(block == 0)
    def _():
        for s in range(2):
            row = mix_bits(off_ref[s : s + 1, :])
            row = mix_bits(row ^ word_ref[0])
            tok_s[s * tokens : (s + 1) * tokens, :] = jnp.broadcast_to(row, (128, tokens)).T

    count = out_ref.shape[0]
    for c in range(count):
        lanes = slice(c * 128, (c + 1) * 128)
        channel = word_ref[1] + (block * count + c) * 128 + lax.broadcasted_iota(jnp.int32, (1, 128), 1)
        channel = channel * jnp.int32(668265263)
        for s in range(2):
            rows = slice(s * tokens, (s + 1) * tokens)
            hashed = mix_bits(tok_s[rows, :] ^ channel)
            low_bits = lax.shift_right_logical(hashed, jnp.full_like(hashed, 8)) & 65535
            keep = jnp.where(low_bits >= drop_level, jnp.float32(keep_scale), jnp.float32(0.0))
            product = key_ref[s, :, lanes].astype(jnp.float32) * value_ref[s, :, lanes].astype(jnp.float32)
            out_ref[c, rows, :] = (product * keep).astype(jnp.bfloat16)
        out_ref[c, 2 * tokens : 3 * tokens, :] = taps_ref[:, lanes].astype(jnp.bfloat16)


def gate_and_pack(words, offsets, key_proj, value_proj, taps):
    _, tokens, width = key_proj.shape
    blocks = width // 128
    count = 4
    part = pl.BlockSpec((2, tokens, count * 128), lambda d: (0, 0, d))
    return pl.pallas_call(
        gate_kernel,
        grid=(blocks // count,),
        out_shape=jax.ShapeDtypeStruct((blocks, 3 * tokens, 128), jnp.bfloat16),
        in_specs=[
            SMEM,
            pl.BlockSpec((2, tokens), lambda d: (0, 0)),
            part,
            part,
            pl.BlockSpec((tokens, count * 128), lambda d: (0, d)),
        ],
        out_specs=pl.BlockSpec((count, 3 * tokens, 128), lambda d: (d, 0, 0)),
        scratch_shapes=[pltpu.VMEM((2 * tokens, 128), jnp.int32)],
        name="gate_and_pack",
    )(words, offsets, key_proj, value_proj, taps)


def gate_rows(query_ref, mixed_ref, rows_ref):
    tokens = query_ref.shape[1]
    for c in range(mixed_ref.shape[0]):
        lanes = slice(c * 128, (c + 1) * 128)
        for s in range(2):
            rows = slice(s * tokens, (s + 1) * tokens)
            mixed = mixed_ref[c, rows, :].astype(jnp.float32)
            rows_ref[rows, lanes] = (query_ref[s, :, lanes].astype(jnp.float32) * mixed).astype(jnp.bfloat16)


def fetch(sources, index, held, sem):
    for place, source in enumerate(sources):

        @pl.when(index == place)
        def _():
            pltpu.make_async_copy(source, held, sem).start()


def arrived(sources, held, sem):
    pltpu.make_async_copy(sources[0], held, sem).wait()


def place_of(sel_ref, pair, mine):
    kept = jnp.where(pair == 0, sel_ref[0], sel_ref[1])
    return 2 * pair + (kept if mine else 1 - kept)


def dots_into(rows_ref, sources, wanted, held, sems, store, before=lambda: None):
    for i, (side, place) in enumerate(wanted):
        fetch(sources[4 * side : 4 * side + 4], place, held.at[i], sems.at[i])
    before()
    for i in range(len(wanted)):
        arrived(sources, held.at[i], sems.at[i])
        store(i, jnp.dot(rows_ref[...], held[i], preferred_element_type=jnp.float32))


def half_products(sel_ref, rows_ref, sources, give_ref, keep_ref, held, sems, before=lambda: None):
    home, away = sel_ref[2], 1 - sel_ref[2]
    wanted = [(0, place_of(sel_ref, pair, mine)) for pair, mine in ((away, False), (home, False), (away, True))]

    def store(i, part):
        if i < 2:
            give_ref[i] = part.astype(give_ref.dtype)
        else:
            keep_ref[...] = part

    dots_into(rows_ref, sources, wanted, held, sems, store, before)


def line_kernel(sel_ref, query_ref, mixed_ref, *refs):
    sources, (rows_ref, give_ref, keep_ref, held, sems) = refs[:4], refs[4:]
    before = functools.partial(gate_rows, query_ref, mixed_ref, rows_ref)
    half_products(sel_ref, rows_ref, sources, give_ref, keep_ref, held, sems, before)


def across_kernel(sel_ref, rows_ref, *refs):
    sources, (give_ref, keep_ref, held, sems) = refs[:4], refs[4:]
    half_products(sel_ref, rows_ref, sources, give_ref, keep_ref, held, sems)


def home_kernel(sel_ref, rows_ref, given_ref, given_x_ref, *refs):
    sources, (out_ref, held, sems) = refs[:8], refs[8:]
    wanted = [(side, place_of(sel_ref, sel_ref[2], True)) for side in (0, 1)]

    def store(i, part):
        out_ref[i] = part + (given_ref, given_x_ref)[i][1].astype(jnp.float32)

    dots_into(rows_ref, sources, wanted, held, sems, store)


def products(kernel, outs, sel, left, weights, dots, grant=56):
    rows, (depth, width) = outs[-1].shape[-2], weights[0].shape
    return pl.pallas_call(
        kernel,
        out_shape=outs,
        in_specs=[SMEM] + [VMEM] * len(left) + [pl.BlockSpec(memory_space=pl.ANY)] * len(weights),
        out_specs=(VMEM,) * len(outs),
        scratch_shapes=[
            pltpu.VMEM((dots, depth, width), jnp.bfloat16),
            pltpu.SemaphoreType.DMA((dots,)),
        ],
        compiler_params=pltpu.CompilerParams(vmem_limit_bytes=grant << 20),
        cost_estimate=pl.CostEstimate(
            flops=2 * dots * rows * depth * width, bytes_accessed=8 << 20, transcendentals=0
        ),
        name="products",
    )(sel, *left, *weights)


def finish_kernel(x_ref, home_ref, here_ref, there_ref, out_ref):
    width = here_ref.shape[1]
    for half, away_ref in enumerate((here_ref, there_ref)):
        total = (home_ref[half] + away_ref[...].astype(jnp.float32)).astype(jnp.bfloat16)

        @pl.when(x_ref[0] == half)
        def _():
            out_ref[:, :width] = total

        @pl.when(x_ref[0] != half)
        def _():
            out_ref[:, width:] = total


def finish(x, home, here, there):
    rows, width = here.shape
    return pl.pallas_call(
        finish_kernel,
        out_shape=jax.ShapeDtypeStruct((rows, 2 * width), jnp.bfloat16),
        in_specs=[SMEM, VMEM, VMEM, VMEM],
        out_specs=VMEM,
        compiler_params=pltpu.CompilerParams(vmem_limit_bytes=16 << 20),
        name="finish",
    )(x, home, here, there)


def per_device_mesh(
    query_proj,
    key_proj,
    value_proj,
    filter_taps,
    skip_gain,
    out_weight,
    drop_seed,
    drop_step,
    offsets,
):
    group_width = query_proj.shape[2]
    ctx, ch = lax.axis_index("ctx"), lax.axis_index("ch")
    z, x, y, core = ctx // 2, ctx % 2, ch // 2, ch % 2

    def along_z(value, pairs):
        return lax.ppermute(value, "ctx", [(2 * a + k, 2 * b + k) for a, b in pairs for k in (0, 1)])

    def across_x(value):
        return lax.ppermute(value, "ctx", [(i, i ^ 1) for i in range(8)])

    def to_sibling(value):
        return lax.ppermute(value, "ch", [(j, j ^ 1) for j in range(4)])

    def across_y(value):
        return lax.ppermute(value, "ch", [(j, j ^ 2) for j in range(4)])

    own = out_weight
    near = along_z(own, [(0, 1), (1, 0), (2, 3), (3, 2)])
    middle = along_z(own, [(1, 2), (2, 1)])
    seed_word = mix_bits(drop_seed[0] * jnp.int32(-1640531535) + drop_step[0])
    words = jnp.stack([seed_word, ch * group_width])
    packed = gate_and_pack(words, offsets, key_proj, value_proj, filter_taps)
    got = lax.all_to_all(packed, "ctx", split_axis=0, concat_axis=0, tiled=True)
    own, packed = lax.optimization_barrier((own, packed))
    own_x = across_x(own)

    near, small = lax.optimization_barrier((near, small_waves()))
    far_mid = along_z(near, [(2, 1), (1, 2)])
    tabs = tables(small)
    middle, tabs = lax.optimization_barrier((middle, tabs))
    far_ends = along_z(middle, [(1, 0), (2, 3)])
    near, own_x, tabs = lax.optimization_barrier((near, own_x, tabs))
    near_x = across_x(near)
    inner = (z == 1) | (z == 2)
    third = jnp.where(inner, middle, far_ends)
    got, third, far_mid, tabs = lax.optimization_barrier((got, third, far_mid, tabs))
    three_ends = along_z(far_mid, [(1, 0), (2, 3)])
    third, near_x = lax.optimization_barrier((third, near_x))
    third_x = across_x(third)
    skip_local = lax.dynamic_slice_in_dim(skip_gain, ctx * 128, 128)
    mixed = conv(got, skip_local[None, :], tabs)
    back = lax.all_to_all(mixed, "ctx", split_axis=0, concat_axis=0, tiled=True)
    three_ends, third_x, mixed = lax.optimization_barrier((three_ends, third_x, mixed))
    fourth = jnp.where(inner, far_mid, three_ends)
    fourth_x = across_x(fourth)

    near_kept = (z + core) % 2
    sel = jnp.stack([near_kept, (near_kept + inner) % 2, (z // 2 + y) % 2]).astype(jnp.int32)
    line, line_x = (own, near, third, fourth), (own_x, near_x, third_x, fourth_x)
    row_count, half_width = 2 * query_proj.shape[1], own.shape[1]

    def out(dtype, *lead):
        return jax.ShapeDtypeStruct(lead + (row_count, half_width), dtype)

    outs = (out(jnp.bfloat16, 2), out(jnp.float32))
    rows_type = jax.ShapeDtypeStruct((row_count, group_width), jnp.bfloat16)
    rows, give, keep = products(line_kernel, (rows_type,) + outs, sel, (query_proj, back), line, 3)
    given = to_sibling(give)
    here = across_y((keep + given[0].astype(jnp.float32)).astype(jnp.bfloat16))
    give, keep = products(across_kernel, outs, sel, (rows,), line_x, 3)
    given_x = to_sibling(give)
    there = across_y((keep + given_x[0].astype(jnp.float32)).astype(jnp.bfloat16))
    (home,) = products(home_kernel, (out(jnp.float32, 2),), sel, (rows, given, given_x), line + line_x, 2, 24)
    return finish(x.astype(jnp.int32)[None], home, here, there).reshape(query_proj.shape)


def solution(mesh):
    sizes = dict(mesh.shape)

    def per_device(query_proj, *rest):
        width = query_proj.shape[2]
        length = query_proj.shape[1] * sizes["ctx"]
        fits = sizes["ctx"] == 8 and sizes["ch"] == 4 and width == 1024 and length == 2048
        return (per_device_mesh if fits else per_device_plain)(query_proj, *rest)

    return jax.shard_map(
        per_device,
        mesh=mesh,
        in_specs=(
            P(None, "ctx", "ch"),
            P(None, "ctx", "ch"),
            P(None, "ctx", "ch"),
            P("ctx", "ch"),
            P("ch"),
            P("ch", "ctx"),
            P(),
            P(),
            P(None, "ctx"),
        ),
        out_specs=P(None, "ctx", "ch"),
        check_vma=False,
    )
```

```python
import functools
import math

import jax
import jax.numpy as jnp
from jax import lax
from jax.experimental import pallas as pl
from jax.experimental.pallas import tpu as pltpu
from jax.sharding import PartitionSpec as P

drop_level = 6554
keep_scale = 65536.0 / (65536.0 - 6554.0)


def mix_bits(hashed):
    hashed = hashed ^ lax.shift_right_logical(hashed, jnp.full_like(hashed, 16))
    hashed = hashed * jnp.int32(73244475)
    hashed = hashed ^ lax.shift_right_logical(hashed, jnp.full_like(hashed, 16))
    hashed = hashed * jnp.int32(73244475)
    hashed = hashed ^ lax.shift_right_logical(hashed, jnp.full_like(hashed, 16))
    return hashed


def keep_mask(drop_seed, drop_step, positions, channel_ids):
    seed_word = mix_bits(drop_seed[0] * jnp.int32(-1640531535) + drop_step[0])
    hashed = mix_bits(seed_word ^ mix_bits(positions))
    hashed = mix_bits(hashed ^ channel_ids * jnp.int32(668265263))
    low_bits = lax.shift_right_logical(hashed, jnp.full_like(hashed, 8)) & 65535
    return low_bits >= drop_level


def phase_table(count_rows, count_cols, period, direction):
    product = (
        jnp.arange(count_rows, dtype=jnp.int32)[:, None]
        * jnp.arange(count_cols, dtype=jnp.int32)[None, :]
        % period
    )
    angles = direction * 2.0 * math.pi * product.astype(jnp.float32) / period
    return (jnp.cos(angles), jnp.sin(angles))


def einsum_high(formula, left_part, right_part):
    return jnp.einsum(formula, left_part, right_part, precision=lax.Precision.HIGHEST)


def complex_einsum(formula, left_pair, right_pair):
    left_real, left_imag = left_pair
    right_real, right_imag = right_pair
    real_part = einsum_high(formula, left_real, right_real)
    imag_part = None
    if left_imag is not None and right_imag is not None:
        real_part = real_part - einsum_high(formula, left_imag, right_imag)
    if right_imag is not None:
        imag_part = einsum_high(formula, left_real, right_imag)
    cross_term = einsum_high(formula, left_imag, right_real)
    imag_part = cross_term if imag_part is None else imag_part + cross_term
    return (real_part, imag_part)


def complex_product(first_pair, second_pair):
    return (
        first_pair[0] * second_pair[0] - first_pair[1] * second_pair[1],
        first_pair[0] * second_pair[1] + first_pair[1] * second_pair[0],
    )


def grid_shape(length):
    columns = min(256, length)
    period = 2 * length
    return (columns, period // columns, period)


def forward_spectrum(signal_pair, length):
    columns, rows_all, period = grid_shape(length)
    half_rows = rows_all // 2
    shaped = tuple(
        (
            (
                None
                if part_item is None
                else part_item.reshape(part_item.shape[0], half_rows, columns, part_item.shape[2])
            )
            for part_item in signal_pair
        )
    )
    sectioned = complex_einsum(
        "kr,nrcd->ndkc", phase_table(rows_all, half_rows, rows_all, -1.0), shaped
    )
    sectioned = complex_product(sectioned, phase_table(rows_all, columns, period, -1.0))
    return complex_einsum("ndkc,cj->ndkj", sectioned, phase_table(columns, columns, columns, -1.0))


def inverse_signal(spectrum, length):
    columns, rows_all, period = grid_shape(length)
    half_rows = rows_all // 2
    sectioned = complex_einsum(
        "ndkj,jc->ndkc", spectrum, phase_table(columns, columns, columns, 1.0)
    )
    sectioned = complex_product(sectioned, phase_table(rows_all, columns, period, 1.0))
    last_table = phase_table(half_rows, rows_all, rows_all, 1.0)
    real_part = einsum_high("rk,ndkc->nrcd", last_table[0], sectioned[0]) - einsum_high(
        "rk,ndkc->nrcd", last_table[1], sectioned[1]
    )
    pieces_out = (real_part,)
    return tuple(
        (
            item_part.reshape(item_part.shape[0], length, item_part.shape[3]) / period
            for item_part in pieces_out
        )
    )


def convolve_plain(signal, filter_spec):
    length = signal.shape[1]
    spectrum = forward_spectrum((signal, None), length)
    product = complex_product(spectrum, filter_spec)
    return inverse_signal(product, length)[0]


def per_device_plain(
    query_proj,
    key_proj,
    value_proj,
    filter_taps,
    skip_gain,
    out_weight,
    drop_seed,
    drop_step,
    offsets,
):
    group_width = query_proj.shape[2]
    channel_ids = lax.axis_index("ch") * group_width + jnp.arange(group_width, dtype=jnp.int32)
    keep_flags = keep_mask(drop_seed, drop_step, offsets[:, :, None], channel_ids[None, None, :])
    gated = (
        key_proj.astype(jnp.float32)
        * value_proj.astype(jnp.float32)
        * jnp.where(keep_flags, keep_scale, 0.0)
    ).astype(jnp.bfloat16)
    tap_cols = lax.all_to_all(filter_taps, "ctx", split_axis=1, concat_axis=0, tiled=True)
    local_width = tap_cols.shape[1]
    skip_local = lax.dynamic_slice_in_dim(
        skip_gain, lax.axis_index("ctx") * local_width, local_width
    )
    filter_spec = forward_spectrum((tap_cols[None], None), tap_cols.shape[0])
    signal = lax.all_to_all(gated, "ctx", split_axis=2, concat_axis=1, tiled=True).astype(
        jnp.float32
    )
    convolved = convolve_plain(signal, filter_spec)
    mixed_cols = (convolved + skip_local * signal).astype(jnp.bfloat16)
    mixed = lax.all_to_all(mixed_cols, "ctx", split_axis=1, concat_axis=2, tiled=True)
    gate_out = (query_proj.astype(jnp.float32) * mixed.astype(jnp.float32)).astype(jnp.bfloat16)
    flat_rows = gate_out.reshape(-1, group_width)
    partial_value = jnp.dot(
        flat_rows,
        lax.all_gather(out_weight, "ctx", axis=1, tiled=True),
        preferred_element_type=jnp.float32,
    )
    summed = lax.psum_scatter(partial_value, "ch", scatter_dimension=1, tiled=True)
    return summed.astype(jnp.bfloat16).reshape(query_proj.shape)


SIDE = 64
WIDE = 2 * SIDE + 8
NARROW = SIDE + 8


def numbers(shape):
    return tuple(lax.broadcasted_iota(jnp.int32, shape, axis) for axis in range(len(shape)))


def waves(steps):
    angle = (steps % (SIDE * SIDE)).astype(jnp.float32) * (2.0 * math.pi / (SIDE * SIDE))
    return jnp.cos(angle), jnp.sin(angle)


def turn(row_part, col_part, sign):
    return (row_part - col_part) * (sign * SIDE * SIDE // 4)


def high_low(value, low):
    high = lax.reduce_precision(value, 8, 7)
    return jnp.where(low, value - high, high).astype(jnp.bfloat16)


def small_waves():
    half = SIDE // 2
    row, col = numbers((2 * SIDE, 4 * half))
    first = waves(SIDE * (col % half) * (row % SIDE) + turn(row // SIDE, col // half % 2, 1))
    n2, row = numbers((SIDE, 2 * SIDE))
    first_shift = waves(n2 * (row % SIDE))
    row, col = numbers((2 * SIDE, 4 * SIDE))
    steps = SIDE * (row % SIDE) * (col % SIDE)
    second = waves(steps + turn(row // SIDE, col // SIDE % 2, 1))[0]
    third = waves(steps + turn(row // SIDE, col // SIDE % 2, -1))[0]
    row, col = numbers((2 * half, 4 * SIDE))
    last = waves(SIDE * (row % half) * (col % SIDE) + turn(row // half, col // SIDE % 2, -1))
    n2, col = numbers((SIDE, 4 * SIDE))
    last_shift = waves(n2 * (col % SIDE))
    return first, first_shift, second, third, last, last_shift


def tables(small):
    first, first_shift, second, third, last, last_shift = small
    value = first[0][None] * first_shift[0][:, :, None] - first[1][None] * first_shift[1][:, :, None]
    first_table = high_low(value, numbers(value.shape)[2] >= SIDE)
    value = last[0][None] * last_shift[0][:, None, :] - last[1][None] * last_shift[1][:, None, :]
    last_table = high_low(value, numbers(value.shape)[2] >= 2 * SIDE)
    low = numbers(second.shape)[1] >= 2 * SIDE
    return first_table, high_low(second, low), high_low(third, low), last_table


def conv_kernel(
    got_ref, skip_ref, source_ref, second_ref, third_ref, last_ref, out_ref,
    sig_s, tap_s, mids_s, midt_s, back_s, res_s, first_ref, sem, *, blocks, tokens
):
    half = SIDE // 2
    copy = pltpu.make_async_copy(source_ref, first_ref, sem)
    copy.start()
    parts = tokens // SIDE
    for d in range(blocks):
        for a in range(parts):
            n1 = d * parts + a
            for s in range(3):
                ref, row = (tap_s, n1) if s == 2 else (sig_s, s * half + n1)
                begin = s * tokens + a * SIDE
                ref[row * NARROW : row * NARROW + SIDE, :] = got_ref[d, begin : begin + SIDE, :].astype(jnp.float32)
    zero = jnp.zeros((half, 128), jnp.float32)
    copy.wait()

    def stage_first(i, carry):
        for u in range(16):
            n2 = i * 16 + u
            sig = sig_s[pl.ds(n2, 2 * half, stride=NARROW), :]
            tap = jnp.concatenate([tap_s[pl.ds(n2, half, stride=NARROW), :], zero], axis=0)
            right = jnp.concatenate([sig, tap], axis=1).astype(jnp.bfloat16)
            right = jnp.concatenate([right, right], axis=0)
            spec = jnp.dot(first_ref[n2], right, preferred_element_type=jnp.float32)
            rows = pl.ds(pl.multiple_of(n2 * WIDE, 8), 2 * SIDE)
            mids_s[rows, :] = spec[:, :128]
            midt_s[rows, :] = spec[:, 128:]
        return carry

    lax.fori_loop(0, SIDE // 16, stage_first, 0)
    skip = skip_ref[...]
    scale = 1.0 / (SIDE * SIDE)

    def column(ref, k):
        real = ref[pl.ds(k, SIDE, stride=WIDE), :]
        return jnp.concatenate([real, ref[pl.ds(SIDE + k, SIDE, stride=WIDE), :]], axis=0)

    def stage_spectrum(i, carry):
        for v in range(4):
            products = []
            for u in range(2):
                k1 = i * 8 + v * 2 + u
                right = jnp.concatenate([column(mids_s, k1), column(midt_s, k1)], axis=1).astype(jnp.bfloat16)
                right = jnp.concatenate([right, right], axis=0)
                spec = jnp.dot(second_ref[...], right, preferred_element_type=jnp.float32)
                sig_r, sig_i = spec[:SIDE, :128], spec[SIDE:, :128]
                tap_r, tap_i = (spec[:SIDE, 128:] + skip) * scale, spec[SIDE:, 128:] * scale
                pair = [sig_r * tap_r - sig_i * tap_i, sig_r * tap_i + sig_i * tap_r]
                products.append(jnp.concatenate(pair, axis=0).astype(jnp.bfloat16))
            right = jnp.concatenate(products, axis=1)
            right = jnp.concatenate([right, right], axis=0)
            back = jnp.dot(third_ref[...], right, preferred_element_type=jnp.float32)
            for u in range(2):
                k1 = i * 8 + v * 2 + u
                back_s[pl.ds(pl.multiple_of(k1 * WIDE, 8), 2 * SIDE), :] = back[:, u * 128 : (u + 1) * 128]
        return carry

    lax.fori_loop(0, SIDE // 8, stage_spectrum, 0)

    def stage_last(i, carry):
        for u in range(16):
            n2 = i * 16 + u
            right = column(back_s, n2).astype(jnp.bfloat16)
            right = jnp.concatenate([right, right], axis=0)
            res_s[pl.ds(n2, 2 * half, stride=NARROW), :] = jnp.dot(
                last_ref[n2], right, preferred_element_type=jnp.float32
            )
        return carry

    lax.fori_loop(0, SIDE // 16, stage_last, 0)
    for d in range(blocks):
        for a in range(parts):
            for s in range(2):
                row = (s * half + d * parts + a) * NARROW
                begin = s * tokens + a * SIDE
                out_ref[d, begin : begin + SIDE, :] = res_s[row : row + SIDE, :].astype(jnp.bfloat16)


def conv(got, skip, tabs):
    blocks, rows, lanes = got.shape
    tokens = rows // 3
    full = pl.BlockSpec(memory_space=pltpu.VMEM)
    return pl.pallas_call(
        functools.partial(conv_kernel, blocks=blocks, tokens=tokens),
        out_shape=jax.ShapeDtypeStruct((blocks, 2 * tokens, lanes), jnp.bfloat16),
        in_specs=[full] * 2 + [pl.BlockSpec(memory_space=pl.ANY)] + [full] * 3,
        out_specs=full,
        scratch_shapes=[
            pltpu.VMEM((SIDE * NARROW, lanes), jnp.float32),
            pltpu.VMEM((SIDE // 2 * NARROW, lanes), jnp.float32),
            pltpu.VMEM((SIDE * WIDE, lanes), jnp.float32),
            pltpu.VMEM((SIDE * WIDE, lanes), jnp.float32),
            pltpu.VMEM((SIDE * WIDE, lanes), jnp.float32),
            pltpu.VMEM((SIDE * NARROW, lanes), jnp.float32),
            pltpu.VMEM(tabs[0].shape, jnp.bfloat16),
            pltpu.SemaphoreType.DMA,
        ],
        compiler_params=pltpu.CompilerParams(vmem_limit_bytes=32 << 20),
        cost_estimate=pl.CostEstimate(flops=1_000_000_000, bytes_accessed=1 << 20, transcendentals=0),
        name="long_conv",
    )(got, skip, *tabs)


VMEM = pl.BlockSpec(memory_space=pltpu.VMEM)
SMEM = pl.BlockSpec(memory_space=pltpu.SMEM)


def gate_kernel(word_ref, off_ref, key_ref, value_ref, taps_ref, out_ref, tok_s):
    tokens = off_ref.shape[1]
    block = pl.program_id(0)

    @pl.when(block == 0)
    def _():
        for s in range(2):
            row = mix_bits(off_ref[s : s + 1, :])
            row = mix_bits(row ^ word_ref[0])
            tok_s[s * tokens : (s + 1) * tokens, :] = jnp.broadcast_to(row, (128, tokens)).T

    count = out_ref.shape[0]
    for c in range(count):
        lanes = slice(c * 128, (c + 1) * 128)
        channel = word_ref[1] + (block * count + c) * 128 + lax.broadcasted_iota(jnp.int32, (1, 128), 1)
        channel = channel * jnp.int32(668265263)
        for s in range(2):
            rows = slice(s * tokens, (s + 1) * tokens)
            hashed = mix_bits(tok_s[rows, :] ^ channel)
            low_bits = lax.shift_right_logical(hashed, jnp.full_like(hashed, 8)) & 65535
            keep = jnp.where(low_bits >= drop_level, jnp.float32(keep_scale), jnp.float32(0.0))
            product = key_ref[s, :, lanes].astype(jnp.float32) * value_ref[s, :, lanes].astype(jnp.float32)
            out_ref[c, rows, :] = (product * keep).astype(jnp.bfloat16)
        out_ref[c, 2 * tokens : 3 * tokens, :] = taps_ref[:, lanes].astype(jnp.bfloat16)


def gate_and_pack(words, offsets, key_proj, value_proj, taps):
    _, tokens, width = key_proj.shape
    blocks = width // 128
    count = 4
    part = pl.BlockSpec((2, tokens, count * 128), lambda d: (0, 0, d))
    return pl.pallas_call(
        gate_kernel,
        grid=(blocks // count,),
        out_shape=jax.ShapeDtypeStruct((blocks, 3 * tokens, 128), jnp.bfloat16),
        in_specs=[
            SMEM,
            pl.BlockSpec((2, tokens), lambda d: (0, 0)),
            part,
            part,
            pl.BlockSpec((tokens, count * 128), lambda d: (0, d)),
        ],
        out_specs=pl.BlockSpec((count, 3 * tokens, 128), lambda d: (d, 0, 0)),
        scratch_shapes=[pltpu.VMEM((2 * tokens, 128), jnp.int32)],
        name="gate_and_pack",
    )(words, offsets, key_proj, value_proj, taps)


def gate_rows(query_ref, mixed_ref, rows_ref):
    tokens = query_ref.shape[1]
    for c in range(mixed_ref.shape[0]):
        lanes = slice(c * 128, (c + 1) * 128)
        for s in range(2):
            rows = slice(s * tokens, (s + 1) * tokens)
            mixed = mixed_ref[c, rows, :].astype(jnp.float32)
            rows_ref[rows, lanes] = (query_ref[s, :, lanes].astype(jnp.float32) * mixed).astype(jnp.bfloat16)


def fetch(sources, index, held, sem):
    for place, source in enumerate(sources):

        @pl.when(index == place)
        def _():
            pltpu.make_async_copy(source, held, sem).start()


def arrived(sources, held, sem):
    pltpu.make_async_copy(sources[0], held, sem).wait()


def place_of(sel_ref, pair, mine):
    kept = jnp.where(pair == 0, sel_ref[0], sel_ref[1])
    return 2 * pair + (kept if mine else 1 - kept)


def dots_into(rows_ref, sources, wanted, held, sems, store, before=lambda: None):
    for i, (side, place) in enumerate(wanted):
        fetch(sources[4 * side : 4 * side + 4], place, held.at[i], sems.at[i])
    before()
    for i in range(len(wanted)):
        arrived(sources, held.at[i], sems.at[i])
        store(i, jnp.dot(rows_ref[...], held[i], preferred_element_type=jnp.float32))


def half_products(sel_ref, rows_ref, sources, give_refs, keep_ref, held, sems, before=lambda: None):
    home, away = sel_ref[2], 1 - sel_ref[2]
    wanted = [(0, place_of(sel_ref, pair, mine)) for pair, mine in ((away, False), (home, False), (away, True))]

    def store(i, part):
        if i == 2:
            keep_ref[...] = part
        else:
            give = part.astype(jnp.bfloat16)
            if isinstance(give_refs[i], tuple):
                depth = give.shape[0] // 2
                for half, ref in enumerate(give_refs[i]):
                    ref[...] = give[half * depth : (half + 1) * depth]
            else:
                give_refs[i][...] = give

    dots_into(rows_ref, sources, wanted, held, sems, store, before)


def line_kernel(sel_ref, query_ref, mixed_ref, *refs):
    sources, (rows_ref, give_ref, keep_ref, held, sems) = refs[:4], refs[4:]
    before = functools.partial(gate_rows, query_ref, mixed_ref, rows_ref)
    half_products(sel_ref, rows_ref, sources, (give_ref.at[0], give_ref.at[1]), keep_ref, held, sems, before)


def across_kernel(sel_ref, rows_ref, *refs):
    sources, (top_ref, bottom_ref, home_ref, keep_ref, held, sems) = refs[:4], refs[4:]
    half_products(sel_ref, rows_ref, sources, ((top_ref, bottom_ref), home_ref), keep_ref, held, sems)


def home_kernel(sel_ref, rows_ref, given_ref, given_x_ref, *refs):
    sources, (out_ref, held, sems) = refs[:8], refs[8:]
    wanted = [(side, place_of(sel_ref, sel_ref[2], True)) for side in (0, 1)]

    def store(i, part):
        out_ref[i] = part + (given_ref[1] if i == 0 else given_x_ref[...]).astype(jnp.float32)

    dots_into(rows_ref, sources, wanted, held, sems, store)


def products(kernel, outs, sel, left, weights, dots, grant=56):
    rows, (depth, width) = outs[-1].shape[-2], weights[0].shape
    return pl.pallas_call(
        kernel,
        out_shape=outs,
        in_specs=[SMEM] + [VMEM] * len(left) + [pl.BlockSpec(memory_space=pl.ANY)] * len(weights),
        out_specs=(VMEM,) * len(outs),
        scratch_shapes=[
            pltpu.VMEM((dots, depth, width), jnp.bfloat16),
            pltpu.SemaphoreType.DMA((dots,)),
        ],
        compiler_params=pltpu.CompilerParams(vmem_limit_bytes=grant << 20),
        cost_estimate=pl.CostEstimate(
            flops=2 * dots * rows * depth * width, bytes_accessed=8 << 20, transcendentals=0
        ),
        name="products",
    )(sel, *left, *weights)


def finish_kernel(x_ref, home_ref, here_ref, there_ref, out_ref):
    width = here_ref.shape[1]
    for half, away_ref in enumerate((here_ref, there_ref)):
        total = (home_ref[half] + away_ref[...].astype(jnp.float32)).astype(jnp.bfloat16)

        @pl.when(x_ref[0] == half)
        def _():
            out_ref[:, :width] = total

        @pl.when(x_ref[0] != half)
        def _():
            out_ref[:, width:] = total


def finish(x, home, here, there):
    rows, width = here.shape
    return pl.pallas_call(
        finish_kernel,
        out_shape=jax.ShapeDtypeStruct((rows, 2 * width), jnp.bfloat16),
        in_specs=[SMEM, VMEM, VMEM, VMEM],
        out_specs=VMEM,
        compiler_params=pltpu.CompilerParams(vmem_limit_bytes=16 << 20),
        name="finish",
    )(x, home, here, there)


def per_device_mesh(
    query_proj,
    key_proj,
    value_proj,
    filter_taps,
    skip_gain,
    out_weight,
    drop_seed,
    drop_step,
    offsets,
):
    group_width = query_proj.shape[2]
    ctx, ch = lax.axis_index("ctx"), lax.axis_index("ch")
    z, x, y, core = ctx // 2, ctx % 2, ch // 2, ch % 2

    def along_z(value, pairs):
        return lax.ppermute(value, "ctx", [(2 * a + k, 2 * b + k) for a, b in pairs for k in (0, 1)])

    def across_x(value):
        return lax.ppermute(value, "ctx", [(i, i ^ 1) for i in range(8)])

    def to_sibling(value):
        return lax.ppermute(value, "ch", [(j, j ^ 1) for j in range(4)])

    def across_y(value):
        return lax.ppermute(value, "ch", [(j, j ^ 2) for j in range(4)])

    own = out_weight
    middle = along_z(own, [(1, 2), (2, 1)])
    near = along_z(own, [(0, 1), (1, 0), (2, 3), (3, 2)])
    own_x = across_x(own)
    seed_word = mix_bits(drop_seed[0] * jnp.int32(-1640531535) + drop_step[0])
    words = jnp.stack([seed_word, ch * group_width])
    packed = gate_and_pack(words, offsets, key_proj, value_proj, filter_taps)
    got = lax.all_to_all(packed, "ctx", split_axis=0, concat_axis=0, tiled=True)

    tabs = tables(lax.optimization_barrier(small_waves()))
    near, middle, tabs = lax.optimization_barrier((near, middle, tabs))
    far_mid = along_z(near, [(2, 1), (1, 2)])
    far_ends = along_z(middle, [(1, 0), (2, 3)])
    near, own_x = lax.optimization_barrier((near, own_x))
    near_x = across_x(near)
    inner = (z == 1) | (z == 2)
    third = jnp.where(inner, middle, far_ends)
    got, third, far_mid, tabs = lax.optimization_barrier((got, third, far_mid, tabs))
    three_ends = along_z(far_mid, [(1, 0), (2, 3)])
    third, near_x = lax.optimization_barrier((third, near_x))
    third_x = across_x(third)
    skip_local = lax.dynamic_slice_in_dim(skip_gain, ctx * 128, 128)
    mixed = conv(got, skip_local[None, :], tabs)
    back = lax.all_to_all(mixed, "ctx", split_axis=0, concat_axis=0, tiled=True)
    three_ends, third_x, mixed = lax.optimization_barrier((three_ends, third_x, mixed))
    fourth = jnp.where(inner, far_mid, three_ends)
    fourth_x = across_x(fourth)

    near_kept = (z + core) % 2
    sel = jnp.stack([near_kept, (near_kept + inner) % 2, (z // 2 + y) % 2]).astype(jnp.int32)
    line = (own, near, third, fourth)
    row_count, half_width = 2 * query_proj.shape[1], own.shape[1]

    def out(dtype, *lead, rows=row_count):
        return jax.ShapeDtypeStruct(lead + (rows, half_width), dtype)

    rows_type = jax.ShapeDtypeStruct((row_count, group_width), jnp.bfloat16)
    outs = (rows_type, out(jnp.bfloat16, 2), out(jnp.float32))
    rows, give, keep = products(line_kernel, outs, sel, (query_proj, back), line, 3)
    give, fourth_x = lax.optimization_barrier((give, fourth_x))
    line_x = (own_x, near_x, third_x, fourth_x)
    given = to_sibling(give)
    here = across_y((keep + given[0].astype(jnp.float32)).astype(jnp.bfloat16))
    quarter = out(jnp.bfloat16, rows=row_count // 2)
    outs = (quarter, quarter, out(jnp.bfloat16), out(jnp.float32))
    top, bottom, give_home, keep = products(across_kernel, outs, sel, (rows,), line_x, 3)
    top, bottom = to_sibling(top), to_sibling(bottom)
    top, bottom, keep, here = lax.optimization_barrier((top, bottom, keep, here))
    away = keep + jnp.concatenate([top, bottom], axis=0).astype(jnp.float32)
    there = across_y(away.astype(jnp.bfloat16))
    left = (rows, given, to_sibling(give_home))
    (home,) = products(home_kernel, (out(jnp.float32, 2),), sel, left, line + line_x, 2, 24)
    return finish(x.astype(jnp.int32)[None], home, here, there).reshape(query_proj.shape)


def solution(mesh):
    sizes = dict(mesh.shape)

    def per_device(query_proj, *rest):
        width = query_proj.shape[2]
        length = query_proj.shape[1] * sizes["ctx"]
        fits = sizes["ctx"] == 8 and sizes["ch"] == 4 and width == 1024 and length == 2048
        return (per_device_mesh if fits else per_device_plain)(query_proj, *rest)

    return jax.shard_map(
        per_device,
        mesh=mesh,
        in_specs=(
            P(None, "ctx", "ch"),
            P(None, "ctx", "ch"),
            P(None, "ctx", "ch"),
            P("ctx", "ch"),
            P("ch"),
            P("ch", "ctx"),
            P(),
            P(),
            P(None, "ctx"),
        ),
        out_specs=P(None, "ctx", "ch"),
        check_vma=False,
    )
```

```python
import functools
import math

import jax
import jax.numpy as jnp
from jax import lax
from jax.experimental import pallas as pl
from jax.experimental.pallas import tpu as pltpu
from jax.sharding import PartitionSpec as P

drop_level = 6554
keep_scale = 65536.0 / (65536.0 - 6554.0)


def mix_bits(hashed):
    hashed = hashed ^ lax.shift_right_logical(hashed, jnp.full_like(hashed, 16))
    hashed = hashed * jnp.int32(73244475)
    hashed = hashed ^ lax.shift_right_logical(hashed, jnp.full_like(hashed, 16))
    hashed = hashed * jnp.int32(73244475)
    hashed = hashed ^ lax.shift_right_logical(hashed, jnp.full_like(hashed, 16))
    return hashed


def keep_mask(drop_seed, drop_step, positions, channel_ids):
    seed_word = mix_bits(drop_seed[0] * jnp.int32(-1640531535) + drop_step[0])
    hashed = mix_bits(seed_word ^ mix_bits(positions))
    hashed = mix_bits(hashed ^ channel_ids * jnp.int32(668265263))
    low_bits = lax.shift_right_logical(hashed, jnp.full_like(hashed, 8)) & 65535
    return low_bits >= drop_level


def phase_table(count_rows, count_cols, period, direction):
    product = (
        jnp.arange(count_rows, dtype=jnp.int32)[:, None]
        * jnp.arange(count_cols, dtype=jnp.int32)[None, :]
        % period
    )
    angles = direction * 2.0 * math.pi * product.astype(jnp.float32) / period
    return (jnp.cos(angles), jnp.sin(angles))


def einsum_high(formula, left_part, right_part):
    return jnp.einsum(formula, left_part, right_part, precision=lax.Precision.HIGHEST)


def complex_einsum(formula, left_pair, right_pair):
    left_real, left_imag = left_pair
    right_real, right_imag = right_pair
    real_part = einsum_high(formula, left_real, right_real)
    imag_part = None
    if left_imag is not None and right_imag is not None:
        real_part = real_part - einsum_high(formula, left_imag, right_imag)
    if right_imag is not None:
        imag_part = einsum_high(formula, left_real, right_imag)
    cross_term = einsum_high(formula, left_imag, right_real)
    imag_part = cross_term if imag_part is None else imag_part + cross_term
    return (real_part, imag_part)


def complex_product(first_pair, second_pair):
    return (
        first_pair[0] * second_pair[0] - first_pair[1] * second_pair[1],
        first_pair[0] * second_pair[1] + first_pair[1] * second_pair[0],
    )


def grid_shape(length):
    columns = min(256, length)
    period = 2 * length
    return (columns, period // columns, period)


def forward_spectrum(signal_pair, length):
    columns, rows_all, period = grid_shape(length)
    half_rows = rows_all // 2
    shaped = tuple(
        (
            (
                None
                if part_item is None
                else part_item.reshape(part_item.shape[0], half_rows, columns, part_item.shape[2])
            )
            for part_item in signal_pair
        )
    )
    sectioned = complex_einsum(
        "kr,nrcd->ndkc", phase_table(rows_all, half_rows, rows_all, -1.0), shaped
    )
    sectioned = complex_product(sectioned, phase_table(rows_all, columns, period, -1.0))
    return complex_einsum("ndkc,cj->ndkj", sectioned, phase_table(columns, columns, columns, -1.0))


def inverse_signal(spectrum, length):
    columns, rows_all, period = grid_shape(length)
    half_rows = rows_all // 2
    sectioned = complex_einsum(
        "ndkj,jc->ndkc", spectrum, phase_table(columns, columns, columns, 1.0)
    )
    sectioned = complex_product(sectioned, phase_table(rows_all, columns, period, 1.0))
    last_table = phase_table(half_rows, rows_all, rows_all, 1.0)
    real_part = einsum_high("rk,ndkc->nrcd", last_table[0], sectioned[0]) - einsum_high(
        "rk,ndkc->nrcd", last_table[1], sectioned[1]
    )
    pieces_out = (real_part,)
    return tuple(
        (
            item_part.reshape(item_part.shape[0], length, item_part.shape[3]) / period
            for item_part in pieces_out
        )
    )


def convolve_plain(signal, filter_spec):
    length = signal.shape[1]
    spectrum = forward_spectrum((signal, None), length)
    product = complex_product(spectrum, filter_spec)
    return inverse_signal(product, length)[0]


def per_device_plain(
    query_proj,
    key_proj,
    value_proj,
    filter_taps,
    skip_gain,
    out_weight,
    drop_seed,
    drop_step,
    offsets,
):
    group_width = query_proj.shape[2]
    channel_ids = lax.axis_index("ch") * group_width + jnp.arange(group_width, dtype=jnp.int32)
    keep_flags = keep_mask(drop_seed, drop_step, offsets[:, :, None], channel_ids[None, None, :])
    gated = (
        key_proj.astype(jnp.float32)
        * value_proj.astype(jnp.float32)
        * jnp.where(keep_flags, keep_scale, 0.0)
    ).astype(jnp.bfloat16)
    tap_cols = lax.all_to_all(filter_taps, "ctx", split_axis=1, concat_axis=0, tiled=True)
    local_width = tap_cols.shape[1]
    skip_local = lax.dynamic_slice_in_dim(
        skip_gain, lax.axis_index("ctx") * local_width, local_width
    )
    filter_spec = forward_spectrum((tap_cols[None], None), tap_cols.shape[0])
    signal = lax.all_to_all(gated, "ctx", split_axis=2, concat_axis=1, tiled=True).astype(
        jnp.float32
    )
    convolved = convolve_plain(signal, filter_spec)
    mixed_cols = (convolved + skip_local * signal).astype(jnp.bfloat16)
    mixed = lax.all_to_all(mixed_cols, "ctx", split_axis=1, concat_axis=2, tiled=True)
    gate_out = (query_proj.astype(jnp.float32) * mixed.astype(jnp.float32)).astype(jnp.bfloat16)
    flat_rows = gate_out.reshape(-1, group_width)
    partial_value = jnp.dot(
        flat_rows,
        lax.all_gather(out_weight, "ctx", axis=1, tiled=True),
        preferred_element_type=jnp.float32,
    )
    summed = lax.psum_scatter(partial_value, "ch", scatter_dimension=1, tiled=True)
    return summed.astype(jnp.bfloat16).reshape(query_proj.shape)


SIDE = 64
WIDE = 2 * SIDE + 8
NARROW = SIDE + 8


def numbers(shape):
    return tuple(lax.broadcasted_iota(jnp.int32, shape, axis) for axis in range(len(shape)))


def waves(steps):
    angle = (steps % (SIDE * SIDE)).astype(jnp.float32) * (2.0 * math.pi / (SIDE * SIDE))
    return jnp.cos(angle), jnp.sin(angle)


def turn(row_part, col_part, sign):
    return (row_part - col_part) * (sign * SIDE * SIDE // 4)


def high_low(value, low):
    high = lax.reduce_precision(value, 8, 7)
    return jnp.where(low, value - high, high).astype(jnp.bfloat16)


def small_waves():
    half = SIDE // 2
    row, col = numbers((2 * SIDE, 4 * half))
    first = waves(SIDE * (col % half) * (row % SIDE) + turn(row // SIDE, col // half % 2, 1))
    n2, row = numbers((SIDE, 2 * SIDE))
    first_shift = waves(n2 * (row % SIDE))
    row, col = numbers((2 * SIDE, 4 * SIDE))
    steps = SIDE * (row % SIDE) * (col % SIDE)
    second = waves(steps + turn(row // SIDE, col // SIDE % 2, 1))[0]
    third = waves(steps + turn(row // SIDE, col // SIDE % 2, -1))[0]
    row, col = numbers((2 * half, 4 * SIDE))
    last = waves(SIDE * (row % half) * (col % SIDE) + turn(row // half, col // SIDE % 2, -1))
    n2, col = numbers((SIDE, 4 * SIDE))
    last_shift = waves(n2 * (col % SIDE))
    return first, first_shift, second, third, last, last_shift


def tables(small):
    first, first_shift, second, third, last, last_shift = small
    value = first[0][None] * first_shift[0][:, :, None] - first[1][None] * first_shift[1][:, :, None]
    first_table = high_low(value, numbers(value.shape)[2] >= SIDE)
    value = last[0][None] * last_shift[0][:, None, :] - last[1][None] * last_shift[1][:, None, :]
    last_table = high_low(value, numbers(value.shape)[2] >= 2 * SIDE)
    low = numbers(second.shape)[1] >= 2 * SIDE
    return first_table, high_low(second, low), high_low(third, low), last_table


def conv_kernel(
    got_ref, skip_ref, source_ref, second_ref, third_ref, last_ref, out_ref,
    sig_s, tap_s, mids_s, midt_s, back_s, res_s, first_ref, sem, *, blocks, tokens
):
    half = SIDE // 2
    copy = pltpu.make_async_copy(source_ref, first_ref, sem)
    copy.start()
    parts = tokens // SIDE
    for d in range(blocks):
        for a in range(parts):
            n1 = d * parts + a
            for s in range(3):
                ref, row = (tap_s, n1) if s == 2 else (sig_s, s * half + n1)
                begin = s * tokens + a * SIDE
                ref[row * NARROW : row * NARROW + SIDE, :] = got_ref[d, begin : begin + SIDE, :].astype(jnp.float32)
    zero = jnp.zeros((half, 128), jnp.float32)
    copy.wait()

    def stage_first(i, carry):
        for u in range(16):
            n2 = i * 16 + u
            sig = sig_s[pl.ds(n2, 2 * half, stride=NARROW), :]
            tap = jnp.concatenate([tap_s[pl.ds(n2, half, stride=NARROW), :], zero], axis=0)
            right = jnp.concatenate([sig, tap], axis=1).astype(jnp.bfloat16)
            right = jnp.concatenate([right, right], axis=0)
            spec = jnp.dot(first_ref[n2], right, preferred_element_type=jnp.float32)
            rows = pl.ds(pl.multiple_of(n2 * WIDE, 8), 2 * SIDE)
            mids_s[rows, :] = spec[:, :128]
            midt_s[rows, :] = spec[:, 128:]
        return carry

    lax.fori_loop(0, SIDE // 16, stage_first, 0)
    skip = skip_ref[...]
    scale = 1.0 / (SIDE * SIDE)

    def column(ref, k):
        real = ref[pl.ds(k, SIDE, stride=WIDE), :]
        return jnp.concatenate([real, ref[pl.ds(SIDE + k, SIDE, stride=WIDE), :]], axis=0)

    def stage_spectrum(i, carry):
        for v in range(4):
            products = []
            for u in range(2):
                k1 = i * 8 + v * 2 + u
                right = jnp.concatenate([column(mids_s, k1), column(midt_s, k1)], axis=1).astype(jnp.bfloat16)
                right = jnp.concatenate([right, right], axis=0)
                spec = jnp.dot(second_ref[...], right, preferred_element_type=jnp.float32)
                sig_r, sig_i = spec[:SIDE, :128], spec[SIDE:, :128]
                tap_r, tap_i = (spec[:SIDE, 128:] + skip) * scale, spec[SIDE:, 128:] * scale
                pair = [sig_r * tap_r - sig_i * tap_i, sig_r * tap_i + sig_i * tap_r]
                products.append(jnp.concatenate(pair, axis=0).astype(jnp.bfloat16))
            right = jnp.concatenate(products, axis=1)
            right = jnp.concatenate([right, right], axis=0)
            back = jnp.dot(third_ref[...], right, preferred_element_type=jnp.float32)
            for u in range(2):
                k1 = i * 8 + v * 2 + u
                back_s[pl.ds(pl.multiple_of(k1 * WIDE, 8), 2 * SIDE), :] = back[:, u * 128 : (u + 1) * 128]
        return carry

    lax.fori_loop(0, SIDE // 8, stage_spectrum, 0)

    def stage_last(i, carry):
        for u in range(16):
            n2 = i * 16 + u
            right = column(back_s, n2).astype(jnp.bfloat16)
            right = jnp.concatenate([right, right], axis=0)
            res_s[pl.ds(n2, 2 * half, stride=NARROW), :] = jnp.dot(
                last_ref[n2], right, preferred_element_type=jnp.float32
            )
        return carry

    lax.fori_loop(0, SIDE // 16, stage_last, 0)
    for d in range(blocks):
        for a in range(parts):
            for s in range(2):
                row = (s * half + d * parts + a) * NARROW
                begin = s * tokens + a * SIDE
                out_ref[d, begin : begin + SIDE, :] = res_s[row : row + SIDE, :].astype(jnp.bfloat16)


def conv(got, skip, tabs):
    blocks, rows, lanes = got.shape
    tokens = rows // 3
    full = pl.BlockSpec(memory_space=pltpu.VMEM)
    return pl.pallas_call(
        functools.partial(conv_kernel, blocks=blocks, tokens=tokens),
        out_shape=jax.ShapeDtypeStruct((blocks, 2 * tokens, lanes), jnp.bfloat16),
        in_specs=[full] * 2 + [pl.BlockSpec(memory_space=pl.ANY)] + [full] * 3,
        out_specs=full,
        scratch_shapes=[
            pltpu.VMEM((SIDE * NARROW, lanes), jnp.float32),
            pltpu.VMEM((SIDE // 2 * NARROW, lanes), jnp.float32),
            pltpu.VMEM((SIDE * WIDE, lanes), jnp.float32),
            pltpu.VMEM((SIDE * WIDE, lanes), jnp.float32),
            pltpu.VMEM((SIDE * WIDE, lanes), jnp.float32),
            pltpu.VMEM((SIDE * NARROW, lanes), jnp.float32),
            pltpu.VMEM(tabs[0].shape, jnp.bfloat16),
            pltpu.SemaphoreType.DMA,
        ],
        compiler_params=pltpu.CompilerParams(vmem_limit_bytes=32 << 20),
        cost_estimate=pl.CostEstimate(flops=1_000_000_000, bytes_accessed=1 << 20, transcendentals=0),
        name="long_conv",
    )(got, skip, *tabs)


VMEM = pl.BlockSpec(memory_space=pltpu.VMEM)
SMEM = pl.BlockSpec(memory_space=pltpu.SMEM)


def gate_kernel(word_ref, off_ref, key_ref, value_ref, taps_ref, out_ref, tok_s):
    tokens = off_ref.shape[1]
    block = pl.program_id(0)

    @pl.when(block == 0)
    def _():
        for s in range(2):
            row = mix_bits(off_ref[s : s + 1, :])
            row = mix_bits(row ^ word_ref[0])
            tok_s[s * tokens : (s + 1) * tokens, :] = jnp.broadcast_to(row, (128, tokens)).T

    count = out_ref.shape[0]
    for c in range(count):
        lanes = slice(c * 128, (c + 1) * 128)
        channel = word_ref[1] + (block * count + c) * 128 + lax.broadcasted_iota(jnp.int32, (1, 128), 1)
        channel = channel * jnp.int32(668265263)
        for s in range(2):
            rows = slice(s * tokens, (s + 1) * tokens)
            hashed = mix_bits(tok_s[rows, :] ^ channel)
            low_bits = lax.shift_right_logical(hashed, jnp.full_like(hashed, 8)) & 65535
            keep = jnp.where(low_bits >= drop_level, jnp.float32(keep_scale), jnp.float32(0.0))
            product = key_ref[s, :, lanes].astype(jnp.float32) * value_ref[s, :, lanes].astype(jnp.float32)
            out_ref[c, rows, :] = (product * keep).astype(jnp.bfloat16)
        out_ref[c, 2 * tokens : 3 * tokens, :] = taps_ref[:, lanes].astype(jnp.bfloat16)


def gate_and_pack(words, offsets, key_proj, value_proj, taps):
    _, tokens, width = key_proj.shape
    blocks = width // 128
    count = 4
    part = pl.BlockSpec((2, tokens, count * 128), lambda d: (0, 0, d))
    return pl.pallas_call(
        gate_kernel,
        grid=(blocks // count,),
        out_shape=jax.ShapeDtypeStruct((blocks, 3 * tokens, 128), jnp.bfloat16),
        in_specs=[
            SMEM,
            pl.BlockSpec((2, tokens), lambda d: (0, 0)),
            part,
            part,
            pl.BlockSpec((tokens, count * 128), lambda d: (0, d)),
        ],
        out_specs=pl.BlockSpec((count, 3 * tokens, 128), lambda d: (d, 0, 0)),
        scratch_shapes=[pltpu.VMEM((2 * tokens, 128), jnp.int32)],
        name="gate_and_pack",
    )(words, offsets, key_proj, value_proj, taps)


def gate_rows(query_ref, mixed_ref, rows_ref):
    tokens = query_ref.shape[1]
    for c in range(mixed_ref.shape[0]):
        lanes = slice(c * 128, (c + 1) * 128)
        for s in range(2):
            rows = slice(s * tokens, (s + 1) * tokens)
            mixed = mixed_ref[c, rows, :].astype(jnp.float32)
            rows_ref[rows, lanes] = (query_ref[s, :, lanes].astype(jnp.float32) * mixed).astype(jnp.bfloat16)


def fetch(sources, index, held, sem):
    for place, source in enumerate(sources):

        @pl.when(index == place)
        def _():
            pltpu.make_async_copy(source, held, sem).start()


def arrived(sources, held, sem):
    pltpu.make_async_copy(sources[0], held, sem).wait()


def place_of(sel_ref, pair, mine):
    kept = jnp.where(pair == 0, sel_ref[0], sel_ref[1])
    return 2 * pair + (kept if mine else 1 - kept)


def dots_into(rows_ref, sources, wanted, held, sems, store, before=lambda: None):
    for i, (side, place) in enumerate(wanted):
        fetch(sources[4 * side : 4 * side + 4], place, held.at[i], sems.at[i])
    before()
    for i in range(len(wanted)):
        arrived(sources, held.at[i], sems.at[i])
        store(i, jnp.dot(rows_ref[...], held[i], preferred_element_type=jnp.float32))


def half_products(sel_ref, rows_ref, sources, give_refs, keep_ref, held, sems, before=lambda: None):
    home, away = sel_ref[2], 1 - sel_ref[2]
    wanted = [(0, place_of(sel_ref, pair, mine)) for pair, mine in ((away, False), (home, False), (away, True))]

    def store(i, part):
        if i == 2:
            keep_ref[...] = part
        else:
            give = part.astype(jnp.bfloat16)
            if isinstance(give_refs[i], tuple):
                depth = give.shape[0] // 2
                for half, ref in enumerate(give_refs[i]):
                    ref[...] = give[half * depth : (half + 1) * depth]
            else:
                give_refs[i][...] = give

    dots_into(rows_ref, sources, wanted, held, sems, store, before)


def line_kernel(sel_ref, query_ref, mixed_ref, *refs):
    sources, (rows_ref, give_ref, home_ref, keep_ref, held, sems) = refs[:4], refs[4:]
    before = functools.partial(gate_rows, query_ref, mixed_ref, rows_ref)
    half_products(sel_ref, rows_ref, sources, (give_ref, home_ref), keep_ref, held, sems, before)


def across_kernel(sel_ref, rows_ref, *refs):
    sources, (top_ref, bottom_ref, home_ref, keep_ref, held, sems) = refs[:4], refs[4:]
    half_products(sel_ref, rows_ref, sources, ((top_ref, bottom_ref), home_ref), keep_ref, held, sems)


def home_kernel(sel_ref, rows_ref, given_ref, given_x_ref, *refs):
    sources, (out_ref, held, sems) = refs[:8], refs[8:]
    wanted = [(side, place_of(sel_ref, sel_ref[2], True)) for side in (0, 1)]

    def store(i, part):
        out_ref[i] = part + (given_ref, given_x_ref)[i][...].astype(jnp.float32)

    dots_into(rows_ref, sources, wanted, held, sems, store)


def products(kernel, outs, sel, left, weights, dots, grant=56):
    rows, (depth, width) = outs[-1].shape[-2], weights[0].shape
    return pl.pallas_call(
        kernel,
        out_shape=outs,
        in_specs=[SMEM] + [VMEM] * len(left) + [pl.BlockSpec(memory_space=pl.ANY)] * len(weights),
        out_specs=(VMEM,) * len(outs),
        scratch_shapes=[
            pltpu.VMEM((dots, depth, width), jnp.bfloat16),
            pltpu.SemaphoreType.DMA((dots,)),
        ],
        compiler_params=pltpu.CompilerParams(vmem_limit_bytes=grant << 20),
        cost_estimate=pl.CostEstimate(
            flops=2 * dots * rows * depth * width, bytes_accessed=8 << 20, transcendentals=0
        ),
        name="products",
    )(sel, *left, *weights)


def finish_kernel(x_ref, home_ref, here_ref, there_ref, out_ref):
    width = here_ref.shape[1]
    for half, away_ref in enumerate((here_ref, there_ref)):
        total = (home_ref[half] + away_ref[...].astype(jnp.float32)).astype(jnp.bfloat16)

        @pl.when(x_ref[0] == half)
        def _():
            out_ref[:, :width] = total

        @pl.when(x_ref[0] != half)
        def _():
            out_ref[:, width:] = total


def finish(x, home, here, there):
    rows, width = here.shape
    return pl.pallas_call(
        finish_kernel,
        out_shape=jax.ShapeDtypeStruct((rows, 2 * width), jnp.bfloat16),
        in_specs=[SMEM, VMEM, VMEM, VMEM],
        out_specs=VMEM,
        compiler_params=pltpu.CompilerParams(vmem_limit_bytes=16 << 20),
        name="finish",
    )(x, home, here, there)


def per_device_mesh(
    query_proj,
    key_proj,
    value_proj,
    filter_taps,
    skip_gain,
    out_weight,
    drop_seed,
    drop_step,
    offsets,
):
    group_width = query_proj.shape[2]
    ctx, ch = lax.axis_index("ctx"), lax.axis_index("ch")
    z, x, y, core = ctx // 2, ctx % 2, ch // 2, ch % 2

    def along_z(value, pairs):
        return lax.ppermute(value, "ctx", [(2 * a + k, 2 * b + k) for a, b in pairs for k in (0, 1)])

    def across_x(value):
        return lax.ppermute(value, "ctx", [(i, i ^ 1) for i in range(8)])

    def to_sibling(value):
        return lax.ppermute(value, "ch", [(j, j ^ 1) for j in range(4)])

    def across_y(value):
        return lax.ppermute(value, "ch", [(j, j ^ 2) for j in range(4)])

    own = out_weight
    middle = along_z(own, [(1, 2), (2, 1)])
    near = along_z(own, [(0, 1), (1, 0), (2, 3), (3, 2)])
    own_x = across_x(own)
    seed_word = mix_bits(drop_seed[0] * jnp.int32(-1640531535) + drop_step[0])
    words = jnp.stack([seed_word, ch * group_width])
    packed = gate_and_pack(words, offsets, key_proj, value_proj, filter_taps)
    got = lax.all_to_all(packed, "ctx", split_axis=0, concat_axis=0, tiled=True)

    tabs = tables(lax.optimization_barrier(small_waves()))
    near, middle, tabs = lax.optimization_barrier((near, middle, tabs))
    far_ends = along_z(middle, [(1, 0), (2, 3)])
    near, own_x = lax.optimization_barrier((near, own_x))
    near_x = across_x(near)
    inner = (z == 1) | (z == 2)
    third = jnp.where(inner, middle, far_ends)
    got, third, near, tabs = lax.optimization_barrier((got, third, near, tabs))
    far_mid = along_z(near, [(2, 1), (1, 2)])
    third_x = across_x(third)
    skip_local = lax.dynamic_slice_in_dim(skip_gain, ctx * 128, 128)
    mixed = conv(got, skip_local[None, :], tabs)
    back = lax.all_to_all(mixed, "ctx", split_axis=0, concat_axis=0, tiled=True)
    far_mid, third_x, near_x, mixed = lax.optimization_barrier((far_mid, third_x, near_x, mixed))
    three_ends = along_z(far_mid, [(1, 0), (2, 3)])
    fourth = jnp.where(inner, far_mid, three_ends)
    fourth_x = across_x(fourth)

    near_kept = (z + core) % 2
    sel = jnp.stack([near_kept, (near_kept + inner) % 2, (z // 2 + y) % 2]).astype(jnp.int32)
    line = (own, near, third, fourth)
    row_count, half_width = 2 * query_proj.shape[1], own.shape[1]

    def out(dtype, *lead, rows=row_count):
        return jax.ShapeDtypeStruct(lead + (rows, half_width), dtype)

    rows_type = jax.ShapeDtypeStruct((row_count, group_width), jnp.bfloat16)
    outs = (rows_type, out(jnp.bfloat16), out(jnp.bfloat16), out(jnp.float32))
    rows, give, give_line, keep = products(line_kernel, outs, sel, (query_proj, back), line, 3)
    given, keep, fourth_x = lax.optimization_barrier((to_sibling(give), keep, fourth_x))
    line_x = (own_x, near_x, third_x, fourth_x)
    here = across_y((keep + given.astype(jnp.float32)).astype(jnp.bfloat16))
    quarter = out(jnp.bfloat16, rows=row_count // 2)
    outs = (quarter, quarter, out(jnp.bfloat16), out(jnp.float32))
    top, bottom, give_home, keep = products(across_kernel, outs, sel, (rows,), line_x, 3)
    top, bottom = to_sibling(top), to_sibling(bottom)
    top, bottom, keep, here = lax.optimization_barrier((top, bottom, keep, here))
    away = keep + jnp.concatenate([top, bottom], axis=0).astype(jnp.float32)
    there = across_y(away.astype(jnp.bfloat16))
    left = (rows, to_sibling(give_line), to_sibling(give_home))
    (home,) = products(home_kernel, (out(jnp.float32, 2),), sel, left, line + line_x, 2, 24)
    return finish(x.astype(jnp.int32)[None], home, here, there).reshape(query_proj.shape)


def solution(mesh):
    sizes = dict(mesh.shape)

    def per_device(query_proj, *rest):
        width = query_proj.shape[2]
        length = query_proj.shape[1] * sizes["ctx"]
        fits = sizes["ctx"] == 8 and sizes["ch"] == 4 and width == 1024 and length == 2048
        return (per_device_mesh if fits else per_device_plain)(query_proj, *rest)

    return jax.shard_map(
        per_device,
        mesh=mesh,
        in_specs=(
            P(None, "ctx", "ch"),
            P(None, "ctx", "ch"),
            P(None, "ctx", "ch"),
            P("ctx", "ch"),
            P("ch"),
            P("ch", "ctx"),
            P(),
            P(),
            P(None, "ctx"),
        ),
        out_specs=P(None, "ctx", "ch"),
        check_vma=False,
    )
```

```python
import functools
import math

import jax
import jax.numpy as jnp
from jax import lax
from jax.experimental import pallas as pl
from jax.experimental.pallas import tpu as pltpu
from jax.sharding import PartitionSpec as P

drop_level = 6554
keep_scale = 65536.0 / (65536.0 - 6554.0)


def mix_bits(hashed):
    hashed = hashed ^ lax.shift_right_logical(hashed, jnp.full_like(hashed, 16))
    hashed = hashed * jnp.int32(73244475)
    hashed = hashed ^ lax.shift_right_logical(hashed, jnp.full_like(hashed, 16))
    hashed = hashed * jnp.int32(73244475)
    hashed = hashed ^ lax.shift_right_logical(hashed, jnp.full_like(hashed, 16))
    return hashed


def keep_mask(drop_seed, drop_step, positions, channel_ids):
    seed_word = mix_bits(drop_seed[0] * jnp.int32(-1640531535) + drop_step[0])
    hashed = mix_bits(seed_word ^ mix_bits(positions))
    hashed = mix_bits(hashed ^ channel_ids * jnp.int32(668265263))
    low_bits = lax.shift_right_logical(hashed, jnp.full_like(hashed, 8)) & 65535
    return low_bits >= drop_level


def phase_table(count_rows, count_cols, period, direction):
    product = (
        jnp.arange(count_rows, dtype=jnp.int32)[:, None]
        * jnp.arange(count_cols, dtype=jnp.int32)[None, :]
        % period
    )
    angles = direction * 2.0 * math.pi * product.astype(jnp.float32) / period
    return (jnp.cos(angles), jnp.sin(angles))


def einsum_high(formula, left_part, right_part):
    return jnp.einsum(formula, left_part, right_part, precision=lax.Precision.HIGHEST)


def complex_einsum(formula, left_pair, right_pair):
    left_real, left_imag = left_pair
    right_real, right_imag = right_pair
    real_part = einsum_high(formula, left_real, right_real)
    imag_part = None
    if left_imag is not None and right_imag is not None:
        real_part = real_part - einsum_high(formula, left_imag, right_imag)
    if right_imag is not None:
        imag_part = einsum_high(formula, left_real, right_imag)
    cross_term = einsum_high(formula, left_imag, right_real)
    imag_part = cross_term if imag_part is None else imag_part + cross_term
    return (real_part, imag_part)


def complex_product(first_pair, second_pair):
    return (
        first_pair[0] * second_pair[0] - first_pair[1] * second_pair[1],
        first_pair[0] * second_pair[1] + first_pair[1] * second_pair[0],
    )


def grid_shape(length):
    columns = min(256, length)
    period = 2 * length
    return (columns, period // columns, period)


def forward_spectrum(signal_pair, length):
    columns, rows_all, period = grid_shape(length)
    half_rows = rows_all // 2
    shaped = tuple(
        (
            (
                None
                if part_item is None
                else part_item.reshape(part_item.shape[0], half_rows, columns, part_item.shape[2])
            )
            for part_item in signal_pair
        )
    )
    sectioned = complex_einsum(
        "kr,nrcd->ndkc", phase_table(rows_all, half_rows, rows_all, -1.0), shaped
    )
    sectioned = complex_product(sectioned, phase_table(rows_all, columns, period, -1.0))
    return complex_einsum("ndkc,cj->ndkj", sectioned, phase_table(columns, columns, columns, -1.0))


def inverse_signal(spectrum, length):
    columns, rows_all, period = grid_shape(length)
    half_rows = rows_all // 2
    sectioned = complex_einsum(
        "ndkj,jc->ndkc", spectrum, phase_table(columns, columns, columns, 1.0)
    )
    sectioned = complex_product(sectioned, phase_table(rows_all, columns, period, 1.0))
    last_table = phase_table(half_rows, rows_all, rows_all, 1.0)
    real_part = einsum_high("rk,ndkc->nrcd", last_table[0], sectioned[0]) - einsum_high(
        "rk,ndkc->nrcd", last_table[1], sectioned[1]
    )
    pieces_out = (real_part,)
    return tuple(
        (
            item_part.reshape(item_part.shape[0], length, item_part.shape[3]) / period
            for item_part in pieces_out
        )
    )


def convolve_plain(signal, filter_spec):
    length = signal.shape[1]
    spectrum = forward_spectrum((signal, None), length)
    product = complex_product(spectrum, filter_spec)
    return inverse_signal(product, length)[0]


def per_device_plain(
    query_proj,
    key_proj,
    value_proj,
    filter_taps,
    skip_gain,
    out_weight,
    drop_seed,
    drop_step,
    offsets,
):
    group_width = query_proj.shape[2]
    channel_ids = lax.axis_index("ch") * group_width + jnp.arange(group_width, dtype=jnp.int32)
    keep_flags = keep_mask(drop_seed, drop_step, offsets[:, :, None], channel_ids[None, None, :])
    gated = (
        key_proj.astype(jnp.float32)
        * value_proj.astype(jnp.float32)
        * jnp.where(keep_flags, keep_scale, 0.0)
    ).astype(jnp.bfloat16)
    tap_cols = lax.all_to_all(filter_taps, "ctx", split_axis=1, concat_axis=0, tiled=True)
    local_width = tap_cols.shape[1]
    skip_local = lax.dynamic_slice_in_dim(
        skip_gain, lax.axis_index("ctx") * local_width, local_width
    )
    filter_spec = forward_spectrum((tap_cols[None], None), tap_cols.shape[0])
    signal = lax.all_to_all(gated, "ctx", split_axis=2, concat_axis=1, tiled=True).astype(
        jnp.float32
    )
    convolved = convolve_plain(signal, filter_spec)
    mixed_cols = (convolved + skip_local * signal).astype(jnp.bfloat16)
    mixed = lax.all_to_all(mixed_cols, "ctx", split_axis=1, concat_axis=2, tiled=True)
    gate_out = (query_proj.astype(jnp.float32) * mixed.astype(jnp.float32)).astype(jnp.bfloat16)
    flat_rows = gate_out.reshape(-1, group_width)
    partial_value = jnp.dot(
        flat_rows,
        lax.all_gather(out_weight, "ctx", axis=1, tiled=True),
        preferred_element_type=jnp.float32,
    )
    summed = lax.psum_scatter(partial_value, "ch", scatter_dimension=1, tiled=True)
    return summed.astype(jnp.bfloat16).reshape(query_proj.shape)


SIDE = 64
WIDE = 2 * SIDE + 8
NARROW = SIDE + 8


def numbers(shape):
    return tuple(lax.broadcasted_iota(jnp.int32, shape, axis) for axis in range(len(shape)))


def waves(steps):
    angle = (steps % (SIDE * SIDE)).astype(jnp.float32) * (2.0 * math.pi / (SIDE * SIDE))
    return jnp.cos(angle), jnp.sin(angle)


def turn(row_part, col_part, sign):
    return (row_part - col_part) * (sign * SIDE * SIDE // 4)


def high_low(value, low):
    high = lax.reduce_precision(value, 8, 7)
    return jnp.where(low, value - high, high).astype(jnp.bfloat16)


def small_waves():
    half = SIDE // 2
    row, col = numbers((2 * SIDE, 4 * half))
    first = waves(SIDE * (col % half) * (row % SIDE) + turn(row // SIDE, col // half % 2, 1))
    n2, row = numbers((SIDE, 2 * SIDE))
    first_shift = waves(n2 * (row % SIDE))
    row, col = numbers((2 * SIDE, 4 * SIDE))
    steps = SIDE * (row % SIDE) * (col % SIDE)
    second = waves(steps + turn(row // SIDE, col // SIDE % 2, 1))[0]
    third = waves(steps + turn(row // SIDE, col // SIDE % 2, -1))[0]
    row, col = numbers((2 * half, 4 * SIDE))
    last = waves(SIDE * (row % half) * (col % SIDE) + turn(row // half, col // SIDE % 2, -1))
    n2, col = numbers((SIDE, 4 * SIDE))
    last_shift = waves(n2 * (col % SIDE))
    return first, first_shift, second, third, last, last_shift


def tables(small):
    first, first_shift, second, third, last, last_shift = small
    value = first[0][None] * first_shift[0][:, :, None] - first[1][None] * first_shift[1][:, :, None]
    first_table = high_low(value, numbers(value.shape)[2] >= SIDE)
    value = last[0][None] * last_shift[0][:, None, :] - last[1][None] * last_shift[1][:, None, :]
    last_table = high_low(value, numbers(value.shape)[2] >= 2 * SIDE)
    low = numbers(second.shape)[1] >= 2 * SIDE
    return first_table, high_low(second, low), high_low(third, low), last_table


def conv_kernel(
    got_ref, skip_ref, source_ref, second_ref, third_ref, last_ref, out_ref,
    sig_s, tap_s, mids_s, midt_s, back_s, res_s, first_ref, sem, *, blocks, tokens
):
    half = SIDE // 2
    copy = pltpu.make_async_copy(source_ref, first_ref, sem)
    copy.start()
    parts = tokens // SIDE
    for d in range(blocks):
        for a in range(parts):
            n1 = d * parts + a
            for s in range(3):
                ref, row = (tap_s, n1) if s == 2 else (sig_s, s * half + n1)
                begin = s * tokens + a * SIDE
                ref[row * NARROW : row * NARROW + SIDE, :] = got_ref[d, begin : begin + SIDE, :].astype(jnp.float32)
    zero = jnp.zeros((half, 128), jnp.float32)
    copy.wait()

    def stage_first(i, carry):
        for u in range(16):
            n2 = i * 16 + u
            sig = sig_s[pl.ds(n2, 2 * half, stride=NARROW), :]
            tap = jnp.concatenate([tap_s[pl.ds(n2, half, stride=NARROW), :], zero], axis=0)
            right = jnp.concatenate([sig, tap], axis=1).astype(jnp.bfloat16)
            right = jnp.concatenate([right, right], axis=0)
            spec = jnp.dot(first_ref[n2], right, preferred_element_type=jnp.float32)
            rows = pl.ds(pl.multiple_of(n2 * WIDE, 8), 2 * SIDE)
            mids_s[rows, :] = spec[:, :128]
            midt_s[rows, :] = spec[:, 128:]
        return carry

    lax.fori_loop(0, SIDE // 16, stage_first, 0)
    skip = skip_ref[...]
    scale = 1.0 / (SIDE * SIDE)

    def column(ref, k):
        real = ref[pl.ds(k, SIDE, stride=WIDE), :]
        return jnp.concatenate([real, ref[pl.ds(SIDE + k, SIDE, stride=WIDE), :]], axis=0)

    def stage_spectrum(i, carry):
        for v in range(4):
            products = []
            for u in range(2):
                k1 = i * 8 + v * 2 + u
                right = jnp.concatenate([column(mids_s, k1), column(midt_s, k1)], axis=1).astype(jnp.bfloat16)
                right = jnp.concatenate([right, right], axis=0)
                spec = jnp.dot(second_ref[...], right, preferred_element_type=jnp.float32)
                sig_r, sig_i = spec[:SIDE, :128], spec[SIDE:, :128]
                tap_r, tap_i = (spec[:SIDE, 128:] + skip) * scale, spec[SIDE:, 128:] * scale
                pair = [sig_r * tap_r - sig_i * tap_i, sig_r * tap_i + sig_i * tap_r]
                products.append(jnp.concatenate(pair, axis=0).astype(jnp.bfloat16))
            right = jnp.concatenate(products, axis=1)
            right = jnp.concatenate([right, right], axis=0)
            back = jnp.dot(third_ref[...], right, preferred_element_type=jnp.float32)
            for u in range(2):
                k1 = i * 8 + v * 2 + u
                back_s[pl.ds(pl.multiple_of(k1 * WIDE, 8), 2 * SIDE), :] = back[:, u * 128 : (u + 1) * 128]
        return carry

    lax.fori_loop(0, SIDE // 8, stage_spectrum, 0)

    def stage_last(i, carry):
        for u in range(16):
            n2 = i * 16 + u
            right = column(back_s, n2).astype(jnp.bfloat16)
            right = jnp.concatenate([right, right], axis=0)
            res_s[pl.ds(n2, 2 * half, stride=NARROW), :] = jnp.dot(
                last_ref[n2], right, preferred_element_type=jnp.float32
            )
        return carry

    lax.fori_loop(0, SIDE // 16, stage_last, 0)
    for d in range(blocks):
        for a in range(parts):
            for s in range(2):
                row = (s * half + d * parts + a) * NARROW
                begin = s * tokens + a * SIDE
                out_ref[d, begin : begin + SIDE, :] = res_s[row : row + SIDE, :].astype(jnp.bfloat16)


def conv(got, skip, tabs):
    blocks, rows, lanes = got.shape
    tokens = rows // 3
    full = pl.BlockSpec(memory_space=pltpu.VMEM)
    return pl.pallas_call(
        functools.partial(conv_kernel, blocks=blocks, tokens=tokens),
        out_shape=jax.ShapeDtypeStruct((blocks, 2 * tokens, lanes), jnp.bfloat16),
        in_specs=[full] * 2 + [pl.BlockSpec(memory_space=pl.ANY)] + [full] * 3,
        out_specs=full,
        scratch_shapes=[
            pltpu.VMEM((SIDE * NARROW, lanes), jnp.float32),
            pltpu.VMEM((SIDE // 2 * NARROW, lanes), jnp.float32),
            pltpu.VMEM((SIDE * WIDE, lanes), jnp.float32),
            pltpu.VMEM((SIDE * WIDE, lanes), jnp.float32),
            pltpu.VMEM((SIDE * WIDE, lanes), jnp.float32),
            pltpu.VMEM((SIDE * NARROW, lanes), jnp.float32),
            pltpu.VMEM(tabs[0].shape, jnp.bfloat16),
            pltpu.SemaphoreType.DMA,
        ],
        compiler_params=pltpu.CompilerParams(vmem_limit_bytes=32 << 20),
        cost_estimate=pl.CostEstimate(flops=1_000_000_000, bytes_accessed=1 << 20, transcendentals=0),
        name="long_conv",
    )(got, skip, *tabs)


VMEM = pl.BlockSpec(memory_space=pltpu.VMEM)
SMEM = pl.BlockSpec(memory_space=pltpu.SMEM)


def gate_kernel(word_ref, off_ref, key_ref, value_ref, taps_ref, out_ref, tok_s):
    tokens = off_ref.shape[1]
    block = pl.program_id(0)

    @pl.when(block == 0)
    def _():
        for s in range(2):
            row = mix_bits(off_ref[s : s + 1, :])
            row = mix_bits(row ^ word_ref[0])
            tok_s[s * tokens : (s + 1) * tokens, :] = jnp.broadcast_to(row, (128, tokens)).T

    count = out_ref.shape[0]
    for c in range(count):
        lanes = slice(c * 128, (c + 1) * 128)
        channel = word_ref[1] + (block * count + c) * 128 + lax.broadcasted_iota(jnp.int32, (1, 128), 1)
        channel = channel * jnp.int32(668265263)
        for s in range(2):
            rows = slice(s * tokens, (s + 1) * tokens)
            hashed = mix_bits(tok_s[rows, :] ^ channel)
            low_bits = lax.shift_right_logical(hashed, jnp.full_like(hashed, 8)) & 65535
            keep = jnp.where(low_bits >= drop_level, jnp.float32(keep_scale), jnp.float32(0.0))
            product = key_ref[s, :, lanes].astype(jnp.float32) * value_ref[s, :, lanes].astype(jnp.float32)
            out_ref[c, rows, :] = (product * keep).astype(jnp.bfloat16)
        out_ref[c, 2 * tokens : 3 * tokens, :] = taps_ref[:, lanes].astype(jnp.bfloat16)


def gate_and_pack(words, offsets, key_proj, value_proj, taps):
    _, tokens, width = key_proj.shape
    blocks = width // 128
    count = 4
    part = pl.BlockSpec((2, tokens, count * 128), lambda d: (0, 0, d))
    return pl.pallas_call(
        gate_kernel,
        grid=(blocks // count,),
        out_shape=jax.ShapeDtypeStruct((blocks, 3 * tokens, 128), jnp.bfloat16),
        in_specs=[
            SMEM,
            pl.BlockSpec((2, tokens), lambda d: (0, 0)),
            part,
            part,
            pl.BlockSpec((tokens, count * 128), lambda d: (0, d)),
        ],
        out_specs=pl.BlockSpec((count, 3 * tokens, 128), lambda d: (d, 0, 0)),
        scratch_shapes=[pltpu.VMEM((2 * tokens, 128), jnp.int32)],
        name="gate_and_pack",
    )(words, offsets, key_proj, value_proj, taps)


def gate_rows(query_ref, mixed_ref, rows_ref):
    tokens = query_ref.shape[1]
    for c in range(mixed_ref.shape[0]):
        lanes = slice(c * 128, (c + 1) * 128)
        for s in range(2):
            rows = slice(s * tokens, (s + 1) * tokens)
            mixed = mixed_ref[c, rows, :].astype(jnp.float32)
            rows_ref[rows, lanes] = (query_ref[s, :, lanes].astype(jnp.float32) * mixed).astype(jnp.bfloat16)


def fetch(sources, index, held, sem):
    for place, source in enumerate(sources):

        @pl.when(index == place)
        def _():
            pltpu.make_async_copy(source, held, sem).start()


def arrived(sources, held, sem):
    pltpu.make_async_copy(sources[0], held, sem).wait()


def place_of(sel_ref, pair, mine):
    kept = jnp.where(pair == 0, sel_ref[0], sel_ref[1])
    return 2 * pair + (kept if mine else 1 - kept)


def dots_into(rows_ref, sources, wanted, held, sems, store, before=lambda: None):
    for i, (side, place) in enumerate(wanted):
        fetch(sources[4 * side : 4 * side + 4], place, held.at[i], sems.at[i])
    before()
    for i in range(len(wanted)):
        arrived(sources, held.at[i], sems.at[i])
        store(i, jnp.dot(rows_ref[...], held[i], preferred_element_type=jnp.float32))


def half_products(sel_ref, rows_ref, sources, give_refs, keep_ref, held, sems, before=lambda: None):
    home, away = sel_ref[2], 1 - sel_ref[2]
    wanted = [(0, place_of(sel_ref, pair, mine)) for pair, mine in ((away, False), (home, False), (away, True))]

    def store(i, part):
        if i == 2:
            keep_ref[...] = part
        else:
            give = part.astype(jnp.bfloat16)
            if isinstance(give_refs[i], tuple):
                depth = give.shape[0] // 2
                for half, ref in enumerate(give_refs[i]):
                    ref[...] = give[half * depth : (half + 1) * depth]
            else:
                give_refs[i][...] = give

    dots_into(rows_ref, sources, wanted, held, sems, store, before)


def line_kernel(sel_ref, query_ref, mixed_ref, *refs):
    sources, (rows_ref, give_ref, home_ref, keep_ref, held, sems) = refs[:4], refs[4:]
    before = functools.partial(gate_rows, query_ref, mixed_ref, rows_ref)
    half_products(sel_ref, rows_ref, sources, (give_ref, home_ref), keep_ref, held, sems, before)


def across_kernel(sel_ref, rows_ref, *refs):
    sources, (top_ref, bottom_ref, home_ref, keep_ref, held, sems) = refs[:4], refs[4:]
    half_products(sel_ref, rows_ref, sources, ((top_ref, bottom_ref), home_ref), keep_ref, held, sems)


def home_kernel(sel_ref, rows_ref, given_ref, given_x_ref, *refs):
    sources, (out_ref, held, sems) = refs[:8], refs[8:]
    wanted = [(side, place_of(sel_ref, sel_ref[2], True)) for side in (0, 1)]

    def store(i, part):
        out_ref[i] = part + (given_ref, given_x_ref)[i][...].astype(jnp.float32)

    dots_into(rows_ref, sources, wanted, held, sems, store)


def products(kernel, outs, sel, left, weights, dots, grant=56):
    rows, (depth, width) = outs[-1].shape[-2], weights[0].shape
    return pl.pallas_call(
        kernel,
        out_shape=outs,
        in_specs=[SMEM] + [VMEM] * len(left) + [pl.BlockSpec(memory_space=pl.ANY)] * len(weights),
        out_specs=(VMEM,) * len(outs),
        scratch_shapes=[
            pltpu.VMEM((dots, depth, width), jnp.bfloat16),
            pltpu.SemaphoreType.DMA((dots,)),
        ],
        compiler_params=pltpu.CompilerParams(vmem_limit_bytes=grant << 20),
        cost_estimate=pl.CostEstimate(
            flops=2 * dots * rows * depth * width, bytes_accessed=8 << 20, transcendentals=0
        ),
        name="products",
    )(sel, *left, *weights)


def finish_kernel(x_ref, home_ref, here_ref, there_ref, out_ref):
    width = here_ref.shape[1]
    for half, away_ref in enumerate((here_ref, there_ref)):
        total = (home_ref[half] + away_ref[...].astype(jnp.float32)).astype(jnp.bfloat16)

        @pl.when(x_ref[0] == half)
        def _():
            out_ref[:, :width] = total

        @pl.when(x_ref[0] != half)
        def _():
            out_ref[:, width:] = total


def finish(x, home, here, there):
    rows, width = here.shape
    return pl.pallas_call(
        finish_kernel,
        out_shape=jax.ShapeDtypeStruct((rows, 2 * width), jnp.bfloat16),
        in_specs=[SMEM, VMEM, VMEM, VMEM],
        out_specs=VMEM,
        compiler_params=pltpu.CompilerParams(vmem_limit_bytes=16 << 20),
        name="finish",
    )(x, home, here, there)


def per_device_mesh(
    query_proj,
    key_proj,
    value_proj,
    filter_taps,
    skip_gain,
    out_weight,
    drop_seed,
    drop_step,
    offsets,
):
    group_width = query_proj.shape[2]
    ctx, ch = lax.axis_index("ctx"), lax.axis_index("ch")
    z, x, y, core = ctx // 2, ctx % 2, ch // 2, ch % 2

    def along_z(value, pairs):
        return lax.ppermute(value, "ctx", [(2 * a + k, 2 * b + k) for a, b in pairs for k in (0, 1)])

    def across_x(value):
        return lax.ppermute(value, "ctx", [(i, i ^ 1) for i in range(8)])

    def to_sibling(value):
        return lax.ppermute(value, "ch", [(j, j ^ 1) for j in range(4)])

    def across_y(value):
        return lax.ppermute(value, "ch", [(j, j ^ 2) for j in range(4)])

    own = out_weight
    middle = along_z(own, [(1, 2), (2, 1)])
    near = along_z(own, [(0, 1), (1, 0), (2, 3), (3, 2)])
    own_x = across_x(own)
    seed_word = mix_bits(drop_seed[0] * jnp.int32(-1640531535) + drop_step[0])
    words = jnp.stack([seed_word, ch * group_width])
    packed = gate_and_pack(words, offsets, key_proj, value_proj, filter_taps)
    got = lax.all_to_all(packed, "ctx", split_axis=0, concat_axis=0, tiled=True)

    tabs = tables(lax.optimization_barrier(small_waves()))
    near, middle, tabs = lax.optimization_barrier((near, middle, tabs))
    near, own_x = lax.optimization_barrier((near, own_x))
    near_x = across_x(near)
    got, near, middle, tabs = lax.optimization_barrier((got, near, middle, tabs))
    far_mid = along_z(near, [(2, 1), (1, 2)])
    far_ends = along_z(middle, [(1, 0), (2, 3)])
    skip_local = lax.dynamic_slice_in_dim(skip_gain, ctx * 128, 128)
    mixed = conv(got, skip_local[None, :], tabs)
    back = lax.all_to_all(mixed, "ctx", split_axis=0, concat_axis=0, tiled=True)
    far_mid, far_ends, near_x, mixed = lax.optimization_barrier((far_mid, far_ends, near_x, mixed))
    inner = (z == 1) | (z == 2)
    three_ends = along_z(far_mid, [(1, 0), (2, 3)])
    third = jnp.where(inner, middle, far_ends)
    third_x = across_x(third)
    three_ends, third_x = lax.optimization_barrier((three_ends, third_x))
    fourth = jnp.where(inner, far_mid, three_ends)
    fourth_x = across_x(fourth)

    near_kept = (z + core) % 2
    sel = jnp.stack([near_kept, (near_kept + inner) % 2, (z // 2 + y) % 2]).astype(jnp.int32)
    line = (own, near, third, fourth)
    row_count, half_width = 2 * query_proj.shape[1], own.shape[1]

    def out(dtype, *lead, rows=row_count):
        return jax.ShapeDtypeStruct(lead + (rows, half_width), dtype)

    rows_type = jax.ShapeDtypeStruct((row_count, group_width), jnp.bfloat16)
    outs = (rows_type, out(jnp.bfloat16), out(jnp.bfloat16), out(jnp.float32))
    rows, give, give_line, keep = products(line_kernel, outs, sel, (query_proj, back), line, 3)
    given, keep, fourth_x = lax.optimization_barrier((to_sibling(give), keep, fourth_x))
    line_x = (own_x, near_x, third_x, fourth_x)
    here = across_y((keep + given.astype(jnp.float32)).astype(jnp.bfloat16))
    quarter = out(jnp.bfloat16, rows=row_count // 2)
    outs = (quarter, quarter, out(jnp.bfloat16), out(jnp.float32))
    top, bottom, give_home, keep = products(across_kernel, outs, sel, (rows,), line_x, 3)
    top, bottom = to_sibling(top), to_sibling(bottom)
    top, bottom, keep, here = lax.optimization_barrier((top, bottom, keep, here))
    away = keep + jnp.concatenate([top, bottom], axis=0).astype(jnp.float32)
    there = across_y(away.astype(jnp.bfloat16))
    left = (rows, to_sibling(give_line), to_sibling(give_home))
    (home,) = products(home_kernel, (out(jnp.float32, 2),), sel, left, line + line_x, 2, 24)
    return finish(x.astype(jnp.int32)[None], home, here, there).reshape(query_proj.shape)


def solution(mesh):
    sizes = dict(mesh.shape)

    def per_device(query_proj, *rest):
        width = query_proj.shape[2]
        length = query_proj.shape[1] * sizes["ctx"]
        fits = sizes["ctx"] == 8 and sizes["ch"] == 4 and width == 1024 and length == 2048
        return (per_device_mesh if fits else per_device_plain)(query_proj, *rest)

    return jax.shard_map(
        per_device,
        mesh=mesh,
        in_specs=(
            P(None, "ctx", "ch"),
            P(None, "ctx", "ch"),
            P(None, "ctx", "ch"),
            P("ctx", "ch"),
            P("ch"),
            P("ch", "ctx"),
            P(),
            P(),
            P(None, "ctx"),
        ),
        out_specs=P(None, "ctx", "ch"),
        check_vma=False,
    )
```

```python
import functools
import math

import jax
import jax.numpy as jnp
from jax import lax
from jax.experimental import pallas as pl
from jax.experimental.pallas import tpu as pltpu
from jax.sharding import PartitionSpec as P

drop_level = 6554
keep_scale = 65536.0 / (65536.0 - 6554.0)


def mix_bits(hashed):
    hashed = hashed ^ lax.shift_right_logical(hashed, jnp.full_like(hashed, 16))
    hashed = hashed * jnp.int32(73244475)
    hashed = hashed ^ lax.shift_right_logical(hashed, jnp.full_like(hashed, 16))
    hashed = hashed * jnp.int32(73244475)
    hashed = hashed ^ lax.shift_right_logical(hashed, jnp.full_like(hashed, 16))
    return hashed


def keep_mask(drop_seed, drop_step, positions, channel_ids):
    seed_word = mix_bits(drop_seed[0] * jnp.int32(-1640531535) + drop_step[0])
    hashed = mix_bits(seed_word ^ mix_bits(positions))
    hashed = mix_bits(hashed ^ channel_ids * jnp.int32(668265263))
    low_bits = lax.shift_right_logical(hashed, jnp.full_like(hashed, 8)) & 65535
    return low_bits >= drop_level


def phase_table(count_rows, count_cols, period, direction):
    product = (
        jnp.arange(count_rows, dtype=jnp.int32)[:, None]
        * jnp.arange(count_cols, dtype=jnp.int32)[None, :]
        % period
    )
    angles = direction * 2.0 * math.pi * product.astype(jnp.float32) / period
    return (jnp.cos(angles), jnp.sin(angles))


def einsum_high(formula, left_part, right_part):
    return jnp.einsum(formula, left_part, right_part, precision=lax.Precision.HIGHEST)


def complex_einsum(formula, left_pair, right_pair):
    left_real, left_imag = left_pair
    right_real, right_imag = right_pair
    real_part = einsum_high(formula, left_real, right_real)
    imag_part = None
    if left_imag is not None and right_imag is not None:
        real_part = real_part - einsum_high(formula, left_imag, right_imag)
    if right_imag is not None:
        imag_part = einsum_high(formula, left_real, right_imag)
    cross_term = einsum_high(formula, left_imag, right_real)
    imag_part = cross_term if imag_part is None else imag_part + cross_term
    return (real_part, imag_part)


def complex_product(first_pair, second_pair):
    return (
        first_pair[0] * second_pair[0] - first_pair[1] * second_pair[1],
        first_pair[0] * second_pair[1] + first_pair[1] * second_pair[0],
    )


def grid_shape(length):
    columns = min(256, length)
    period = 2 * length
    return (columns, period // columns, period)


def forward_spectrum(signal_pair, length):
    columns, rows_all, period = grid_shape(length)
    half_rows = rows_all // 2
    shaped = tuple(
        (
            (
                None
                if part_item is None
                else part_item.reshape(part_item.shape[0], half_rows, columns, part_item.shape[2])
            )
            for part_item in signal_pair
        )
    )
    sectioned = complex_einsum(
        "kr,nrcd->ndkc", phase_table(rows_all, half_rows, rows_all, -1.0), shaped
    )
    sectioned = complex_product(sectioned, phase_table(rows_all, columns, period, -1.0))
    return complex_einsum("ndkc,cj->ndkj", sectioned, phase_table(columns, columns, columns, -1.0))


def inverse_signal(spectrum, length):
    columns, rows_all, period = grid_shape(length)
    half_rows = rows_all // 2
    sectioned = complex_einsum(
        "ndkj,jc->ndkc", spectrum, phase_table(columns, columns, columns, 1.0)
    )
    sectioned = complex_product(sectioned, phase_table(rows_all, columns, period, 1.0))
    last_table = phase_table(half_rows, rows_all, rows_all, 1.0)
    real_part = einsum_high("rk,ndkc->nrcd", last_table[0], sectioned[0]) - einsum_high(
        "rk,ndkc->nrcd", last_table[1], sectioned[1]
    )
    pieces_out = (real_part,)
    return tuple(
        (
            item_part.reshape(item_part.shape[0], length, item_part.shape[3]) / period
            for item_part in pieces_out
        )
    )


def convolve_plain(signal, filter_spec):
    length = signal.shape[1]
    spectrum = forward_spectrum((signal, None), length)
    product = complex_product(spectrum, filter_spec)
    return inverse_signal(product, length)[0]


def per_device_plain(
    query_proj,
    key_proj,
    value_proj,
    filter_taps,
    skip_gain,
    out_weight,
    drop_seed,
    drop_step,
    offsets,
):
    group_width = query_proj.shape[2]
    channel_ids = lax.axis_index("ch") * group_width + jnp.arange(group_width, dtype=jnp.int32)
    keep_flags = keep_mask(drop_seed, drop_step, offsets[:, :, None], channel_ids[None, None, :])
    gated = (
        key_proj.astype(jnp.float32)
        * value_proj.astype(jnp.float32)
        * jnp.where(keep_flags, keep_scale, 0.0)
    ).astype(jnp.bfloat16)
    tap_cols = lax.all_to_all(filter_taps, "ctx", split_axis=1, concat_axis=0, tiled=True)
    local_width = tap_cols.shape[1]
    skip_local = lax.dynamic_slice_in_dim(
        skip_gain, lax.axis_index("ctx") * local_width, local_width
    )
    filter_spec = forward_spectrum((tap_cols[None], None), tap_cols.shape[0])
    signal = lax.all_to_all(gated, "ctx", split_axis=2, concat_axis=1, tiled=True).astype(
        jnp.float32
    )
    convolved = convolve_plain(signal, filter_spec)
    mixed_cols = (convolved + skip_local * signal).astype(jnp.bfloat16)
    mixed = lax.all_to_all(mixed_cols, "ctx", split_axis=1, concat_axis=2, tiled=True)
    gate_out = (query_proj.astype(jnp.float32) * mixed.astype(jnp.float32)).astype(jnp.bfloat16)
    flat_rows = gate_out.reshape(-1, group_width)
    partial_value = jnp.dot(
        flat_rows,
        lax.all_gather(out_weight, "ctx", axis=1, tiled=True),
        preferred_element_type=jnp.float32,
    )
    summed = lax.psum_scatter(partial_value, "ch", scatter_dimension=1, tiled=True)
    return summed.astype(jnp.bfloat16).reshape(query_proj.shape)


SIDE = 64
WIDE = 2 * SIDE + 8
NARROW = SIDE + 8


def numbers(shape):
    return tuple(lax.broadcasted_iota(jnp.int32, shape, axis) for axis in range(len(shape)))


def waves(steps):
    angle = (steps % (SIDE * SIDE)).astype(jnp.float32) * (2.0 * math.pi / (SIDE * SIDE))
    return jnp.cos(angle), jnp.sin(angle)


def turn(row_part, col_part, sign):
    return (row_part - col_part) * (sign * SIDE * SIDE // 4)


def high_low(value, low):
    high = lax.reduce_precision(value, 8, 7)
    return jnp.where(low, value - high, high).astype(jnp.bfloat16)


def small_waves():
    half = SIDE // 2
    row, col = numbers((2 * SIDE, 4 * half))
    first = waves(SIDE * (col % half) * (row % SIDE) + turn(row // SIDE, col // half % 2, 1))
    n2, row = numbers((SIDE, 2 * SIDE))
    first_shift = waves(n2 * (row % SIDE))
    row, col = numbers((2 * SIDE, 4 * SIDE))
    steps = SIDE * (row % SIDE) * (col % SIDE)
    second = waves(steps + turn(row // SIDE, col // SIDE % 2, 1))[0]
    third = waves(steps + turn(row // SIDE, col // SIDE % 2, -1))[0]
    row, col = numbers((2 * half, 4 * SIDE))
    last = waves(SIDE * (row % half) * (col % SIDE) + turn(row // half, col // SIDE % 2, -1))
    n2, col = numbers((SIDE, 4 * SIDE))
    last_shift = waves(n2 * (col % SIDE))
    return first, first_shift, second, third, last, last_shift


def tables(small):
    first, first_shift, second, third, last, last_shift = small
    value = first[0][None] * first_shift[0][:, :, None] - first[1][None] * first_shift[1][:, :, None]
    first_table = high_low(value, numbers(value.shape)[2] >= SIDE)
    value = last[0][None] * last_shift[0][:, None, :] - last[1][None] * last_shift[1][:, None, :]
    last_table = high_low(value, numbers(value.shape)[2] >= 2 * SIDE)
    low = numbers(second.shape)[1] >= 2 * SIDE
    return first_table, high_low(second, low), high_low(third, low), last_table


def conv_kernel(
    got_ref, skip_ref, source_ref, second_ref, third_ref, last_ref, out_ref,
    sig_s, tap_s, mids_s, midt_s, back_s, res_s, first_ref, sem, *, blocks, tokens
):
    half = SIDE // 2
    copy = pltpu.make_async_copy(source_ref, first_ref, sem)
    copy.start()
    parts = tokens // SIDE
    for d in range(blocks):
        for a in range(parts):
            n1 = d * parts + a
            for s in range(3):
                ref, row = (tap_s, n1) if s == 2 else (sig_s, s * half + n1)
                begin = s * tokens + a * SIDE
                ref[row * NARROW : row * NARROW + SIDE, :] = got_ref[d, begin : begin + SIDE, :].astype(jnp.float32)
    zero = jnp.zeros((half, 128), jnp.float32)
    copy.wait()

    def stage_first(i, carry):
        for u in range(16):
            n2 = i * 16 + u
            sig = sig_s[pl.ds(n2, 2 * half, stride=NARROW), :]
            tap = jnp.concatenate([tap_s[pl.ds(n2, half, stride=NARROW), :], zero], axis=0)
            right = jnp.concatenate([sig, tap], axis=1).astype(jnp.bfloat16)
            right = jnp.concatenate([right, right], axis=0)
            spec = jnp.dot(first_ref[n2], right, preferred_element_type=jnp.float32)
            rows = pl.ds(pl.multiple_of(n2 * WIDE, 8), 2 * SIDE)
            mids_s[rows, :] = spec[:, :128]
            midt_s[rows, :] = spec[:, 128:]
        return carry

    lax.fori_loop(0, SIDE // 16, stage_first, 0)
    skip = skip_ref[...]
    scale = 1.0 / (SIDE * SIDE)

    def column(ref, k):
        real = ref[pl.ds(k, SIDE, stride=WIDE), :]
        return jnp.concatenate([real, ref[pl.ds(SIDE + k, SIDE, stride=WIDE), :]], axis=0)

    def stage_spectrum(i, carry):
        for v in range(4):
            products = []
            for u in range(2):
                k1 = i * 8 + v * 2 + u
                right = jnp.concatenate([column(mids_s, k1), column(midt_s, k1)], axis=1).astype(jnp.bfloat16)
                right = jnp.concatenate([right, right], axis=0)
                spec = jnp.dot(second_ref[...], right, preferred_element_type=jnp.float32)
                sig_r, sig_i = spec[:SIDE, :128], spec[SIDE:, :128]
                tap_r, tap_i = (spec[:SIDE, 128:] + skip) * scale, spec[SIDE:, 128:] * scale
                pair = [sig_r * tap_r - sig_i * tap_i, sig_r * tap_i + sig_i * tap_r]
                products.append(jnp.concatenate(pair, axis=0).astype(jnp.bfloat16))
            right = jnp.concatenate(products, axis=1)
            right = jnp.concatenate([right, right], axis=0)
            back = jnp.dot(third_ref[...], right, preferred_element_type=jnp.float32)
            for u in range(2):
                k1 = i * 8 + v * 2 + u
                back_s[pl.ds(pl.multiple_of(k1 * WIDE, 8), 2 * SIDE), :] = back[:, u * 128 : (u + 1) * 128]
        return carry

    lax.fori_loop(0, SIDE // 8, stage_spectrum, 0)

    def stage_last(i, carry):
        for u in range(16):
            n2 = i * 16 + u
            right = column(back_s, n2).astype(jnp.bfloat16)
            right = jnp.concatenate([right, right], axis=0)
            res_s[pl.ds(n2, 2 * half, stride=NARROW), :] = jnp.dot(
                last_ref[n2], right, preferred_element_type=jnp.float32
            )
        return carry

    lax.fori_loop(0, SIDE // 16, stage_last, 0)
    for d in range(blocks):
        for a in range(parts):
            for s in range(2):
                row = (s * half + d * parts + a) * NARROW
                begin = s * tokens + a * SIDE
                out_ref[d, begin : begin + SIDE, :] = res_s[row : row + SIDE, :].astype(jnp.bfloat16)


def conv(got, skip, tabs):
    blocks, rows, lanes = got.shape
    tokens = rows // 3
    full = pl.BlockSpec(memory_space=pltpu.VMEM)
    return pl.pallas_call(
        functools.partial(conv_kernel, blocks=blocks, tokens=tokens),
        out_shape=jax.ShapeDtypeStruct((blocks, 2 * tokens, lanes), jnp.bfloat16),
        in_specs=[full] * 2 + [pl.BlockSpec(memory_space=pl.ANY)] + [full] * 3,
        out_specs=full,
        scratch_shapes=[
            pltpu.VMEM((SIDE * NARROW, lanes), jnp.float32),
            pltpu.VMEM((SIDE // 2 * NARROW, lanes), jnp.float32),
            pltpu.VMEM((SIDE * WIDE, lanes), jnp.float32),
            pltpu.VMEM((SIDE * WIDE, lanes), jnp.float32),
            pltpu.VMEM((SIDE * WIDE, lanes), jnp.float32),
            pltpu.VMEM((SIDE * NARROW, lanes), jnp.float32),
            pltpu.VMEM(tabs[0].shape, jnp.bfloat16),
            pltpu.SemaphoreType.DMA,
        ],
        compiler_params=pltpu.CompilerParams(vmem_limit_bytes=32 << 20),
        cost_estimate=pl.CostEstimate(flops=1_000_000_000, bytes_accessed=1 << 20, transcendentals=0),
        name="long_conv",
    )(got, skip, *tabs)


VMEM = pl.BlockSpec(memory_space=pltpu.VMEM)
SMEM = pl.BlockSpec(memory_space=pltpu.SMEM)


def gate_kernel(word_ref, off_ref, key_ref, value_ref, taps_ref, out_ref, tok_s):
    tokens = off_ref.shape[1]
    block = pl.program_id(0)

    @pl.when(block == 0)
    def _():
        for s in range(2):
            row = mix_bits(off_ref[s : s + 1, :])
            row = mix_bits(row ^ word_ref[0])
            tok_s[s * tokens : (s + 1) * tokens, :] = jnp.broadcast_to(row, (128, tokens)).T

    count = out_ref.shape[0]
    for c in range(count):
        lanes = slice(c * 128, (c + 1) * 128)
        channel = word_ref[1] + (block * count + c) * 128 + lax.broadcasted_iota(jnp.int32, (1, 128), 1)
        channel = channel * jnp.int32(668265263)
        for s in range(2):
            rows = slice(s * tokens, (s + 1) * tokens)
            hashed = mix_bits(tok_s[rows, :] ^ channel)
            low_bits = lax.shift_right_logical(hashed, jnp.full_like(hashed, 8)) & 65535
            keep = jnp.where(low_bits >= drop_level, jnp.float32(keep_scale), jnp.float32(0.0))
            product = key_ref[s, :, lanes].astype(jnp.float32) * value_ref[s, :, lanes].astype(jnp.float32)
            out_ref[c, rows, :] = (product * keep).astype(jnp.bfloat16)
        out_ref[c, 2 * tokens : 3 * tokens, :] = taps_ref[:, lanes].astype(jnp.bfloat16)


def gate_and_pack(words, offsets, key_proj, value_proj, taps):
    _, tokens, width = key_proj.shape
    blocks = width // 128
    count = 4
    part = pl.BlockSpec((2, tokens, count * 128), lambda d: (0, 0, d))
    return pl.pallas_call(
        gate_kernel,
        grid=(blocks // count,),
        out_shape=jax.ShapeDtypeStruct((blocks, 3 * tokens, 128), jnp.bfloat16),
        in_specs=[
            SMEM,
            pl.BlockSpec((2, tokens), lambda d: (0, 0)),
            part,
            part,
            pl.BlockSpec((tokens, count * 128), lambda d: (0, d)),
        ],
        out_specs=pl.BlockSpec((count, 3 * tokens, 128), lambda d: (d, 0, 0)),
        scratch_shapes=[pltpu.VMEM((2 * tokens, 128), jnp.int32)],
        name="gate_and_pack",
    )(words, offsets, key_proj, value_proj, taps)


def gate_rows(query_ref, mixed_ref, rows_ref):
    tokens = query_ref.shape[1]
    for c in range(mixed_ref.shape[0]):
        lanes = slice(c * 128, (c + 1) * 128)
        for s in range(2):
            rows = slice(s * tokens, (s + 1) * tokens)
            mixed = mixed_ref[c, rows, :].astype(jnp.float32)
            rows_ref[rows, lanes] = (query_ref[s, :, lanes].astype(jnp.float32) * mixed).astype(jnp.bfloat16)


def fetch(sources, index, held, sem):
    for place, source in enumerate(sources):

        @pl.when(index == place)
        def _():
            pltpu.make_async_copy(source, held, sem).start()


def arrived(sources, held, sem):
    pltpu.make_async_copy(sources[0], held, sem).wait()


def place_of(sel_ref, pair, mine):
    kept = sel_ref[0]
    return 2 * pair + (kept if mine else 1 - kept)


def dots_into(rows_ref, sources, wanted, held, sems, store, before=lambda: None):
    for i, (side, place) in enumerate(wanted):
        fetch(sources[4 * side : 4 * side + 4], place, held.at[i], sems.at[i])
    before()
    for i in range(len(wanted)):
        arrived(sources, held.at[i], sems.at[i])
        store(i, jnp.dot(rows_ref[...], held[i], preferred_element_type=jnp.float32))


def half_products(sel_ref, rows_ref, sources, give_refs, keep_ref, held, sems, before=lambda: None):
    home, away = sel_ref[1], 1 - sel_ref[1]
    wanted = [(0, place_of(sel_ref, pair, mine)) for pair, mine in ((away, False), (home, False), (away, True))]

    def store(i, part):
        if i == 2:
            keep_ref[...] = part
        else:
            give = part.astype(jnp.bfloat16)
            if isinstance(give_refs[i], tuple):
                depth = give.shape[0] // 2
                for half, ref in enumerate(give_refs[i]):
                    ref[...] = give[half * depth : (half + 1) * depth]
            else:
                give_refs[i][...] = give

    dots_into(rows_ref, sources, wanted, held, sems, store, before)


def line_kernel(sel_ref, query_ref, mixed_ref, *refs):
    sources, (rows_ref, give_ref, home_ref, keep_ref, held, sems) = refs[:4], refs[4:]
    before = functools.partial(gate_rows, query_ref, mixed_ref, rows_ref)
    half_products(sel_ref, rows_ref, sources, (give_ref, home_ref), keep_ref, held, sems, before)


def across_kernel(sel_ref, rows_ref, *refs):
    sources, (top_ref, bottom_ref, home_ref, keep_ref, held, sems) = refs[:4], refs[4:]
    half_products(sel_ref, rows_ref, sources, ((top_ref, bottom_ref), home_ref), keep_ref, held, sems)


def home_kernel(sel_ref, rows_ref, given_ref, given_x_ref, *refs):
    sources, (out_ref, held, sems) = refs[:8], refs[8:]
    wanted = [(side, place_of(sel_ref, sel_ref[1], True)) for side in (0, 1)]

    def store(i, part):
        out_ref[i] = part + (given_ref, given_x_ref)[i][...].astype(jnp.float32)

    dots_into(rows_ref, sources, wanted, held, sems, store)


def products(kernel, outs, sel, left, weights, dots, grant=56):
    rows, (depth, width) = outs[-1].shape[-2], weights[0].shape
    return pl.pallas_call(
        kernel,
        out_shape=outs,
        in_specs=[SMEM] + [VMEM] * len(left) + [pl.BlockSpec(memory_space=pl.ANY)] * len(weights),
        out_specs=(VMEM,) * len(outs),
        scratch_shapes=[
            pltpu.VMEM((dots, depth, width), jnp.bfloat16),
            pltpu.SemaphoreType.DMA((dots,)),
        ],
        compiler_params=pltpu.CompilerParams(vmem_limit_bytes=grant << 20),
        cost_estimate=pl.CostEstimate(
            flops=2 * dots * rows * depth * width, bytes_accessed=8 << 20, transcendentals=0
        ),
        name="products",
    )(sel, *left, *weights)


def finish_kernel(x_ref, home_ref, here_ref, there_ref, out_ref):
    width = here_ref.shape[1]
    for half, away_ref in enumerate((here_ref, there_ref)):
        total = (home_ref[half] + away_ref[...].astype(jnp.float32)).astype(jnp.bfloat16)

        @pl.when(x_ref[0] == half)
        def _():
            out_ref[:, :width] = total

        @pl.when(x_ref[0] != half)
        def _():
            out_ref[:, width:] = total


def finish(x, home, here, there):
    rows, width = here.shape
    return pl.pallas_call(
        finish_kernel,
        out_shape=jax.ShapeDtypeStruct((rows, 2 * width), jnp.bfloat16),
        in_specs=[SMEM, VMEM, VMEM, VMEM],
        out_specs=VMEM,
        compiler_params=pltpu.CompilerParams(vmem_limit_bytes=16 << 20),
        name="finish",
    )(x, home, here, there)


def per_device_mesh(
    query_proj,
    key_proj,
    value_proj,
    filter_taps,
    skip_gain,
    out_weight,
    drop_seed,
    drop_step,
    offsets,
):
    group_width = query_proj.shape[2]
    ctx, ch = lax.axis_index("ctx"), lax.axis_index("ch")
    z, x, y, core = ctx // 2, ctx % 2, ch // 2, ch % 2

    def along_z(value, pairs):
        return lax.ppermute(value, "ctx", [(2 * a + k, 2 * b + k) for a, b in pairs for k in (0, 1)])

    def across_x(value):
        return lax.ppermute(value, "ctx", [(i, i ^ 1) for i in range(8)])

    def to_sibling(value):
        return lax.ppermute(value, "ch", [(j, j ^ 1) for j in range(4)])

    def across_y(value):
        return lax.ppermute(value, "ch", [(j, j ^ 2) for j in range(4)])

    own = out_weight
    three = along_z(own, [(0, 3), (3, 0), (1, 2), (2, 1)])
    near = along_z(own, [(0, 1), (1, 0), (2, 3), (3, 2)])
    own_x = across_x(own)
    seed_word = mix_bits(drop_seed[0] * jnp.int32(-1640531535) + drop_step[0])
    words = jnp.stack([seed_word, ch * group_width])
    packed = gate_and_pack(words, offsets, key_proj, value_proj, filter_taps)
    got = lax.all_to_all(packed, "ctx", split_axis=0, concat_axis=0, tiled=True)

    tabs = tables(lax.optimization_barrier(small_waves()))
    near, tabs = lax.optimization_barrier((near, tabs))
    near, own_x = lax.optimization_barrier((near, own_x))
    near_x = across_x(near)
    three_x = across_x(three)
    got, near, near_x, three, tabs = lax.optimization_barrier((got, near, near_x, three, tabs))
    far_mid = along_z(near, [(2, 1), (1, 2)])
    far_ends = along_z(three, [(1, 0), (2, 3)])
    skip_local = lax.dynamic_slice_in_dim(skip_gain, ctx * 128, 128)
    mixed = conv(got, skip_local[None, :], tabs)
    back = lax.all_to_all(mixed, "ctx", split_axis=0, concat_axis=0, tiled=True)
    far_mid, far_ends, three_x, mixed = lax.optimization_barrier((far_mid, far_ends, three_x, mixed))
    two = jnp.where((z == 1) | (z == 2), far_mid, far_ends)
    two_x = across_x(two)

    kept = (z + core) % 2
    sel = jnp.stack([kept, (z // 2 + y) % 2]).astype(jnp.int32)
    line = (own, near, two, three)
    row_count, half_width = 2 * query_proj.shape[1], own.shape[1]

    def out(dtype, *lead, rows=row_count):
        return jax.ShapeDtypeStruct(lead + (rows, half_width), dtype)

    rows_type = jax.ShapeDtypeStruct((row_count, group_width), jnp.bfloat16)
    outs = (rows_type, out(jnp.bfloat16), out(jnp.bfloat16), out(jnp.float32))
    rows, give, give_line, keep = products(line_kernel, outs, sel, (query_proj, back), line, 3)
    give, two_x = lax.optimization_barrier((give, two_x))
    given = to_sibling(give)
    line_x = (own_x, near_x, two_x, three_x)
    here = across_y((keep + given.astype(jnp.float32)).astype(jnp.bfloat16))
    quarter = out(jnp.bfloat16, rows=row_count // 2)
    outs = (quarter, quarter, out(jnp.bfloat16), out(jnp.float32))
    top, bottom, give_home, keep = products(across_kernel, outs, sel, (rows,), line_x, 3)
    top, bottom = to_sibling(top), to_sibling(bottom)
    top, bottom, keep, here = lax.optimization_barrier((top, bottom, keep, here))
    away = keep + jnp.concatenate([top, bottom], axis=0).astype(jnp.float32)
    there = across_y(away.astype(jnp.bfloat16))
    left = (rows, to_sibling(give_line), to_sibling(give_home))
    (home,) = products(home_kernel, (out(jnp.float32, 2),), sel, left, line + line_x, 2, 24)
    return finish(x.astype(jnp.int32)[None], home, here, there).reshape(query_proj.shape)


def solution(mesh):
    sizes = dict(mesh.shape)

    def per_device(query_proj, *rest):
        width = query_proj.shape[2]
        length = query_proj.shape[1] * sizes["ctx"]
        fits = sizes["ctx"] == 8 and sizes["ch"] == 4 and width == 1024 and length == 2048
        return (per_device_mesh if fits else per_device_plain)(query_proj, *rest)

    return jax.shard_map(
        per_device,
        mesh=mesh,
        in_specs=(
            P(None, "ctx", "ch"),
            P(None, "ctx", "ch"),
            P(None, "ctx", "ch"),
            P("ctx", "ch"),
            P("ch"),
            P("ch", "ctx"),
            P(),
            P(),
            P(None, "ctx"),
        ),
        out_specs=P(None, "ctx", "ch"),
        check_vma=False,
    )
```

```python
import functools
import math

import jax
import jax.numpy as jnp
from jax import lax
from jax.experimental import pallas as pl
from jax.experimental.pallas import tpu as pltpu
from jax.sharding import PartitionSpec as P

drop_level = 6554
keep_scale = 65536.0 / (65536.0 - 6554.0)


def mix_bits(hashed):
    hashed = hashed ^ lax.shift_right_logical(hashed, jnp.full_like(hashed, 16))
    hashed = hashed * jnp.int32(73244475)
    hashed = hashed ^ lax.shift_right_logical(hashed, jnp.full_like(hashed, 16))
    hashed = hashed * jnp.int32(73244475)
    hashed = hashed ^ lax.shift_right_logical(hashed, jnp.full_like(hashed, 16))
    return hashed


def keep_mask(drop_seed, drop_step, positions, channel_ids):
    seed_word = mix_bits(drop_seed[0] * jnp.int32(-1640531535) + drop_step[0])
    hashed = mix_bits(seed_word ^ mix_bits(positions))
    hashed = mix_bits(hashed ^ channel_ids * jnp.int32(668265263))
    low_bits = lax.shift_right_logical(hashed, jnp.full_like(hashed, 8)) & 65535
    return low_bits >= drop_level


def phase_table(count_rows, count_cols, period, direction):
    product = (
        jnp.arange(count_rows, dtype=jnp.int32)[:, None]
        * jnp.arange(count_cols, dtype=jnp.int32)[None, :]
        % period
    )
    angles = direction * 2.0 * math.pi * product.astype(jnp.float32) / period
    return (jnp.cos(angles), jnp.sin(angles))


def einsum_high(formula, left_part, right_part):
    return jnp.einsum(formula, left_part, right_part, precision=lax.Precision.HIGHEST)


def complex_einsum(formula, left_pair, right_pair):
    left_real, left_imag = left_pair
    right_real, right_imag = right_pair
    real_part = einsum_high(formula, left_real, right_real)
    imag_part = None
    if left_imag is not None and right_imag is not None:
        real_part = real_part - einsum_high(formula, left_imag, right_imag)
    if right_imag is not None:
        imag_part = einsum_high(formula, left_real, right_imag)
    cross_term = einsum_high(formula, left_imag, right_real)
    imag_part = cross_term if imag_part is None else imag_part + cross_term
    return (real_part, imag_part)


def complex_product(first_pair, second_pair):
    return (
        first_pair[0] * second_pair[0] - first_pair[1] * second_pair[1],
        first_pair[0] * second_pair[1] + first_pair[1] * second_pair[0],
    )


def grid_shape(length):
    columns = min(256, length)
    period = 2 * length
    return (columns, period // columns, period)


def forward_spectrum(signal_pair, length):
    columns, rows_all, period = grid_shape(length)
    half_rows = rows_all // 2
    shaped = tuple(
        (
            (
                None
                if part_item is None
                else part_item.reshape(part_item.shape[0], half_rows, columns, part_item.shape[2])
            )
            for part_item in signal_pair
        )
    )
    sectioned = complex_einsum(
        "kr,nrcd->ndkc", phase_table(rows_all, half_rows, rows_all, -1.0), shaped
    )
    sectioned = complex_product(sectioned, phase_table(rows_all, columns, period, -1.0))
    return complex_einsum("ndkc,cj->ndkj", sectioned, phase_table(columns, columns, columns, -1.0))


def inverse_signal(spectrum, length):
    columns, rows_all, period = grid_shape(length)
    half_rows = rows_all // 2
    sectioned = complex_einsum(
        "ndkj,jc->ndkc", spectrum, phase_table(columns, columns, columns, 1.0)
    )
    sectioned = complex_product(sectioned, phase_table(rows_all, columns, period, 1.0))
    last_table = phase_table(half_rows, rows_all, rows_all, 1.0)
    real_part = einsum_high("rk,ndkc->nrcd", last_table[0], sectioned[0]) - einsum_high(
        "rk,ndkc->nrcd", last_table[1], sectioned[1]
    )
    pieces_out = (real_part,)
    return tuple(
        (
            item_part.reshape(item_part.shape[0], length, item_part.shape[3]) / period
            for item_part in pieces_out
        )
    )


def convolve_plain(signal, filter_spec):
    length = signal.shape[1]
    spectrum = forward_spectrum((signal, None), length)
    product = complex_product(spectrum, filter_spec)
    return inverse_signal(product, length)[0]


def per_device_plain(
    query_proj,
    key_proj,
    value_proj,
    filter_taps,
    skip_gain,
    out_weight,
    drop_seed,
    drop_step,
    offsets,
):
    group_width = query_proj.shape[2]
    channel_ids = lax.axis_index("ch") * group_width + jnp.arange(group_width, dtype=jnp.int32)
    keep_flags = keep_mask(drop_seed, drop_step, offsets[:, :, None], channel_ids[None, None, :])
    gated = (
        key_proj.astype(jnp.float32)
        * value_proj.astype(jnp.float32)
        * jnp.where(keep_flags, keep_scale, 0.0)
    ).astype(jnp.bfloat16)
    tap_cols = lax.all_to_all(filter_taps, "ctx", split_axis=1, concat_axis=0, tiled=True)
    local_width = tap_cols.shape[1]
    skip_local = lax.dynamic_slice_in_dim(
        skip_gain, lax.axis_index("ctx") * local_width, local_width
    )
    filter_spec = forward_spectrum((tap_cols[None], None), tap_cols.shape[0])
    signal = lax.all_to_all(gated, "ctx", split_axis=2, concat_axis=1, tiled=True).astype(
        jnp.float32
    )
    convolved = convolve_plain(signal, filter_spec)
    mixed_cols = (convolved + skip_local * signal).astype(jnp.bfloat16)
    mixed = lax.all_to_all(mixed_cols, "ctx", split_axis=1, concat_axis=2, tiled=True)
    gate_out = (query_proj.astype(jnp.float32) * mixed.astype(jnp.float32)).astype(jnp.bfloat16)
    flat_rows = gate_out.reshape(-1, group_width)
    partial_value = jnp.dot(
        flat_rows,
        lax.all_gather(out_weight, "ctx", axis=1, tiled=True),
        preferred_element_type=jnp.float32,
    )
    summed = lax.psum_scatter(partial_value, "ch", scatter_dimension=1, tiled=True)
    return summed.astype(jnp.bfloat16).reshape(query_proj.shape)


SIDE = 64
WIDE = 2 * SIDE + 8
NARROW = SIDE + 8


def numbers(shape):
    return tuple(lax.broadcasted_iota(jnp.int32, shape, axis) for axis in range(len(shape)))


def waves(steps):
    angle = (steps % (SIDE * SIDE)).astype(jnp.float32) * (2.0 * math.pi / (SIDE * SIDE))
    return jnp.cos(angle), jnp.sin(angle)


def turn(row_part, col_part, sign):
    return (row_part - col_part) * (sign * SIDE * SIDE // 4)


def high_low(value, low):
    high = lax.reduce_precision(value, 8, 7)
    return jnp.where(low, value - high, high).astype(jnp.bfloat16)


def small_waves():
    half = SIDE // 2
    row, col = numbers((2 * SIDE, 4 * half))
    first = waves(SIDE * (col % half) * (row % SIDE) + turn(row // SIDE, col // half % 2, 1))
    n2, row = numbers((SIDE, 2 * SIDE))
    first_shift = waves(n2 * (row % SIDE))
    row, col = numbers((2 * SIDE, 4 * SIDE))
    steps = SIDE * (row % SIDE) * (col % SIDE)
    second = waves(steps + turn(row // SIDE, col // SIDE % 2, 1))[0]
    third = waves(steps + turn(row // SIDE, col // SIDE % 2, -1))[0]
    row, col = numbers((2 * half, 4 * SIDE))
    last = waves(SIDE * (row % half) * (col % SIDE) + turn(row // half, col // SIDE % 2, -1))
    n2, col = numbers((SIDE, 4 * SIDE))
    last_shift = waves(n2 * (col % SIDE))
    return first, first_shift, second, third, last, last_shift


def tables(small):
    first, first_shift, second, third, last, last_shift = small
    value = first[0][None] * first_shift[0][:, :, None] - first[1][None] * first_shift[1][:, :, None]
    first_table = high_low(value, numbers(value.shape)[2] >= SIDE)
    value = last[0][None] * last_shift[0][:, None, :] - last[1][None] * last_shift[1][:, None, :]
    last_table = high_low(value, numbers(value.shape)[2] >= 2 * SIDE)
    low = numbers(second.shape)[1] >= 2 * SIDE
    return first_table, high_low(second, low), high_low(third, low), last_table


def conv_kernel(
    got_ref, skip_ref, source_ref, second_ref, third_ref, last_ref, out_ref,
    sig_s, tap_s, mids_s, midt_s, back_s, res_s, first_ref, sem, *, blocks, tokens
):
    half = SIDE // 2
    copy = pltpu.make_async_copy(source_ref, first_ref, sem)
    copy.start()
    parts = tokens // SIDE
    for d in range(blocks):
        for a in range(parts):
            n1 = d * parts + a
            for s in range(3):
                ref, row = (tap_s, n1) if s == 2 else (sig_s, s * half + n1)
                begin = s * tokens + a * SIDE
                ref[row * NARROW : row * NARROW + SIDE, :] = got_ref[d, begin : begin + SIDE, :].astype(jnp.float32)
    zero = jnp.zeros((half, 128), jnp.float32)
    copy.wait()

    def stage_first(i, carry):
        for u in range(16):
            n2 = i * 16 + u
            sig = sig_s[pl.ds(n2, 2 * half, stride=NARROW), :]
            tap = jnp.concatenate([tap_s[pl.ds(n2, half, stride=NARROW), :], zero], axis=0)
            right = jnp.concatenate([sig, tap], axis=1).astype(jnp.bfloat16)
            right = jnp.concatenate([right, right], axis=0)
            spec = jnp.dot(first_ref[n2], right, preferred_element_type=jnp.float32)
            rows = pl.ds(pl.multiple_of(n2 * WIDE, 8), 2 * SIDE)
            mids_s[rows, :] = spec[:, :128]
            midt_s[rows, :] = spec[:, 128:]
        return carry

    lax.fori_loop(0, SIDE // 16, stage_first, 0)
    skip = skip_ref[...]
    scale = 1.0 / (SIDE * SIDE)

    def column(ref, k):
        real = ref[pl.ds(k, SIDE, stride=WIDE), :]
        return jnp.concatenate([real, ref[pl.ds(SIDE + k, SIDE, stride=WIDE), :]], axis=0)

    def stage_spectrum(i, carry):
        for v in range(4):
            products = []
            for u in range(2):
                k1 = i * 8 + v * 2 + u
                right = jnp.concatenate([column(mids_s, k1), column(midt_s, k1)], axis=1).astype(jnp.bfloat16)
                right = jnp.concatenate([right, right], axis=0)
                spec = jnp.dot(second_ref[...], right, preferred_element_type=jnp.float32)
                sig_r, sig_i = spec[:SIDE, :128], spec[SIDE:, :128]
                tap_r, tap_i = (spec[:SIDE, 128:] + skip) * scale, spec[SIDE:, 128:] * scale
                pair = [sig_r * tap_r - sig_i * tap_i, sig_r * tap_i + sig_i * tap_r]
                products.append(jnp.concatenate(pair, axis=0).astype(jnp.bfloat16))
            right = jnp.concatenate(products, axis=1)
            right = jnp.concatenate([right, right], axis=0)
            back = jnp.dot(third_ref[...], right, preferred_element_type=jnp.float32)
            for u in range(2):
                k1 = i * 8 + v * 2 + u
                back_s[pl.ds(pl.multiple_of(k1 * WIDE, 8), 2 * SIDE), :] = back[:, u * 128 : (u + 1) * 128]
        return carry

    lax.fori_loop(0, SIDE // 8, stage_spectrum, 0)

    def stage_last(i, carry):
        for u in range(16):
            n2 = i * 16 + u
            right = column(back_s, n2).astype(jnp.bfloat16)
            right = jnp.concatenate([right, right], axis=0)
            res_s[pl.ds(n2, 2 * half, stride=NARROW), :] = jnp.dot(
                last_ref[n2], right, preferred_element_type=jnp.float32
            )
        return carry

    lax.fori_loop(0, SIDE // 16, stage_last, 0)
    for d in range(blocks):
        for a in range(parts):
            for s in range(2):
                row = (s * half + d * parts + a) * NARROW
                begin = s * tokens + a * SIDE
                out_ref[d, begin : begin + SIDE, :] = res_s[row : row + SIDE, :].astype(jnp.bfloat16)


def conv(got, skip, tabs):
    blocks, rows, lanes = got.shape
    tokens = rows // 3
    full = pl.BlockSpec(memory_space=pltpu.VMEM)
    return pl.pallas_call(
        functools.partial(conv_kernel, blocks=blocks, tokens=tokens),
        out_shape=jax.ShapeDtypeStruct((blocks, 2 * tokens, lanes), jnp.bfloat16),
        in_specs=[full] * 2 + [pl.BlockSpec(memory_space=pl.ANY)] + [full] * 3,
        out_specs=full,
        scratch_shapes=[
            pltpu.VMEM((SIDE * NARROW, lanes), jnp.float32),
            pltpu.VMEM((SIDE // 2 * NARROW, lanes), jnp.float32),
            pltpu.VMEM((SIDE * WIDE, lanes), jnp.float32),
            pltpu.VMEM((SIDE * WIDE, lanes), jnp.float32),
            pltpu.VMEM((SIDE * WIDE, lanes), jnp.float32),
            pltpu.VMEM((SIDE * NARROW, lanes), jnp.float32),
            pltpu.VMEM(tabs[0].shape, jnp.bfloat16),
            pltpu.SemaphoreType.DMA,
        ],
        compiler_params=pltpu.CompilerParams(vmem_limit_bytes=32 << 20),
        cost_estimate=pl.CostEstimate(flops=1_000_000_000, bytes_accessed=1 << 20, transcendentals=0),
        name="long_conv",
    )(got, skip, *tabs)


VMEM = pl.BlockSpec(memory_space=pltpu.VMEM)
SMEM = pl.BlockSpec(memory_space=pltpu.SMEM)


def gate_kernel(word_ref, off_ref, key_ref, value_ref, taps_ref, out_ref, tok_s):
    tokens = off_ref.shape[1]
    block = pl.program_id(0)

    @pl.when(block == 0)
    def _():
        for s in range(2):
            row = mix_bits(off_ref[s : s + 1, :])
            row = mix_bits(row ^ word_ref[0])
            tok_s[s * tokens : (s + 1) * tokens, :] = jnp.broadcast_to(row, (128, tokens)).T

    count = out_ref.shape[0]
    for c in range(count):
        lanes = slice(c * 128, (c + 1) * 128)
        channel = word_ref[1] + (block * count + c) * 128 + lax.broadcasted_iota(jnp.int32, (1, 128), 1)
        channel = channel * jnp.int32(668265263)
        for s in range(2):
            rows = slice(s * tokens, (s + 1) * tokens)
            hashed = mix_bits(tok_s[rows, :] ^ channel)
            low_bits = lax.shift_right_logical(hashed, jnp.full_like(hashed, 8)) & 65535
            keep = jnp.where(low_bits >= drop_level, jnp.float32(keep_scale), jnp.float32(0.0))
            product = key_ref[s, :, lanes].astype(jnp.float32) * value_ref[s, :, lanes].astype(jnp.float32)
            out_ref[c, rows, :] = (product * keep).astype(jnp.bfloat16)
        out_ref[c, 2 * tokens : 3 * tokens, :] = taps_ref[:, lanes].astype(jnp.bfloat16)


def gate_and_pack(words, offsets, key_proj, value_proj, taps):
    _, tokens, width = key_proj.shape
    blocks = width // 128
    count = 4
    part = pl.BlockSpec((2, tokens, count * 128), lambda d: (0, 0, d))
    return pl.pallas_call(
        gate_kernel,
        grid=(blocks // count,),
        out_shape=jax.ShapeDtypeStruct((blocks, 3 * tokens, 128), jnp.bfloat16),
        in_specs=[
            SMEM,
            pl.BlockSpec((2, tokens), lambda d: (0, 0)),
            part,
            part,
            pl.BlockSpec((tokens, count * 128), lambda d: (0, d)),
        ],
        out_specs=pl.BlockSpec((count, 3 * tokens, 128), lambda d: (d, 0, 0)),
        scratch_shapes=[pltpu.VMEM((2 * tokens, 128), jnp.int32)],
        name="gate_and_pack",
    )(words, offsets, key_proj, value_proj, taps)


def gate_rows(query_ref, mixed_ref, rows_ref):
    tokens = query_ref.shape[1]
    for c in range(mixed_ref.shape[0]):
        lanes = slice(c * 128, (c + 1) * 128)
        for s in range(2):
            rows = slice(s * tokens, (s + 1) * tokens)
            mixed = mixed_ref[c, rows, :].astype(jnp.float32)
            rows_ref[rows, lanes] = (query_ref[s, :, lanes].astype(jnp.float32) * mixed).astype(jnp.bfloat16)


def fetch(sources, index, held, sem):
    for place, source in enumerate(sources):

        @pl.when(index == place)
        def _():
            pltpu.make_async_copy(source, held, sem).start()


def arrived(sources, held, sem):
    pltpu.make_async_copy(sources[0], held, sem).wait()


def place_of(sel_ref, pair, mine):
    kept = jnp.where(pair == 0, sel_ref[0], sel_ref[1])
    return 2 * pair + (kept if mine else 1 - kept)


def half_products(sel_ref, rows_s, sources, give_ref, keep_ref, held, give_s, keep_s, sems, before):
    home, away = sel_ref[2], 1 - sel_ref[2]
    for i, (pair, mine) in enumerate(((away, False), (home, False), (away, True))):
        fetch(sources, place_of(sel_ref, pair, mine), held.at[i], sems.at[i])
    before()
    copies = []
    for i in range(3):
        arrived(sources, held.at[i], sems.at[i])
        part = jnp.dot(rows_s[...], held[i], preferred_element_type=jnp.float32)
        if i < 2:
            give_s[i] = part.astype(jnp.bfloat16)
            copy = pltpu.make_async_copy(give_s.at[i], give_ref.at[i], sems.at[3 + i])
        else:
            keep_s[...] = part
            copy = pltpu.make_async_copy(keep_s, keep_ref, sems.at[5])
        copy.start()
        copies.append(copy)
    for copy in copies:
        copy.wait()


def line_kernel(sel_ref, query_ref, mixed_ref, *refs):
    sources, (rows_ref, give_ref, keep_ref) = refs[:4], refs[4:7]
    held, give_s, keep_s, rows_s, sems, query_s, mixed_s = refs[7:]
    query_in = pltpu.make_async_copy(query_ref, query_s, sems.at[6])
    mixed_in = pltpu.make_async_copy(mixed_ref, mixed_s, sems.at[7])
    rows_out = pltpu.make_async_copy(rows_s, rows_ref, sems.at[8])
    mixed_in.start()
    query_in.start()

    def before():
        mixed_in.wait()
        query_in.wait()
        gate_rows(query_s, mixed_s, rows_s)
        rows_out.start()

    half_products(sel_ref, rows_s, sources, give_ref, keep_ref, held, give_s, keep_s, sems, before)
    rows_out.wait()


def across_kernel(sel_ref, rows_ref, *refs):
    sources, (give_ref, keep_ref) = refs[:4], refs[4:6]
    held, give_s, keep_s, rows_s, sems = refs[6:]
    rows_in = pltpu.make_async_copy(rows_ref, rows_s, sems.at[6])
    rows_in.start()
    half_products(sel_ref, rows_s, sources, give_ref, keep_ref, held, give_s, keep_s, sems, rows_in.wait)


def dots_into(rows_ref, sources, wanted, held, sems, store):
    for i, (side, place) in enumerate(wanted):
        fetch(sources[4 * side : 4 * side + 4], place, held.at[i], sems.at[i])
    for i in range(len(wanted)):
        arrived(sources, held.at[i], sems.at[i])
        store(i, jnp.dot(rows_ref[...], held[i], preferred_element_type=jnp.float32))


def put_half(x_ref, same, block, out_ref, sem):
    width = block.shape[1]
    for place in range(2):

        @pl.when((x_ref[0] == same) == (place == 0))
        def _():
            copy = pltpu.make_async_copy(block, out_ref.at[:, place * width : (place + 1) * width], sem)
            copy.start()
            copy.wait()


def home_kernel(sel_ref, x_ref, rows_ref, given_ref, given_x_ref, here_ref, *refs):
    sources, (out_ref, part_ref, held, block, sems) = refs[:8], refs[8:]
    wanted = [(side, place_of(sel_ref, sel_ref[2], True)) for side in (0, 1)]

    def store(i, part):
        if i == 0:
            total = part + given_ref[1].astype(jnp.float32) + here_ref[...].astype(jnp.float32)
            block[...] = total.astype(jnp.bfloat16)
        else:
            part_ref[...] = part + given_x_ref[1].astype(jnp.float32)

    dots_into(rows_ref, sources, wanted, held, sems, store)
    put_half(x_ref, 0, block, out_ref, sems.at[2])


def home_products(sel, x, rows, given, given_x, here, weights):
    count, (depth, width) = rows.shape[0], weights[0].shape
    anywhere = pl.BlockSpec(memory_space=pl.ANY)
    return pl.pallas_call(
        home_kernel,
        out_shape=(
            jax.ShapeDtypeStruct((count, 2 * width), jnp.bfloat16),
            jax.ShapeDtypeStruct((count, width), jnp.float32),
        ),
        in_specs=[SMEM, SMEM] + [VMEM] * 4 + [anywhere] * 8,
        out_specs=(anywhere, VMEM),
        scratch_shapes=[
            pltpu.VMEM((2, depth, width), jnp.bfloat16),
            pltpu.VMEM((count, width), jnp.bfloat16),
            pltpu.SemaphoreType.DMA((3,)),
        ],
        compiler_params=pltpu.CompilerParams(vmem_limit_bytes=56 << 20),
        cost_estimate=pl.CostEstimate(
            flops=4 * count * depth * width, bytes_accessed=8 << 20, transcendentals=0
        ),
        name="products",
    )(sel, x, rows, given, given_x, here, *weights)


def finish_kernel(x_ref, part_ref, there_ref, so_far_ref, out_ref, block, sem):
    del so_far_ref
    block[...] = (part_ref[...] + there_ref[...].astype(jnp.float32)).astype(jnp.bfloat16)
    put_half(x_ref, 1, block, out_ref, sem)


def finish(x, part, there, so_far):
    anywhere = pl.BlockSpec(memory_space=pl.ANY)
    return pl.pallas_call(
        finish_kernel,
        out_shape=jax.ShapeDtypeStruct(so_far.shape, so_far.dtype),
        in_specs=[SMEM, VMEM, VMEM, anywhere],
        out_specs=anywhere,
        scratch_shapes=[pltpu.VMEM(there.shape, jnp.bfloat16), pltpu.SemaphoreType.DMA],
        input_output_aliases={3: 0},
        compiler_params=pltpu.CompilerParams(vmem_limit_bytes=16 << 20),
        name="finish",
    )(x, part, there, so_far)


def half_call(kernel, outs, sel, left, weights, scratch=()):
    rows, (depth, width) = outs[-1].shape[-2], weights[0].shape
    anywhere = pl.BlockSpec(memory_space=pl.ANY)
    return pl.pallas_call(
        kernel,
        out_shape=outs,
        in_specs=[SMEM] + [anywhere] * (len(left) + len(weights)),
        out_specs=(anywhere,) * len(outs),
        scratch_shapes=[
            pltpu.VMEM((3, depth, width), jnp.bfloat16),
            pltpu.VMEM((2, rows, width), jnp.bfloat16),
            pltpu.VMEM((rows, width), jnp.float32),
            pltpu.VMEM((rows, depth), jnp.bfloat16),
            pltpu.SemaphoreType.DMA((9,)),
            *scratch,
        ],
        compiler_params=pltpu.CompilerParams(vmem_limit_bytes=56 << 20),
        cost_estimate=pl.CostEstimate(
            flops=6 * rows * depth * width, bytes_accessed=8 << 20, transcendentals=0
        ),
        name="products",
    )(sel, *left, *weights)


def per_device_mesh(
    query_proj,
    key_proj,
    value_proj,
    filter_taps,
    skip_gain,
    out_weight,
    drop_seed,
    drop_step,
    offsets,
):
    group_width = query_proj.shape[2]
    ctx, ch = lax.axis_index("ctx"), lax.axis_index("ch")
    z, x, y, core = ctx // 2, ctx % 2, ch // 2, ch % 2

    def along_z(value, pairs):
        return lax.ppermute(value, "ctx", [(2 * a + k, 2 * b + k) for a, b in pairs for k in (0, 1)])

    def across_x(value):
        return lax.ppermute(value, "ctx", [(i, i ^ 1) for i in range(8)])

    def to_sibling(value):
        return lax.ppermute(value, "ch", [(j, j ^ 1) for j in range(4)])

    def across_y(value):
        return lax.ppermute(value, "ch", [(j, j ^ 2) for j in range(4)])

    own = out_weight
    near = along_z(own, [(0, 1), (1, 0), (2, 3), (3, 2)])
    middle = along_z(own, [(1, 2), (2, 1)])
    seed_word = mix_bits(drop_seed[0] * jnp.int32(-1640531535) + drop_step[0])
    words = jnp.stack([seed_word, ch * group_width])
    packed = gate_and_pack(words, offsets, key_proj, value_proj, filter_taps)
    got = lax.all_to_all(packed, "ctx", split_axis=0, concat_axis=0, tiled=True)
    own, packed = lax.optimization_barrier((own, packed))
    own_x = across_x(own)

    near, small = lax.optimization_barrier((near, small_waves()))
    far_mid = along_z(near, [(2, 1), (1, 2)])
    tabs = tables(small)
    middle, tabs = lax.optimization_barrier((middle, tabs))
    far_ends = along_z(middle, [(1, 0), (2, 3)])
    near, own_x, tabs = lax.optimization_barrier((near, own_x, tabs))
    near_x = across_x(near)
    inner = (z == 1) | (z == 2)
    third = jnp.where(inner, middle, far_ends)
    got, third, far_mid, tabs = lax.optimization_barrier((got, third, far_mid, tabs))
    three_ends = along_z(far_mid, [(1, 0), (2, 3)])
    third, near_x = lax.optimization_barrier((third, near_x))
    third_x = across_x(third)
    skip_local = lax.dynamic_slice_in_dim(skip_gain, ctx * 128, 128)
    mixed = conv(got, skip_local[None, :], tabs)
    back = lax.all_to_all(mixed, "ctx", split_axis=0, concat_axis=0, tiled=True)
    three_ends, third_x, mixed = lax.optimization_barrier((three_ends, third_x, mixed))
    fourth = jnp.where(inner, far_mid, three_ends)
    fourth_x = across_x(fourth)

    near_kept = (z + core) % 2
    sel = jnp.stack([near_kept, (near_kept + inner) % 2, (z // 2 + y) % 2]).astype(jnp.int32)
    line, line_x = (own, near, third, fourth), (own_x, near_x, third_x, fourth_x)
    row_count, half_width = 2 * query_proj.shape[1], own.shape[1]

    def out(dtype, *lead):
        return jax.ShapeDtypeStruct(lead + (row_count, half_width), dtype)

    outs = (out(jnp.bfloat16, 2), out(jnp.float32))
    rows_type = jax.ShapeDtypeStruct((row_count, group_width), jnp.bfloat16)
    scratch = (pltpu.VMEM(query_proj.shape, jnp.bfloat16), pltpu.VMEM(back.shape, jnp.bfloat16))
    rows, give, keep = half_call(line_kernel, (rows_type,) + outs, sel, (query_proj, back), line, scratch)
    given = to_sibling(give)
    here = across_y((keep + given[0].astype(jnp.float32)).astype(jnp.bfloat16))
    give, keep = half_call(across_kernel, outs, sel, (rows,), line_x)
    given_x = to_sibling(give)
    there = across_y((keep + given_x[0].astype(jnp.float32)).astype(jnp.bfloat16))
    x_word = x.astype(jnp.int32)[None]
    so_far, part = home_products(sel, x_word, rows, given, given_x, here, line + line_x)
    return finish(x_word, part, there, so_far).reshape(query_proj.shape)


def solution(mesh):
    sizes = dict(mesh.shape)

    def per_device(query_proj, *rest):
        width = query_proj.shape[2]
        length = query_proj.shape[1] * sizes["ctx"]
        fits = sizes["ctx"] == 8 and sizes["ch"] == 4 and width == 1024 and length == 2048
        return (per_device_mesh if fits else per_device_plain)(query_proj, *rest)

    return jax.shard_map(
        per_device,
        mesh=mesh,
        in_specs=(
            P(None, "ctx", "ch"),
            P(None, "ctx", "ch"),
            P(None, "ctx", "ch"),
            P("ctx", "ch"),
            P("ch"),
            P("ch", "ctx"),
            P(),
            P(),
            P(None, "ctx"),
        ),
        out_specs=P(None, "ctx", "ch"),
        check_vma=False,
    )
```

```python
import functools
import math

import jax
import jax.numpy as jnp
from jax import lax
from jax.experimental import pallas as pl
from jax.experimental.pallas import tpu as pltpu
from jax.sharding import PartitionSpec as P

drop_level = 6554
keep_scale = 65536.0 / (65536.0 - 6554.0)


def mix_bits(hashed):
    hashed = hashed ^ lax.shift_right_logical(hashed, jnp.full_like(hashed, 16))
    hashed = hashed * jnp.int32(73244475)
    hashed = hashed ^ lax.shift_right_logical(hashed, jnp.full_like(hashed, 16))
    hashed = hashed * jnp.int32(73244475)
    hashed = hashed ^ lax.shift_right_logical(hashed, jnp.full_like(hashed, 16))
    return hashed


def keep_mask(drop_seed, drop_step, positions, channel_ids):
    seed_word = mix_bits(drop_seed[0] * jnp.int32(-1640531535) + drop_step[0])
    hashed = mix_bits(seed_word ^ mix_bits(positions))
    hashed = mix_bits(hashed ^ channel_ids * jnp.int32(668265263))
    low_bits = lax.shift_right_logical(hashed, jnp.full_like(hashed, 8)) & 65535
    return low_bits >= drop_level


def phase_table(count_rows, count_cols, period, direction):
    product = (
        jnp.arange(count_rows, dtype=jnp.int32)[:, None]
        * jnp.arange(count_cols, dtype=jnp.int32)[None, :]
        % period
    )
    angles = direction * 2.0 * math.pi * product.astype(jnp.float32) / period
    return (jnp.cos(angles), jnp.sin(angles))


def einsum_high(formula, left_part, right_part):
    return jnp.einsum(formula, left_part, right_part, precision=lax.Precision.HIGHEST)


def complex_einsum(formula, left_pair, right_pair):
    left_real, left_imag = left_pair
    right_real, right_imag = right_pair
    real_part = einsum_high(formula, left_real, right_real)
    imag_part = None
    if left_imag is not None and right_imag is not None:
        real_part = real_part - einsum_high(formula, left_imag, right_imag)
    if right_imag is not None:
        imag_part = einsum_high(formula, left_real, right_imag)
    cross_term = einsum_high(formula, left_imag, right_real)
    imag_part = cross_term if imag_part is None else imag_part + cross_term
    return (real_part, imag_part)


def complex_product(first_pair, second_pair):
    return (
        first_pair[0] * second_pair[0] - first_pair[1] * second_pair[1],
        first_pair[0] * second_pair[1] + first_pair[1] * second_pair[0],
    )


def grid_shape(length):
    columns = min(256, length)
    period = 2 * length
    return (columns, period // columns, period)


def forward_spectrum(signal_pair, length):
    columns, rows_all, period = grid_shape(length)
    half_rows = rows_all // 2
    shaped = tuple(
        (
            (
                None
                if part_item is None
                else part_item.reshape(part_item.shape[0], half_rows, columns, part_item.shape[2])
            )
            for part_item in signal_pair
        )
    )
    sectioned = complex_einsum(
        "kr,nrcd->ndkc", phase_table(rows_all, half_rows, rows_all, -1.0), shaped
    )
    sectioned = complex_product(sectioned, phase_table(rows_all, columns, period, -1.0))
    return complex_einsum("ndkc,cj->ndkj", sectioned, phase_table(columns, columns, columns, -1.0))


def inverse_signal(spectrum, length):
    columns, rows_all, period = grid_shape(length)
    half_rows = rows_all // 2
    sectioned = complex_einsum(
        "ndkj,jc->ndkc", spectrum, phase_table(columns, columns, columns, 1.0)
    )
    sectioned = complex_product(sectioned, phase_table(rows_all, columns, period, 1.0))
    last_table = phase_table(half_rows, rows_all, rows_all, 1.0)
    real_part = einsum_high("rk,ndkc->nrcd", last_table[0], sectioned[0]) - einsum_high(
        "rk,ndkc->nrcd", last_table[1], sectioned[1]
    )
    pieces_out = (real_part,)
    return tuple(
        (
            item_part.reshape(item_part.shape[0], length, item_part.shape[3]) / period
            for item_part in pieces_out
        )
    )


def convolve_plain(signal, filter_spec):
    length = signal.shape[1]
    spectrum = forward_spectrum((signal, None), length)
    product = complex_product(spectrum, filter_spec)
    return inverse_signal(product, length)[0]


def per_device_plain(
    query_proj,
    key_proj,
    value_proj,
    filter_taps,
    skip_gain,
    out_weight,
    drop_seed,
    drop_step,
    offsets,
):
    group_width = query_proj.shape[2]
    channel_ids = lax.axis_index("ch") * group_width + jnp.arange(group_width, dtype=jnp.int32)
    keep_flags = keep_mask(drop_seed, drop_step, offsets[:, :, None], channel_ids[None, None, :])
    gated = (
        key_proj.astype(jnp.float32)
        * value_proj.astype(jnp.float32)
        * jnp.where(keep_flags, keep_scale, 0.0)
    ).astype(jnp.bfloat16)
    tap_cols = lax.all_to_all(filter_taps, "ctx", split_axis=1, concat_axis=0, tiled=True)
    local_width = tap_cols.shape[1]
    skip_local = lax.dynamic_slice_in_dim(
        skip_gain, lax.axis_index("ctx") * local_width, local_width
    )
    filter_spec = forward_spectrum((tap_cols[None], None), tap_cols.shape[0])
    signal = lax.all_to_all(gated, "ctx", split_axis=2, concat_axis=1, tiled=True).astype(
        jnp.float32
    )
    convolved = convolve_plain(signal, filter_spec)
    mixed_cols = (convolved + skip_local * signal).astype(jnp.bfloat16)
    mixed = lax.all_to_all(mixed_cols, "ctx", split_axis=1, concat_axis=2, tiled=True)
    gate_out = (query_proj.astype(jnp.float32) * mixed.astype(jnp.float32)).astype(jnp.bfloat16)
    flat_rows = gate_out.reshape(-1, group_width)
    partial_value = jnp.dot(
        flat_rows,
        lax.all_gather(out_weight, "ctx", axis=1, tiled=True),
        preferred_element_type=jnp.float32,
    )
    summed = lax.psum_scatter(partial_value, "ch", scatter_dimension=1, tiled=True)
    return summed.astype(jnp.bfloat16).reshape(query_proj.shape)


SIDE = 64
WIDE = 2 * SIDE + 8
NARROW = SIDE + 8


def numbers(shape):
    return tuple(lax.broadcasted_iota(jnp.int32, shape, axis) for axis in range(len(shape)))


def waves(steps):
    angle = (steps % (SIDE * SIDE)).astype(jnp.float32) * (2.0 * math.pi / (SIDE * SIDE))
    return jnp.cos(angle), jnp.sin(angle)


def turn(row_part, col_part, sign):
    return (row_part - col_part) * (sign * SIDE * SIDE // 4)


def high_low(value, low):
    high = lax.reduce_precision(value, 8, 7)
    return jnp.where(low, value - high, high).astype(jnp.bfloat16)


def small_waves():
    half = SIDE // 2
    row, col = numbers((2 * SIDE, 4 * half))
    first = waves(SIDE * (col % half) * (row % SIDE) + turn(row // SIDE, col // half % 2, 1))
    n2, row = numbers((SIDE, 2 * SIDE))
    first_shift = waves(n2 * (row % SIDE))
    row, col = numbers((2 * SIDE, 4 * SIDE))
    steps = SIDE * (row % SIDE) * (col % SIDE)
    second = waves(steps + turn(row // SIDE, col // SIDE % 2, 1))[0]
    third = waves(steps + turn(row // SIDE, col // SIDE % 2, -1))[0]
    row, col = numbers((2 * half, 4 * SIDE))
    last = waves(SIDE * (row % half) * (col % SIDE) + turn(row // half, col // SIDE % 2, -1))
    n2, col = numbers((SIDE, 4 * SIDE))
    last_shift = waves(n2 * (col % SIDE))
    return first, first_shift, second, third, last, last_shift


def tables(small):
    first, first_shift, second, third, last, last_shift = small
    value = first[0][None] * first_shift[0][:, :, None] - first[1][None] * first_shift[1][:, :, None]
    first_table = high_low(value, numbers(value.shape)[2] >= SIDE)
    value = last[0][None] * last_shift[0][:, None, :] - last[1][None] * last_shift[1][:, None, :]
    last_table = high_low(value, numbers(value.shape)[2] >= 2 * SIDE)
    low = numbers(second.shape)[1] >= 2 * SIDE
    return first_table, high_low(second, low), high_low(third, low), last_table


def conv_kernel(
    got_ref, skip_ref, source_ref, second_ref, third_ref, last_ref, out_ref,
    sig_s, tap_s, mids_s, midt_s, back_s, res_s, first_ref, sem, *, blocks, tokens
):
    half = SIDE // 2
    copy = pltpu.make_async_copy(source_ref, first_ref, sem)
    copy.start()
    parts = tokens // SIDE
    for d in range(blocks):
        for a in range(parts):
            n1 = d * parts + a
            for s in range(3):
                ref, row = (tap_s, n1) if s == 2 else (sig_s, s * half + n1)
                begin = s * tokens + a * SIDE
                ref[row * NARROW : row * NARROW + SIDE, :] = got_ref[d, begin : begin + SIDE, :].astype(jnp.float32)
    zero = jnp.zeros((half, 128), jnp.float32)
    copy.wait()

    def stage_first(i, carry):
        for u in range(16):
            n2 = i * 16 + u
            sig = sig_s[pl.ds(n2, 2 * half, stride=NARROW), :]
            tap = jnp.concatenate([tap_s[pl.ds(n2, half, stride=NARROW), :], zero], axis=0)
            right = jnp.concatenate([sig, tap], axis=1).astype(jnp.bfloat16)
            right = jnp.concatenate([right, right], axis=0)
            spec = jnp.dot(first_ref[n2], right, preferred_element_type=jnp.float32)
            rows = pl.ds(pl.multiple_of(n2 * WIDE, 8), 2 * SIDE)
            mids_s[rows, :] = spec[:, :128]
            midt_s[rows, :] = spec[:, 128:]
        return carry

    lax.fori_loop(0, SIDE // 16, stage_first, 0)
    skip = skip_ref[...]
    scale = 1.0 / (SIDE * SIDE)

    def column(ref, k):
        real = ref[pl.ds(k, SIDE, stride=WIDE), :]
        return jnp.concatenate([real, ref[pl.ds(SIDE + k, SIDE, stride=WIDE), :]], axis=0)

    def stage_spectrum(i, carry):
        for v in range(4):
            products = []
            for u in range(2):
                k1 = i * 8 + v * 2 + u
                right = jnp.concatenate([column(mids_s, k1), column(midt_s, k1)], axis=1).astype(jnp.bfloat16)
                right = jnp.concatenate([right, right], axis=0)
                spec = jnp.dot(second_ref[...], right, preferred_element_type=jnp.float32)
                sig_r, sig_i = spec[:SIDE, :128], spec[SIDE:, :128]
                tap_r, tap_i = (spec[:SIDE, 128:] + skip) * scale, spec[SIDE:, 128:] * scale
                pair = [sig_r * tap_r - sig_i * tap_i, sig_r * tap_i + sig_i * tap_r]
                products.append(jnp.concatenate(pair, axis=0).astype(jnp.bfloat16))
            right = jnp.concatenate(products, axis=1)
            right = jnp.concatenate([right, right], axis=0)
            back = jnp.dot(third_ref[...], right, preferred_element_type=jnp.float32)
            for u in range(2):
                k1 = i * 8 + v * 2 + u
                back_s[pl.ds(pl.multiple_of(k1 * WIDE, 8), 2 * SIDE), :] = back[:, u * 128 : (u + 1) * 128]
        return carry

    lax.fori_loop(0, SIDE // 8, stage_spectrum, 0)

    def stage_last(i, carry):
        for u in range(16):
            n2 = i * 16 + u
            right = column(back_s, n2).astype(jnp.bfloat16)
            right = jnp.concatenate([right, right], axis=0)
            res_s[pl.ds(n2, 2 * half, stride=NARROW), :] = jnp.dot(
                last_ref[n2], right, preferred_element_type=jnp.float32
            )
        return carry

    lax.fori_loop(0, SIDE // 16, stage_last, 0)
    for d in range(blocks):
        for a in range(parts):
            for s in range(2):
                row = (s * half + d * parts + a) * NARROW
                begin = s * tokens + a * SIDE
                out_ref[d, begin : begin + SIDE, :] = res_s[row : row + SIDE, :].astype(jnp.bfloat16)


def conv(got, skip, tabs):
    blocks, rows, lanes = got.shape
    tokens = rows // 3
    full = pl.BlockSpec(memory_space=pltpu.VMEM)
    return pl.pallas_call(
        functools.partial(conv_kernel, blocks=blocks, tokens=tokens),
        out_shape=jax.ShapeDtypeStruct((blocks, 2 * tokens, lanes), jnp.bfloat16),
        in_specs=[full] * 2 + [pl.BlockSpec(memory_space=pl.ANY)] + [full] * 3,
        out_specs=full,
        scratch_shapes=[
            pltpu.VMEM((SIDE * NARROW, lanes), jnp.float32),
            pltpu.VMEM((SIDE // 2 * NARROW, lanes), jnp.float32),
            pltpu.VMEM((SIDE * WIDE, lanes), jnp.float32),
            pltpu.VMEM((SIDE * WIDE, lanes), jnp.float32),
            pltpu.VMEM((SIDE * WIDE, lanes), jnp.float32),
            pltpu.VMEM((SIDE * NARROW, lanes), jnp.float32),
            pltpu.VMEM(tabs[0].shape, jnp.bfloat16),
            pltpu.SemaphoreType.DMA,
        ],
        compiler_params=pltpu.CompilerParams(vmem_limit_bytes=32 << 20),
        cost_estimate=pl.CostEstimate(flops=1_000_000_000, bytes_accessed=1 << 20, transcendentals=0),
        name="long_conv",
    )(got, skip, *tabs)


VMEM = pl.BlockSpec(memory_space=pltpu.VMEM)
SMEM = pl.BlockSpec(memory_space=pltpu.SMEM)


def gate_kernel(word_ref, off_ref, key_ref, value_ref, taps_ref, out_ref, tok_s):
    tokens = off_ref.shape[1]
    block = pl.program_id(0)

    @pl.when(block == 0)
    def _():
        for s in range(2):
            row = mix_bits(off_ref[s : s + 1, :])
            row = mix_bits(row ^ word_ref[0])
            tok_s[s * tokens : (s + 1) * tokens, :] = jnp.broadcast_to(row, (128, tokens)).T

    count = out_ref.shape[0]
    for c in range(count):
        lanes = slice(c * 128, (c + 1) * 128)
        channel = word_ref[1] + (block * count + c) * 128 + lax.broadcasted_iota(jnp.int32, (1, 128), 1)
        channel = channel * jnp.int32(668265263)
        for s in range(2):
            rows = slice(s * tokens, (s + 1) * tokens)
            hashed = mix_bits(tok_s[rows, :] ^ channel)
            low_bits = lax.shift_right_logical(hashed, jnp.full_like(hashed, 8)) & 65535
            keep = jnp.where(low_bits >= drop_level, jnp.float32(keep_scale), jnp.float32(0.0))
            product = key_ref[s, :, lanes].astype(jnp.float32) * value_ref[s, :, lanes].astype(jnp.float32)
            out_ref[c, rows, :] = (product * keep).astype(jnp.bfloat16)
        out_ref[c, 2 * tokens : 3 * tokens, :] = taps_ref[:, lanes].astype(jnp.bfloat16)


def gate_and_pack(words, offsets, key_proj, value_proj, taps):
    _, tokens, width = key_proj.shape
    blocks = width // 128
    count = 4
    part = pl.BlockSpec((2, tokens, count * 128), lambda d: (0, 0, d))
    return pl.pallas_call(
        gate_kernel,
        grid=(blocks // count,),
        out_shape=jax.ShapeDtypeStruct((blocks, 3 * tokens, 128), jnp.bfloat16),
        in_specs=[
            SMEM,
            pl.BlockSpec((2, tokens), lambda d: (0, 0)),
            part,
            part,
            pl.BlockSpec((tokens, count * 128), lambda d: (0, d)),
        ],
        out_specs=pl.BlockSpec((count, 3 * tokens, 128), lambda d: (d, 0, 0)),
        scratch_shapes=[pltpu.VMEM((2 * tokens, 128), jnp.int32)],
        name="gate_and_pack",
    )(words, offsets, key_proj, value_proj, taps)


def gate_rows(query_ref, mixed_ref, rows_ref):
    tokens = query_ref.shape[1]
    for c in range(mixed_ref.shape[0]):
        lanes = slice(c * 128, (c + 1) * 128)
        for s in range(2):
            rows = slice(s * tokens, (s + 1) * tokens)
            mixed = mixed_ref[c, rows, :].astype(jnp.float32)
            rows_ref[rows, lanes] = (query_ref[s, :, lanes].astype(jnp.float32) * mixed).astype(jnp.bfloat16)


def fetch(sources, index, held, sem):
    for place, source in enumerate(sources):

        @pl.when(index == place)
        def _():
            pltpu.make_async_copy(source, held, sem).start()


def arrived(sources, held, sem):
    pltpu.make_async_copy(sources[0], held, sem).wait()


def place_of(sel_ref, pair, mine):
    kept = jnp.where(pair == 0, sel_ref[0], sel_ref[1])
    return 2 * pair + (kept if mine else 1 - kept)


def half_products(sel_ref, rows_s, sources, give_ref, keep_ref, held, give_s, keep_s, sems, before):
    home, away = sel_ref[2], 1 - sel_ref[2]
    for i, (pair, mine) in enumerate(((away, False), (home, False), (away, True))):
        fetch(sources, place_of(sel_ref, pair, mine), held.at[i], sems.at[i])
    before()
    copies = []
    for i in range(3):
        arrived(sources, held.at[i], sems.at[i])
        part = jnp.dot(rows_s[...], held[i], preferred_element_type=jnp.float32)
        if i < 2:
            give_s[i] = part.astype(jnp.bfloat16)
            copy = pltpu.make_async_copy(give_s.at[i], give_ref.at[i], sems.at[3 + i])
        else:
            keep_s[...] = part
            copy = pltpu.make_async_copy(keep_s, keep_ref, sems.at[5])
        copy.start()
        copies.append(copy)
    for copy in copies:
        copy.wait()


def line_kernel(sel_ref, query_ref, mixed_ref, *refs):
    sources, (rows_ref, give_ref, keep_ref) = refs[:4], refs[4:7]
    held, give_s, keep_s, rows_s, sems, query_s, mixed_s = refs[7:]
    query_in = pltpu.make_async_copy(query_ref, query_s, sems.at[6])
    mixed_in = pltpu.make_async_copy(mixed_ref, mixed_s, sems.at[7])
    rows_out = pltpu.make_async_copy(rows_s, rows_ref, sems.at[8])
    mixed_in.start()
    query_in.start()

    def before():
        mixed_in.wait()
        query_in.wait()
        gate_rows(query_s, mixed_s, rows_s)
        rows_out.start()

    half_products(sel_ref, rows_s, sources, give_ref, keep_ref, held, give_s, keep_s, sems, before)
    rows_out.wait()


def across_kernel(sel_ref, rows_ref, *refs):
    sources, (give_ref, keep_ref) = refs[:4], refs[4:6]
    held, give_s, keep_s, rows_s, sems = refs[6:]
    rows_in = pltpu.make_async_copy(rows_ref, rows_s, sems.at[6])
    rows_in.start()
    half_products(sel_ref, rows_s, sources, give_ref, keep_ref, held, give_s, keep_s, sems, rows_in.wait)


def dots_into(rows_ref, sources, wanted, held, sems, store):
    for i, (side, place) in enumerate(wanted):
        fetch(sources[4 * side : 4 * side + 4], place, held.at[i], sems.at[i])
    for i in range(len(wanted)):
        arrived(sources, held.at[i], sems.at[i])
        store(i, jnp.dot(rows_ref[...], held[i], preferred_element_type=jnp.float32))


def put_half(x_ref, same, block, out_ref, sem):
    width = block.shape[1]
    for place in range(2):

        @pl.when((x_ref[0] == same) == (place == 0))
        def _():
            copy = pltpu.make_async_copy(block, out_ref.at[:, place * width : (place + 1) * width], sem)
            copy.start()
            copy.wait()


def home_kernel(sel_ref, x_ref, rows_ref, given_ref, given_x_ref, here_ref, *refs):
    sources, (out_ref, part_ref, held, block, sems) = refs[:8], refs[8:]
    wanted = [(side, place_of(sel_ref, sel_ref[2], True)) for side in (0, 1)]

    def store(i, part):
        if i == 0:
            total = part + given_ref[1].astype(jnp.float32) + here_ref[...].astype(jnp.float32)
            block[...] = total.astype(jnp.bfloat16)
        else:
            part_ref[...] = part + given_x_ref[1].astype(jnp.float32)

    dots_into(rows_ref, sources, wanted, held, sems, store)
    put_half(x_ref, 0, block, out_ref, sems.at[2])


def home_products(sel, x, rows, given, given_x, here, weights):
    count, (depth, width) = rows.shape[0], weights[0].shape
    anywhere = pl.BlockSpec(memory_space=pl.ANY)
    return pl.pallas_call(
        home_kernel,
        out_shape=(
            jax.ShapeDtypeStruct((count, 2 * width), jnp.bfloat16),
            jax.ShapeDtypeStruct((count, width), jnp.float32),
        ),
        in_specs=[SMEM, SMEM] + [VMEM] * 4 + [anywhere] * 8,
        out_specs=(anywhere, VMEM),
        scratch_shapes=[
            pltpu.VMEM((2, depth, width), jnp.bfloat16),
            pltpu.VMEM((count, width), jnp.bfloat16),
            pltpu.SemaphoreType.DMA((3,)),
        ],
        compiler_params=pltpu.CompilerParams(vmem_limit_bytes=56 << 20),
        cost_estimate=pl.CostEstimate(
            flops=4 * count * depth * width, bytes_accessed=8 << 20, transcendentals=0
        ),
        name="products",
    )(sel, x, rows, given, given_x, here, *weights)


def finish_kernel(x_ref, part_ref, there_ref, so_far_ref, out_ref, block, sem):
    del so_far_ref
    block[...] = (part_ref[...] + there_ref[...].astype(jnp.float32)).astype(jnp.bfloat16)
    put_half(x_ref, 1, block, out_ref, sem)


def finish(x, part, there, so_far):
    anywhere = pl.BlockSpec(memory_space=pl.ANY)
    return pl.pallas_call(
        finish_kernel,
        out_shape=jax.ShapeDtypeStruct(so_far.shape, so_far.dtype),
        in_specs=[SMEM, VMEM, VMEM, anywhere],
        out_specs=anywhere,
        scratch_shapes=[pltpu.VMEM(there.shape, jnp.bfloat16), pltpu.SemaphoreType.DMA],
        input_output_aliases={3: 0},
        compiler_params=pltpu.CompilerParams(vmem_limit_bytes=16 << 20),
        name="finish",
    )(x, part, there, so_far)


def half_call(kernel, outs, sel, left, weights, scratch=()):
    rows, (depth, width) = outs[-1].shape[-2], weights[0].shape
    anywhere = pl.BlockSpec(memory_space=pl.ANY)
    return pl.pallas_call(
        kernel,
        out_shape=outs,
        in_specs=[SMEM] + [anywhere] * (len(left) + len(weights)),
        out_specs=(anywhere,) * len(outs),
        scratch_shapes=[
            pltpu.VMEM((3, depth, width), jnp.bfloat16),
            pltpu.VMEM((2, rows, width), jnp.bfloat16),
            pltpu.VMEM((rows, width), jnp.float32),
            pltpu.VMEM((rows, depth), jnp.bfloat16),
            pltpu.SemaphoreType.DMA((9,)),
            *scratch,
        ],
        compiler_params=pltpu.CompilerParams(vmem_limit_bytes=20 << 20),
        cost_estimate=pl.CostEstimate(
            flops=6 * rows * depth * width, bytes_accessed=8 << 20, transcendentals=0
        ),
        name="products",
    )(sel, *left, *weights)


def per_device_mesh(
    query_proj,
    key_proj,
    value_proj,
    filter_taps,
    skip_gain,
    out_weight,
    drop_seed,
    drop_step,
    offsets,
):
    group_width = query_proj.shape[2]
    ctx, ch = lax.axis_index("ctx"), lax.axis_index("ch")
    z, x, y, core = ctx // 2, ctx % 2, ch // 2, ch % 2

    def along_z(value, pairs):
        return lax.ppermute(value, "ctx", [(2 * a + k, 2 * b + k) for a, b in pairs for k in (0, 1)])

    def across_x(value):
        return lax.ppermute(value, "ctx", [(i, i ^ 1) for i in range(8)])

    def to_sibling(value):
        return lax.ppermute(value, "ch", [(j, j ^ 1) for j in range(4)])

    def across_y(value):
        return lax.ppermute(value, "ch", [(j, j ^ 2) for j in range(4)])

    own = out_weight
    near = along_z(own, [(0, 1), (1, 0), (2, 3), (3, 2)])
    middle = along_z(own, [(1, 2), (2, 1)])
    seed_word = mix_bits(drop_seed[0] * jnp.int32(-1640531535) + drop_step[0])
    words = jnp.stack([seed_word, ch * group_width])
    packed = gate_and_pack(words, offsets, key_proj, value_proj, filter_taps)
    got = lax.all_to_all(packed, "ctx", split_axis=0, concat_axis=0, tiled=True)
    own, packed = lax.optimization_barrier((own, packed))
    own_x = across_x(own)

    near, small = lax.optimization_barrier((near, small_waves()))
    far_mid = along_z(near, [(2, 1), (1, 2)])
    tabs = tables(small)
    middle, tabs = lax.optimization_barrier((middle, tabs))
    far_ends = along_z(middle, [(1, 0), (2, 3)])
    near, own_x, tabs = lax.optimization_barrier((near, own_x, tabs))
    near_x = across_x(near)
    inner = (z == 1) | (z == 2)
    third = jnp.where(inner, middle, far_ends)
    got, third, far_mid, tabs = lax.optimization_barrier((got, third, far_mid, tabs))
    three_ends = along_z(far_mid, [(1, 0), (2, 3)])
    third, near_x = lax.optimization_barrier((third, near_x))
    third_x = across_x(third)
    skip_local = lax.dynamic_slice_in_dim(skip_gain, ctx * 128, 128)
    mixed = conv(got, skip_local[None, :], tabs)
    back = lax.all_to_all(mixed, "ctx", split_axis=0, concat_axis=0, tiled=True)
    three_ends, third_x, mixed = lax.optimization_barrier((three_ends, third_x, mixed))
    fourth = jnp.where(inner, far_mid, three_ends)
    fourth_x = across_x(fourth)

    near_kept = (z + core) % 2
    sel = jnp.stack([near_kept, (near_kept + inner) % 2, (z // 2 + y) % 2]).astype(jnp.int32)
    line, line_x = (own, near, third, fourth), (own_x, near_x, third_x, fourth_x)
    row_count, half_width = 2 * query_proj.shape[1], own.shape[1]

    def out(dtype, *lead):
        return jax.ShapeDtypeStruct(lead + (row_count, half_width), dtype)

    outs = (out(jnp.bfloat16, 2), out(jnp.float32))
    rows_type = jax.ShapeDtypeStruct((row_count, group_width), jnp.bfloat16)
    scratch = (pltpu.VMEM(query_proj.shape, jnp.bfloat16), pltpu.VMEM(back.shape, jnp.bfloat16))
    rows, give, keep = half_call(line_kernel, (rows_type,) + outs, sel, (query_proj, back), line, scratch)
    given = to_sibling(give)
    here = across_y((keep + given[0].astype(jnp.float32)).astype(jnp.bfloat16))
    give, keep = half_call(across_kernel, outs, sel, (rows,), line_x)
    given_x = to_sibling(give)
    there = across_y((keep + given_x[0].astype(jnp.float32)).astype(jnp.bfloat16))
    x_word = x.astype(jnp.int32)[None]
    so_far, part = home_products(sel, x_word, rows, given, given_x, here, line + line_x)
    return finish(x_word, part, there, so_far).reshape(query_proj.shape)


def solution(mesh):
    sizes = dict(mesh.shape)

    def per_device(query_proj, *rest):
        width = query_proj.shape[2]
        length = query_proj.shape[1] * sizes["ctx"]
        fits = sizes["ctx"] == 8 and sizes["ch"] == 4 and width == 1024 and length == 2048
        return (per_device_mesh if fits else per_device_plain)(query_proj, *rest)

    return jax.shard_map(
        per_device,
        mesh=mesh,
        in_specs=(
            P(None, "ctx", "ch"),
            P(None, "ctx", "ch"),
            P(None, "ctx", "ch"),
            P("ctx", "ch"),
            P("ch"),
            P("ch", "ctx"),
            P(),
            P(),
            P(None, "ctx"),
        ),
        out_specs=P(None, "ctx", "ch"),
        check_vma=False,
    )
```

```python
import functools
import math

import jax
import jax.numpy as jnp
from jax import lax
from jax.experimental import pallas as pl
from jax.experimental.pallas import tpu as pltpu
from jax.sharding import PartitionSpec as P

drop_level = 6554
keep_scale = 65536.0 / (65536.0 - 6554.0)


def mix_bits(hashed):
    hashed = hashed ^ lax.shift_right_logical(hashed, jnp.full_like(hashed, 16))
    hashed = hashed * jnp.int32(73244475)
    hashed = hashed ^ lax.shift_right_logical(hashed, jnp.full_like(hashed, 16))
    hashed = hashed * jnp.int32(73244475)
    hashed = hashed ^ lax.shift_right_logical(hashed, jnp.full_like(hashed, 16))
    return hashed


def keep_mask(drop_seed, drop_step, positions, channel_ids):
    seed_word = mix_bits(drop_seed[0] * jnp.int32(-1640531535) + drop_step[0])
    hashed = mix_bits(seed_word ^ mix_bits(positions))
    hashed = mix_bits(hashed ^ channel_ids * jnp.int32(668265263))
    low_bits = lax.shift_right_logical(hashed, jnp.full_like(hashed, 8)) & 65535
    return low_bits >= drop_level


def phase_table(count_rows, count_cols, period, direction):
    product = (
        jnp.arange(count_rows, dtype=jnp.int32)[:, None]
        * jnp.arange(count_cols, dtype=jnp.int32)[None, :]
        % period
    )
    angles = direction * 2.0 * math.pi * product.astype(jnp.float32) / period
    return (jnp.cos(angles), jnp.sin(angles))


def einsum_high(formula, left_part, right_part):
    return jnp.einsum(formula, left_part, right_part, precision=lax.Precision.HIGHEST)


def complex_einsum(formula, left_pair, right_pair):
    left_real, left_imag = left_pair
    right_real, right_imag = right_pair
    real_part = einsum_high(formula, left_real, right_real)
    imag_part = None
    if left_imag is not None and right_imag is not None:
        real_part = real_part - einsum_high(formula, left_imag, right_imag)
    if right_imag is not None:
        imag_part = einsum_high(formula, left_real, right_imag)
    cross_term = einsum_high(formula, left_imag, right_real)
    imag_part = cross_term if imag_part is None else imag_part + cross_term
    return (real_part, imag_part)


def complex_product(first_pair, second_pair):
    return (
        first_pair[0] * second_pair[0] - first_pair[1] * second_pair[1],
        first_pair[0] * second_pair[1] + first_pair[1] * second_pair[0],
    )


def grid_shape(length):
    columns = min(256, length)
    period = 2 * length
    return (columns, period // columns, period)


def forward_spectrum(signal_pair, length):
    columns, rows_all, period = grid_shape(length)
    half_rows = rows_all // 2
    shaped = tuple(
        (
            (
                None
                if part_item is None
                else part_item.reshape(part_item.shape[0], half_rows, columns, part_item.shape[2])
            )
            for part_item in signal_pair
        )
    )
    sectioned = complex_einsum(
        "kr,nrcd->ndkc", phase_table(rows_all, half_rows, rows_all, -1.0), shaped
    )
    sectioned = complex_product(sectioned, phase_table(rows_all, columns, period, -1.0))
    return complex_einsum("ndkc,cj->ndkj", sectioned, phase_table(columns, columns, columns, -1.0))


def inverse_signal(spectrum, length):
    columns, rows_all, period = grid_shape(length)
    half_rows = rows_all // 2
    sectioned = complex_einsum(
        "ndkj,jc->ndkc", spectrum, phase_table(columns, columns, columns, 1.0)
    )
    sectioned = complex_product(sectioned, phase_table(rows_all, columns, period, 1.0))
    last_table = phase_table(half_rows, rows_all, rows_all, 1.0)
    real_part = einsum_high("rk,ndkc->nrcd", last_table[0], sectioned[0]) - einsum_high(
        "rk,ndkc->nrcd", last_table[1], sectioned[1]
    )
    pieces_out = (real_part,)
    return tuple(
        (
            item_part.reshape(item_part.shape[0], length, item_part.shape[3]) / period
            for item_part in pieces_out
        )
    )


def convolve_plain(signal, filter_spec):
    length = signal.shape[1]
    spectrum = forward_spectrum((signal, None), length)
    product = complex_product(spectrum, filter_spec)
    return inverse_signal(product, length)[0]


def per_device_plain(
    query_proj,
    key_proj,
    value_proj,
    filter_taps,
    skip_gain,
    out_weight,
    drop_seed,
    drop_step,
    offsets,
):
    group_width = query_proj.shape[2]
    channel_ids = lax.axis_index("ch") * group_width + jnp.arange(group_width, dtype=jnp.int32)
    keep_flags = keep_mask(drop_seed, drop_step, offsets[:, :, None], channel_ids[None, None, :])
    gated = (
        key_proj.astype(jnp.float32)
        * value_proj.astype(jnp.float32)
        * jnp.where(keep_flags, keep_scale, 0.0)
    ).astype(jnp.bfloat16)
    tap_cols = lax.all_to_all(filter_taps, "ctx", split_axis=1, concat_axis=0, tiled=True)
    local_width = tap_cols.shape[1]
    skip_local = lax.dynamic_slice_in_dim(
        skip_gain, lax.axis_index("ctx") * local_width, local_width
    )
    filter_spec = forward_spectrum((tap_cols[None], None), tap_cols.shape[0])
    signal = lax.all_to_all(gated, "ctx", split_axis=2, concat_axis=1, tiled=True).astype(
        jnp.float32
    )
    convolved = convolve_plain(signal, filter_spec)
    mixed_cols = (convolved + skip_local * signal).astype(jnp.bfloat16)
    mixed = lax.all_to_all(mixed_cols, "ctx", split_axis=1, concat_axis=2, tiled=True)
    gate_out = (query_proj.astype(jnp.float32) * mixed.astype(jnp.float32)).astype(jnp.bfloat16)
    flat_rows = gate_out.reshape(-1, group_width)
    partial_value = jnp.dot(
        flat_rows,
        lax.all_gather(out_weight, "ctx", axis=1, tiled=True),
        preferred_element_type=jnp.float32,
    )
    summed = lax.psum_scatter(partial_value, "ch", scatter_dimension=1, tiled=True)
    return summed.astype(jnp.bfloat16).reshape(query_proj.shape)


SIDE = 64
WIDE = 2 * SIDE + 8
NARROW = SIDE + 8


def numbers(shape):
    return tuple(lax.broadcasted_iota(jnp.int32, shape, axis) for axis in range(len(shape)))


def waves(steps):
    angle = (steps % (SIDE * SIDE)).astype(jnp.float32) * (2.0 * math.pi / (SIDE * SIDE))
    return jnp.cos(angle), jnp.sin(angle)


def turn(row_part, col_part, sign):
    return (row_part - col_part) * (sign * SIDE * SIDE // 4)


def high_low(value, low):
    high = lax.reduce_precision(value, 8, 7)
    return jnp.where(low, value - high, high).astype(jnp.bfloat16)


def small_waves():
    half = SIDE // 2
    row, col = numbers((2 * SIDE, 4 * half))
    first = waves(SIDE * (col % half) * (row % SIDE) + turn(row // SIDE, col // half % 2, 1))
    n2, row = numbers((SIDE, 2 * SIDE))
    first_shift = waves(n2 * (row % SIDE))
    row, col = numbers((2 * SIDE, 4 * SIDE))
    steps = SIDE * (row % SIDE) * (col % SIDE)
    second = waves(steps + turn(row // SIDE, col // SIDE % 2, 1))[0]
    third = waves(steps + turn(row // SIDE, col // SIDE % 2, -1))[0]
    row, col = numbers((2 * half, 4 * SIDE))
    last = waves(SIDE * (row % half) * (col % SIDE) + turn(row // half, col // SIDE % 2, -1))
    n2, col = numbers((SIDE, 4 * SIDE))
    last_shift = waves(n2 * (col % SIDE))
    return first, first_shift, second, third, last, last_shift


def tables(small):
    first, first_shift, second, third, last, last_shift = small
    value = first[0][None] * first_shift[0][:, :, None] - first[1][None] * first_shift[1][:, :, None]
    first_table = high_low(value, numbers(value.shape)[2] >= SIDE)
    value = last[0][None] * last_shift[0][:, None, :] - last[1][None] * last_shift[1][:, None, :]
    last_table = high_low(value, numbers(value.shape)[2] >= 2 * SIDE)
    low = numbers(second.shape)[1] >= 2 * SIDE
    return first_table, high_low(second, low), high_low(third, low), last_table


def conv_kernel(
    got_ref, skip_ref, source_ref, second_ref, third_ref, last_ref, out_ref,
    sig_s, tap_s, mids_s, midt_s, back_s, res_s, first_ref, sem, *, blocks, tokens
):
    half = SIDE // 2
    copy = pltpu.make_async_copy(source_ref, first_ref, sem)
    copy.start()
    parts = tokens // SIDE
    for d in range(blocks):
        for a in range(parts):
            n1 = d * parts + a
            for s in range(3):
                ref, row = (tap_s, n1) if s == 2 else (sig_s, s * half + n1)
                begin = s * tokens + a * SIDE
                ref[row * NARROW : row * NARROW + SIDE, :] = got_ref[d, begin : begin + SIDE, :].astype(jnp.float32)
    zero = jnp.zeros((half, 128), jnp.float32)
    copy.wait()

    def stage_first(i, carry):
        for u in range(16):
            n2 = i * 16 + u
            sig = sig_s[pl.ds(n2, 2 * half, stride=NARROW), :]
            tap = jnp.concatenate([tap_s[pl.ds(n2, half, stride=NARROW), :], zero], axis=0)
            right = jnp.concatenate([sig, tap], axis=1).astype(jnp.bfloat16)
            right = jnp.concatenate([right, right], axis=0)
            spec = jnp.dot(first_ref[n2], right, preferred_element_type=jnp.float32)
            rows = pl.ds(pl.multiple_of(n2 * WIDE, 8), 2 * SIDE)
            mids_s[rows, :] = spec[:, :128]
            midt_s[rows, :] = spec[:, 128:]
        return carry

    lax.fori_loop(0, SIDE // 16, stage_first, 0)
    skip = skip_ref[...]
    scale = 1.0 / (SIDE * SIDE)

    def column(ref, k):
        real = ref[pl.ds(k, SIDE, stride=WIDE), :]
        return jnp.concatenate([real, ref[pl.ds(SIDE + k, SIDE, stride=WIDE), :]], axis=0)

    def stage_spectrum(i, carry):
        for v in range(4):
            products = []
            for u in range(2):
                k1 = i * 8 + v * 2 + u
                right = jnp.concatenate([column(mids_s, k1), column(midt_s, k1)], axis=1).astype(jnp.bfloat16)
                right = jnp.concatenate([right, right], axis=0)
                spec = jnp.dot(second_ref[...], right, preferred_element_type=jnp.float32)
                sig_r, sig_i = spec[:SIDE, :128], spec[SIDE:, :128]
                tap_r, tap_i = (spec[:SIDE, 128:] + skip) * scale, spec[SIDE:, 128:] * scale
                pair = [sig_r * tap_r - sig_i * tap_i, sig_r * tap_i + sig_i * tap_r]
                products.append(jnp.concatenate(pair, axis=0).astype(jnp.bfloat16))
            right = jnp.concatenate(products, axis=1)
            right = jnp.concatenate([right, right], axis=0)
            back = jnp.dot(third_ref[...], right, preferred_element_type=jnp.float32)
            for u in range(2):
                k1 = i * 8 + v * 2 + u
                back_s[pl.ds(pl.multiple_of(k1 * WIDE, 8), 2 * SIDE), :] = back[:, u * 128 : (u + 1) * 128]
        return carry

    lax.fori_loop(0, SIDE // 8, stage_spectrum, 0)

    def stage_last(i, carry):
        for u in range(16):
            n2 = i * 16 + u
            right = column(back_s, n2).astype(jnp.bfloat16)
            right = jnp.concatenate([right, right], axis=0)
            res_s[pl.ds(n2, 2 * half, stride=NARROW), :] = jnp.dot(
                last_ref[n2], right, preferred_element_type=jnp.float32
            )
        return carry

    lax.fori_loop(0, SIDE // 16, stage_last, 0)
    for d in range(blocks):
        for a in range(parts):
            for s in range(2):
                row = (s * half + d * parts + a) * NARROW
                begin = s * tokens + a * SIDE
                out_ref[d, begin : begin + SIDE, :] = res_s[row : row + SIDE, :].astype(jnp.bfloat16)


def conv(got, skip, tabs):
    blocks, rows, lanes = got.shape
    tokens = rows // 3
    full = pl.BlockSpec(memory_space=pltpu.VMEM)
    return pl.pallas_call(
        functools.partial(conv_kernel, blocks=blocks, tokens=tokens),
        out_shape=jax.ShapeDtypeStruct((blocks, 2 * tokens, lanes), jnp.bfloat16),
        in_specs=[full] * 2 + [pl.BlockSpec(memory_space=pl.ANY)] + [full] * 3,
        out_specs=full,
        scratch_shapes=[
            pltpu.VMEM((SIDE * NARROW + SIDE, lanes), jnp.float32),
            pltpu.VMEM((SIDE // 2 * NARROW + SIDE, lanes), jnp.float32),
            pltpu.VMEM((SIDE * WIDE + 2 * SIDE, lanes), jnp.float32),
            pltpu.VMEM((SIDE * WIDE + 2 * SIDE, lanes), jnp.float32),
            pltpu.VMEM((SIDE * WIDE + 2 * SIDE, lanes), jnp.float32),
            pltpu.VMEM((SIDE * NARROW + SIDE, lanes), jnp.float32),
            pltpu.VMEM(tabs[0].shape, jnp.bfloat16),
            pltpu.SemaphoreType.DMA,
        ],
        compiler_params=pltpu.CompilerParams(vmem_limit_bytes=32 << 20),
        cost_estimate=pl.CostEstimate(flops=1_000_000_000, bytes_accessed=1 << 20, transcendentals=0),
        name="long_conv",
    )(got, skip, *tabs)


VMEM = pl.BlockSpec(memory_space=pltpu.VMEM)
SMEM = pl.BlockSpec(memory_space=pltpu.SMEM)


def gate_kernel(word_ref, off_ref, key_ref, value_ref, taps_ref, out_ref, tok_s):
    tokens = off_ref.shape[1]
    block = pl.program_id(0)

    @pl.when(block == 0)
    def _():
        for s in range(2):
            row = mix_bits(off_ref[s : s + 1, :])
            row = mix_bits(row ^ word_ref[0])
            tok_s[s * tokens : (s + 1) * tokens, :] = jnp.broadcast_to(row, (128, tokens)).T

    count = out_ref.shape[0]
    for c in range(count):
        lanes = slice(c * 128, (c + 1) * 128)
        channel = word_ref[1] + (block * count + c) * 128 + lax.broadcasted_iota(jnp.int32, (1, 128), 1)
        channel = channel * jnp.int32(668265263)
        for s in range(2):
            rows = slice(s * tokens, (s + 1) * tokens)
            hashed = mix_bits(tok_s[rows, :] ^ channel)
            low_bits = lax.shift_right_logical(hashed, jnp.full_like(hashed, 8)) & 65535
            keep = jnp.where(low_bits >= drop_level, jnp.float32(keep_scale), jnp.float32(0.0))
            product = key_ref[s, :, lanes].astype(jnp.float32) * value_ref[s, :, lanes].astype(jnp.float32)
            out_ref[c, rows, :] = (product * keep).astype(jnp.bfloat16)
        out_ref[c, 2 * tokens : 3 * tokens, :] = taps_ref[:, lanes].astype(jnp.bfloat16)


def gate_and_pack(words, offsets, key_proj, value_proj, taps):
    _, tokens, width = key_proj.shape
    blocks = width // 128
    count = 4
    part = pl.BlockSpec((2, tokens, count * 128), lambda d: (0, 0, d))
    return pl.pallas_call(
        gate_kernel,
        grid=(blocks // count,),
        out_shape=jax.ShapeDtypeStruct((blocks, 3 * tokens, 128), jnp.bfloat16),
        in_specs=[
            SMEM,
            pl.BlockSpec((2, tokens), lambda d: (0, 0)),
            part,
            part,
            pl.BlockSpec((tokens, count * 128), lambda d: (0, d)),
        ],
        out_specs=pl.BlockSpec((count, 3 * tokens, 128), lambda d: (d, 0, 0)),
        scratch_shapes=[pltpu.VMEM((2 * tokens, 128), jnp.int32)],
        name="gate_and_pack",
    )(words, offsets, key_proj, value_proj, taps)


def gate_rows(query_ref, mixed_ref, rows_ref):
    tokens = query_ref.shape[1]
    for c in range(mixed_ref.shape[0]):
        lanes = slice(c * 128, (c + 1) * 128)
        for s in range(2):
            rows = slice(s * tokens, (s + 1) * tokens)
            mixed = mixed_ref[c, rows, :].astype(jnp.float32)
            rows_ref[rows, lanes] = (query_ref[s, :, lanes].astype(jnp.float32) * mixed).astype(jnp.bfloat16)


def fetch(sources, index, held, sem):
    for place, source in enumerate(sources):

        @pl.when(index == place)
        def _():
            pltpu.make_async_copy(source, held, sem).start()


def arrived(sources, held, sem):
    pltpu.make_async_copy(sources[0], held, sem).wait()


def place_of(sel_ref, pair, mine):
    kept = jnp.where(pair == 0, sel_ref[0], sel_ref[1])
    return 2 * pair + (kept if mine else 1 - kept)


def half_products(sel_ref, rows_s, sources, give_ref, keep_ref, held, give_s, keep_s, sems, before):
    home, away = sel_ref[2], 1 - sel_ref[2]
    for i, (pair, mine) in enumerate(((away, False), (home, False), (away, True))):
        fetch(sources, place_of(sel_ref, pair, mine), held.at[i], sems.at[i])
    before()
    copies = []
    for i in range(3):
        arrived(sources, held.at[i], sems.at[i])
        part = jnp.dot(rows_s[...], held[i], preferred_element_type=jnp.float32)
        if i < 2:
            give_s[i] = part.astype(jnp.bfloat16)
            copy = pltpu.make_async_copy(give_s.at[i], give_ref.at[i], sems.at[3 + i])
        else:
            keep_s[...] = part
            copy = pltpu.make_async_copy(keep_s, keep_ref, sems.at[5])
        copy.start()
        copies.append(copy)
    for copy in copies:
        copy.wait()


def line_kernel(sel_ref, query_ref, mixed_ref, *refs):
    sources, (rows_ref, give_ref, keep_ref) = refs[:4], refs[4:7]
    held, give_s, keep_s, rows_s, sems, query_s, mixed_s = refs[7:]
    query_in = pltpu.make_async_copy(query_ref, query_s, sems.at[6])
    mixed_in = pltpu.make_async_copy(mixed_ref, mixed_s, sems.at[7])
    rows_out = pltpu.make_async_copy(rows_s, rows_ref, sems.at[8])
    mixed_in.start()
    query_in.start()

    def before():
        mixed_in.wait()
        query_in.wait()
        gate_rows(query_s, mixed_s, rows_s)
        rows_out.start()

    half_products(sel_ref, rows_s, sources, give_ref, keep_ref, held, give_s, keep_s, sems, before)
    rows_out.wait()


def across_kernel(sel_ref, rows_ref, *refs):
    sources, (give_ref, keep_ref) = refs[:4], refs[4:6]
    held, give_s, keep_s, rows_s, sems = refs[6:]
    rows_in = pltpu.make_async_copy(rows_ref, rows_s, sems.at[6])
    rows_in.start()
    half_products(sel_ref, rows_s, sources, give_ref, keep_ref, held, give_s, keep_s, sems, rows_in.wait)


def dots_into(rows_ref, sources, wanted, held, sems, store):
    for i, (side, place) in enumerate(wanted):
        fetch(sources[4 * side : 4 * side + 4], place, held.at[i], sems.at[i])
    for i in range(len(wanted)):
        arrived(sources, held.at[i], sems.at[i])
        store(i, jnp.dot(rows_ref[...], held[i], preferred_element_type=jnp.float32))


def put_half(x_ref, same, block, out_ref, sem):
    width = block.shape[1]
    for place in range(2):

        @pl.when((x_ref[0] == same) == (place == 0))
        def _():
            copy = pltpu.make_async_copy(block, out_ref.at[:, place * width : (place + 1) * width], sem)
            copy.start()
            copy.wait()


def home_kernel(sel_ref, x_ref, rows_ref, given_ref, given_x_ref, here_ref, *refs):
    sources, (out_ref, part_ref, held, block, sems) = refs[:8], refs[8:]
    wanted = [(side, place_of(sel_ref, sel_ref[2], True)) for side in (0, 1)]

    def store(i, part):
        if i == 0:
            total = part + given_ref[1].astype(jnp.float32) + here_ref[...].astype(jnp.float32)
            block[...] = total.astype(jnp.bfloat16)
        else:
            part_ref[...] = part + given_x_ref[1].astype(jnp.float32)

    dots_into(rows_ref, sources, wanted, held, sems, store)
    put_half(x_ref, 0, block, out_ref, sems.at[2])


def home_products(sel, x, rows, given, given_x, here, weights):
    count, (depth, width) = rows.shape[0], weights[0].shape
    anywhere = pl.BlockSpec(memory_space=pl.ANY)
    return pl.pallas_call(
        home_kernel,
        out_shape=(
            jax.ShapeDtypeStruct((count, 2 * width), jnp.bfloat16),
            jax.ShapeDtypeStruct((count, width), jnp.float32),
        ),
        in_specs=[SMEM, SMEM] + [VMEM] * 4 + [anywhere] * 8,
        out_specs=(anywhere, VMEM),
        scratch_shapes=[
            pltpu.VMEM((2, depth, width), jnp.bfloat16),
            pltpu.VMEM((count, width), jnp.bfloat16),
            pltpu.SemaphoreType.DMA((3,)),
        ],
        compiler_params=pltpu.CompilerParams(vmem_limit_bytes=56 << 20),
        cost_estimate=pl.CostEstimate(
            flops=4 * count * depth * width, bytes_accessed=8 << 20, transcendentals=0
        ),
        name="products",
    )(sel, x, rows, given, given_x, here, *weights)


def finish_kernel(x_ref, part_ref, there_ref, so_far_ref, out_ref, block, sem):
    del so_far_ref
    block[...] = (part_ref[...] + there_ref[...].astype(jnp.float32)).astype(jnp.bfloat16)
    put_half(x_ref, 1, block, out_ref, sem)


def finish(x, part, there, so_far):
    anywhere = pl.BlockSpec(memory_space=pl.ANY)
    return pl.pallas_call(
        finish_kernel,
        out_shape=jax.ShapeDtypeStruct(so_far.shape, so_far.dtype),
        in_specs=[SMEM, VMEM, VMEM, anywhere],
        out_specs=anywhere,
        scratch_shapes=[pltpu.VMEM(there.shape, jnp.bfloat16), pltpu.SemaphoreType.DMA],
        input_output_aliases={3: 0},
        compiler_params=pltpu.CompilerParams(vmem_limit_bytes=16 << 20),
        name="finish",
    )(x, part, there, so_far)


def half_call(kernel, outs, sel, left, weights, scratch=()):
    rows, (depth, width) = outs[-1].shape[-2], weights[0].shape
    anywhere = pl.BlockSpec(memory_space=pl.ANY)
    return pl.pallas_call(
        kernel,
        out_shape=outs,
        in_specs=[SMEM] + [anywhere] * (len(left) + len(weights)),
        out_specs=(anywhere,) * len(outs),
        scratch_shapes=[
            pltpu.VMEM((3, depth, width), jnp.bfloat16),
            pltpu.VMEM((2, rows, width), jnp.bfloat16),
            pltpu.VMEM((rows, width), jnp.float32),
            pltpu.VMEM((rows, depth), jnp.bfloat16),
            pltpu.SemaphoreType.DMA((9,)),
            *scratch,
        ],
        compiler_params=pltpu.CompilerParams(vmem_limit_bytes=20 << 20),
        cost_estimate=pl.CostEstimate(
            flops=6 * rows * depth * width, bytes_accessed=8 << 20, transcendentals=0
        ),
        name="products",
    )(sel, *left, *weights)


def per_device_mesh(
    query_proj,
    key_proj,
    value_proj,
    filter_taps,
    skip_gain,
    out_weight,
    drop_seed,
    drop_step,
    offsets,
):
    group_width = query_proj.shape[2]
    ctx, ch = lax.axis_index("ctx"), lax.axis_index("ch")
    z, x, y, core = ctx // 2, ctx % 2, ch // 2, ch % 2

    def along_z(value, pairs):
        return lax.ppermute(value, "ctx", [(2 * a + k, 2 * b + k) for a, b in pairs for k in (0, 1)])

    def across_x(value):
        return lax.ppermute(value, "ctx", [(i, i ^ 1) for i in range(8)])

    def to_sibling(value):
        return lax.ppermute(value, "ch", [(j, j ^ 1) for j in range(4)])

    def across_y(value):
        return lax.ppermute(value, "ch", [(j, j ^ 2) for j in range(4)])

    own = out_weight
    near = along_z(own, [(0, 1), (1, 0), (2, 3), (3, 2)])
    middle = along_z(own, [(1, 2), (2, 1)])
    seed_word = mix_bits(drop_seed[0] * jnp.int32(-1640531535) + drop_step[0])
    words = jnp.stack([seed_word, ch * group_width])
    packed = gate_and_pack(words, offsets, key_proj, value_proj, filter_taps)
    got = lax.all_to_all(packed, "ctx", split_axis=0, concat_axis=0, tiled=True)
    own, packed = lax.optimization_barrier((own, packed))
    own_x = across_x(own)

    near, small = lax.optimization_barrier((near, small_waves()))
    far_mid = along_z(near, [(2, 1), (1, 2)])
    tabs = tables(small)
    middle, tabs = lax.optimization_barrier((middle, tabs))
    far_ends = along_z(middle, [(1, 0), (2, 3)])
    near, own_x, tabs = lax.optimization_barrier((near, own_x, tabs))
    near_x = across_x(near)
    inner = (z == 1) | (z == 2)
    third = jnp.where(inner, middle, far_ends)
    got, third, far_mid, tabs = lax.optimization_barrier((got, third, far_mid, tabs))
    three_ends = along_z(far_mid, [(1, 0), (2, 3)])
    third, near_x = lax.optimization_barrier((third, near_x))
    third_x = across_x(third)
    skip_local = lax.dynamic_slice_in_dim(skip_gain, ctx * 128, 128)
    mixed = conv(got, skip_local[None, :], tabs)
    back = lax.all_to_all(mixed, "ctx", split_axis=0, concat_axis=0, tiled=True)
    three_ends, third_x, mixed = lax.optimization_barrier((three_ends, third_x, mixed))
    fourth = jnp.where(inner, far_mid, three_ends)
    fourth_x = across_x(fourth)

    near_kept = (z + core) % 2
    sel = jnp.stack([near_kept, (near_kept + inner) % 2, (z // 2 + y) % 2]).astype(jnp.int32)
    line, line_x = (own, near, third, fourth), (own_x, near_x, third_x, fourth_x)
    row_count, half_width = 2 * query_proj.shape[1], own.shape[1]

    def out(dtype, *lead):
        return jax.ShapeDtypeStruct(lead + (row_count, half_width), dtype)

    outs = (out(jnp.bfloat16, 2), out(jnp.float32))
    rows_type = jax.ShapeDtypeStruct((row_count, group_width), jnp.bfloat16)
    scratch = (pltpu.VMEM(query_proj.shape, jnp.bfloat16), pltpu.VMEM(back.shape, jnp.bfloat16))
    rows, give, keep = half_call(line_kernel, (rows_type,) + outs, sel, (query_proj, back), line, scratch)
    given = to_sibling(give)
    here = across_y((keep + given[0].astype(jnp.float32)).astype(jnp.bfloat16))
    give, keep = half_call(across_kernel, outs, sel, (rows,), line_x)
    given_x = to_sibling(give)
    there = across_y((keep + given_x[0].astype(jnp.float32)).astype(jnp.bfloat16))
    x_word = x.astype(jnp.int32)[None]
    so_far, part = home_products(sel, x_word, rows, given, given_x, here, line + line_x)
    return finish(x_word, part, there, so_far).reshape(query_proj.shape)


def solution(mesh):
    sizes = dict(mesh.shape)

    def per_device(query_proj, *rest):
        width = query_proj.shape[2]
        length = query_proj.shape[1] * sizes["ctx"]
        fits = sizes["ctx"] == 8 and sizes["ch"] == 4 and width == 1024 and length == 2048
        return (per_device_mesh if fits else per_device_plain)(query_proj, *rest)

    return jax.shard_map(
        per_device,
        mesh=mesh,
        in_specs=(
            P(None, "ctx", "ch"),
            P(None, "ctx", "ch"),
            P(None, "ctx", "ch"),
            P("ctx", "ch"),
            P("ch"),
            P("ch", "ctx"),
            P(),
            P(),
            P(None, "ctx"),
        ),
        out_specs=P(None, "ctx", "ch"),
        check_vma=False,
    )
```

```python
import functools
import math

import jax
import jax.numpy as jnp
from jax import lax
from jax.experimental import pallas as pl
from jax.experimental.pallas import tpu as pltpu
from jax.sharding import PartitionSpec as P

drop_level = 6554
keep_scale = 65536.0 / (65536.0 - 6554.0)


def mix_bits(hashed):
    hashed = hashed ^ lax.shift_right_logical(hashed, jnp.full_like(hashed, 16))
    hashed = hashed * jnp.int32(73244475)
    hashed = hashed ^ lax.shift_right_logical(hashed, jnp.full_like(hashed, 16))
    hashed = hashed * jnp.int32(73244475)
    hashed = hashed ^ lax.shift_right_logical(hashed, jnp.full_like(hashed, 16))
    return hashed


def keep_mask(drop_seed, drop_step, positions, channel_ids):
    seed_word = mix_bits(drop_seed[0] * jnp.int32(-1640531535) + drop_step[0])
    hashed = mix_bits(seed_word ^ mix_bits(positions))
    hashed = mix_bits(hashed ^ channel_ids * jnp.int32(668265263))
    low_bits = lax.shift_right_logical(hashed, jnp.full_like(hashed, 8)) & 65535
    return low_bits >= drop_level


def phase_table(count_rows, count_cols, period, direction):
    product = (
        jnp.arange(count_rows, dtype=jnp.int32)[:, None]
        * jnp.arange(count_cols, dtype=jnp.int32)[None, :]
        % period
    )
    angles = direction * 2.0 * math.pi * product.astype(jnp.float32) / period
    return (jnp.cos(angles), jnp.sin(angles))


def einsum_high(formula, left_part, right_part):
    return jnp.einsum(formula, left_part, right_part, precision=lax.Precision.HIGHEST)


def complex_einsum(formula, left_pair, right_pair):
    left_real, left_imag = left_pair
    right_real, right_imag = right_pair
    real_part = einsum_high(formula, left_real, right_real)
    imag_part = None
    if left_imag is not None and right_imag is not None:
        real_part = real_part - einsum_high(formula, left_imag, right_imag)
    if right_imag is not None:
        imag_part = einsum_high(formula, left_real, right_imag)
    cross_term = einsum_high(formula, left_imag, right_real)
    imag_part = cross_term if imag_part is None else imag_part + cross_term
    return (real_part, imag_part)


def complex_product(first_pair, second_pair):
    return (
        first_pair[0] * second_pair[0] - first_pair[1] * second_pair[1],
        first_pair[0] * second_pair[1] + first_pair[1] * second_pair[0],
    )


def grid_shape(length):
    columns = min(256, length)
    period = 2 * length
    return (columns, period // columns, period)


def forward_spectrum(signal_pair, length):
    columns, rows_all, period = grid_shape(length)
    half_rows = rows_all // 2
    shaped = tuple(
        (
            (
                None
                if part_item is None
                else part_item.reshape(part_item.shape[0], half_rows, columns, part_item.shape[2])
            )
            for part_item in signal_pair
        )
    )
    sectioned = complex_einsum(
        "kr,nrcd->ndkc", phase_table(rows_all, half_rows, rows_all, -1.0), shaped
    )
    sectioned = complex_product(sectioned, phase_table(rows_all, columns, period, -1.0))
    return complex_einsum("ndkc,cj->ndkj", sectioned, phase_table(columns, columns, columns, -1.0))


def inverse_signal(spectrum, length):
    columns, rows_all, period = grid_shape(length)
    half_rows = rows_all // 2
    sectioned = complex_einsum(
        "ndkj,jc->ndkc", spectrum, phase_table(columns, columns, columns, 1.0)
    )
    sectioned = complex_product(sectioned, phase_table(rows_all, columns, period, 1.0))
    last_table = phase_table(half_rows, rows_all, rows_all, 1.0)
    real_part = einsum_high("rk,ndkc->nrcd", last_table[0], sectioned[0]) - einsum_high(
        "rk,ndkc->nrcd", last_table[1], sectioned[1]
    )
    pieces_out = (real_part,)
    return tuple(
        (
            item_part.reshape(item_part.shape[0], length, item_part.shape[3]) / period
            for item_part in pieces_out
        )
    )


def convolve_plain(signal, filter_spec):
    length = signal.shape[1]
    spectrum = forward_spectrum((signal, None), length)
    product = complex_product(spectrum, filter_spec)
    return inverse_signal(product, length)[0]


def per_device_plain(
    query_proj,
    key_proj,
    value_proj,
    filter_taps,
    skip_gain,
    out_weight,
    drop_seed,
    drop_step,
    offsets,
):
    group_width = query_proj.shape[2]
    channel_ids = lax.axis_index("ch") * group_width + jnp.arange(group_width, dtype=jnp.int32)
    keep_flags = keep_mask(drop_seed, drop_step, offsets[:, :, None], channel_ids[None, None, :])
    gated = (
        key_proj.astype(jnp.float32)
        * value_proj.astype(jnp.float32)
        * jnp.where(keep_flags, keep_scale, 0.0)
    ).astype(jnp.bfloat16)
    tap_cols = lax.all_to_all(filter_taps, "ctx", split_axis=1, concat_axis=0, tiled=True)
    local_width = tap_cols.shape[1]
    skip_local = lax.dynamic_slice_in_dim(
        skip_gain, lax.axis_index("ctx") * local_width, local_width
    )
    filter_spec = forward_spectrum((tap_cols[None], None), tap_cols.shape[0])
    signal = lax.all_to_all(gated, "ctx", split_axis=2, concat_axis=1, tiled=True).astype(
        jnp.float32
    )
    convolved = convolve_plain(signal, filter_spec)
    mixed_cols = (convolved + skip_local * signal).astype(jnp.bfloat16)
    mixed = lax.all_to_all(mixed_cols, "ctx", split_axis=1, concat_axis=2, tiled=True)
    gate_out = (query_proj.astype(jnp.float32) * mixed.astype(jnp.float32)).astype(jnp.bfloat16)
    flat_rows = gate_out.reshape(-1, group_width)
    partial_value = jnp.dot(
        flat_rows,
        lax.all_gather(out_weight, "ctx", axis=1, tiled=True),
        preferred_element_type=jnp.float32,
    )
    summed = lax.psum_scatter(partial_value, "ch", scatter_dimension=1, tiled=True)
    return summed.astype(jnp.bfloat16).reshape(query_proj.shape)


SIDE = 64
WIDE = 2 * SIDE + 8
NARROW = SIDE + 8


def numbers(shape):
    return tuple(lax.broadcasted_iota(jnp.int32, shape, axis) for axis in range(len(shape)))


def waves(steps):
    angle = (steps % (SIDE * SIDE)).astype(jnp.float32) * (2.0 * math.pi / (SIDE * SIDE))
    return jnp.cos(angle), jnp.sin(angle)


def turn(row_part, col_part, sign):
    return (row_part - col_part) * (sign * SIDE * SIDE // 4)


def high_low(value, low):
    high = lax.reduce_precision(value, 8, 7)
    return jnp.where(low, value - high, high).astype(jnp.bfloat16)


def small_waves():
    half = SIDE // 2
    row, col = numbers((2 * SIDE, 4 * half))
    first = waves(SIDE * (col % half) * (row % SIDE) + turn(row // SIDE, col // half % 2, 1))
    n2, row = numbers((SIDE, 2 * SIDE))
    first_shift = waves(n2 * (row % SIDE))
    row, col = numbers((2 * SIDE, 4 * SIDE))
    steps = SIDE * (row % SIDE) * (col % SIDE)
    second = waves(steps + turn(row // SIDE, col // SIDE % 2, 1))[0]
    third = waves(steps + turn(row // SIDE, col // SIDE % 2, -1))[0]
    row, col = numbers((2 * half, 4 * SIDE))
    last = waves(SIDE * (row % half) * (col % SIDE) + turn(row // half, col // SIDE % 2, -1))
    n2, col = numbers((SIDE, 4 * SIDE))
    last_shift = waves(n2 * (col % SIDE))
    return first, first_shift, second, third, last, last_shift


def tables(small):
    first, first_shift, second, third, last, last_shift = small
    value = first[0][None] * first_shift[0][:, :, None] - first[1][None] * first_shift[1][:, :, None]
    first_table = high_low(value, numbers(value.shape)[2] >= SIDE)
    value = last[0][None] * last_shift[0][:, None, :] - last[1][None] * last_shift[1][:, None, :]
    last_table = high_low(value, numbers(value.shape)[2] >= 2 * SIDE)
    low = numbers(second.shape)[1] >= 2 * SIDE
    return first_table, high_low(second, low), high_low(third, low), last_table


def conv_kernel(
    got_ref, skip_ref, source_ref, second_ref, third_ref, last_ref, out_ref,
    sig_s, tap_s, mids_s, midt_s, back_s, res_s, first_ref, sem, *, blocks, tokens
):
    half = SIDE // 2
    copy = pltpu.make_async_copy(source_ref, first_ref, sem)
    copy.start()
    parts = tokens // SIDE
    for d in range(blocks):
        for a in range(parts):
            n1 = d * parts + a
            for s in range(3):
                ref, row = (tap_s, n1) if s == 2 else (sig_s, s * half + n1)
                begin = s * tokens + a * SIDE
                ref[row * NARROW : row * NARROW + SIDE, :] = got_ref[d, begin : begin + SIDE, :].astype(jnp.float32)
    zero = jnp.zeros((half, 128), jnp.float32)
    copy.wait()

    def stage_first(i, carry):
        for u in range(16):
            n2 = i * 16 + u
            sig = sig_s[pl.ds(n2, 2 * half, stride=NARROW), :]
            tap = jnp.concatenate([tap_s[pl.ds(n2, half, stride=NARROW), :], zero], axis=0)
            right = jnp.concatenate([sig, tap], axis=1).astype(jnp.bfloat16)
            right = jnp.concatenate([right, right], axis=0)
            spec = jnp.dot(first_ref[n2], right, preferred_element_type=jnp.float32)
            rows = pl.ds(pl.multiple_of(n2 * WIDE, 8), 2 * SIDE)
            mids_s[rows, :] = spec[:, :128]
            midt_s[rows, :] = spec[:, 128:]
        return carry

    lax.fori_loop(0, SIDE // 16, stage_first, 0)
    skip = skip_ref[...]
    scale = 1.0 / (SIDE * SIDE)

    def column(ref, k):
        real = ref[pl.ds(k, SIDE, stride=WIDE), :]
        return jnp.concatenate([real, ref[pl.ds(SIDE + k, SIDE, stride=WIDE), :]], axis=0)

    def stage_spectrum(i, carry):
        for v in range(4):
            products = []
            for u in range(2):
                k1 = i * 8 + v * 2 + u
                right = jnp.concatenate([column(mids_s, k1), column(midt_s, k1)], axis=1).astype(jnp.bfloat16)
                right = jnp.concatenate([right, right], axis=0)
                spec = jnp.dot(second_ref[...], right, preferred_element_type=jnp.float32)
                sig_r, sig_i = spec[:SIDE, :128], spec[SIDE:, :128]
                tap_r, tap_i = (spec[:SIDE, 128:] + skip) * scale, spec[SIDE:, 128:] * scale
                pair = [sig_r * tap_r - sig_i * tap_i, sig_r * tap_i + sig_i * tap_r]
                products.append(jnp.concatenate(pair, axis=0).astype(jnp.bfloat16))
            right = jnp.concatenate(products, axis=1)
            right = jnp.concatenate([right, right], axis=0)
            back = jnp.dot(third_ref[...], right, preferred_element_type=jnp.float32)
            for u in range(2):
                k1 = i * 8 + v * 2 + u
                back_s[pl.ds(pl.multiple_of(k1 * WIDE, 8), 2 * SIDE), :] = back[:, u * 128 : (u + 1) * 128]
        return carry

    lax.fori_loop(0, SIDE // 8, stage_spectrum, 0)

    def stage_last(i, carry):
        for u in range(16):
            n2 = i * 16 + u
            right = column(back_s, n2).astype(jnp.bfloat16)
            right = jnp.concatenate([right, right], axis=0)
            res_s[pl.ds(n2, 2 * half, stride=NARROW), :] = jnp.dot(
                last_ref[n2], right, preferred_element_type=jnp.float32
            )
        return carry

    lax.fori_loop(0, SIDE // 16, stage_last, 0)
    for d in range(blocks):
        for a in range(parts):
            for s in range(2):
                row = (s * half + d * parts + a) * NARROW
                begin = s * tokens + a * SIDE
                out_ref[d, begin : begin + SIDE, :] = res_s[row : row + SIDE, :].astype(jnp.bfloat16)


def conv(got, skip, tabs):
    blocks, rows, lanes = got.shape
    tokens = rows // 3
    full = pl.BlockSpec(memory_space=pltpu.VMEM)
    return pl.pallas_call(
        functools.partial(conv_kernel, blocks=blocks, tokens=tokens),
        out_shape=jax.ShapeDtypeStruct((blocks, 2 * tokens, lanes), jnp.bfloat16),
        in_specs=[full] * 2 + [pl.BlockSpec(memory_space=pl.ANY)] + [full] * 3,
        out_specs=full,
        scratch_shapes=[
            pltpu.VMEM((SIDE * NARROW + SIDE, lanes), jnp.float32),
            pltpu.VMEM((SIDE // 2 * NARROW + SIDE, lanes), jnp.float32),
            pltpu.VMEM((SIDE * WIDE + 2 * SIDE, lanes), jnp.float32),
            pltpu.VMEM((SIDE * WIDE + 2 * SIDE, lanes), jnp.float32),
            pltpu.VMEM((SIDE * WIDE + 2 * SIDE, lanes), jnp.float32),
            pltpu.VMEM((SIDE * NARROW + SIDE, lanes), jnp.float32),
            pltpu.VMEM(tabs[0].shape, jnp.bfloat16),
            pltpu.SemaphoreType.DMA,
        ],
        compiler_params=pltpu.CompilerParams(vmem_limit_bytes=32 << 20),
        cost_estimate=pl.CostEstimate(flops=1_000_000_000, bytes_accessed=1 << 20, transcendentals=0),
        name="long_conv",
    )(got, skip, *tabs)


VMEM = pl.BlockSpec(memory_space=pltpu.VMEM)
SMEM = pl.BlockSpec(memory_space=pltpu.SMEM)


def gate_kernel(word_ref, off_ref, key_ref, value_ref, taps_ref, out_ref, tok_s):
    tokens = off_ref.shape[1]
    block = pl.program_id(0)

    @pl.when(block == 0)
    def _():
        for s in range(2):
            row = mix_bits(off_ref[s : s + 1, :])
            row = mix_bits(row ^ word_ref[0])
            tok_s[s * tokens : (s + 1) * tokens, :] = jnp.broadcast_to(row, (128, tokens)).T

    count = out_ref.shape[0]
    for c in range(count):
        lanes = slice(c * 128, (c + 1) * 128)
        channel = word_ref[1] + (block * count + c) * 128 + lax.broadcasted_iota(jnp.int32, (1, 128), 1)
        channel = channel * jnp.int32(668265263)
        for s in range(2):
            rows = slice(s * tokens, (s + 1) * tokens)
            hashed = mix_bits(tok_s[rows, :] ^ channel)
            low_bits = lax.shift_right_logical(hashed, jnp.full_like(hashed, 8)) & 65535
            keep = jnp.where(low_bits >= drop_level, jnp.float32(keep_scale), jnp.float32(0.0))
            product = key_ref[s, :, lanes].astype(jnp.float32) * value_ref[s, :, lanes].astype(jnp.float32)
            out_ref[c, rows, :] = (product * keep).astype(jnp.bfloat16)
        out_ref[c, 2 * tokens : 3 * tokens, :] = taps_ref[:, lanes].astype(jnp.bfloat16)


def gate_and_pack(words, offsets, key_proj, value_proj, taps):
    _, tokens, width = key_proj.shape
    blocks = width // 128
    count = 4
    part = pl.BlockSpec((2, tokens, count * 128), lambda d: (0, 0, d))
    return pl.pallas_call(
        gate_kernel,
        grid=(blocks // count,),
        out_shape=jax.ShapeDtypeStruct((blocks, 3 * tokens, 128), jnp.bfloat16),
        in_specs=[
            SMEM,
            pl.BlockSpec((2, tokens), lambda d: (0, 0)),
            part,
            part,
            pl.BlockSpec((tokens, count * 128), lambda d: (0, d)),
        ],
        out_specs=pl.BlockSpec((count, 3 * tokens, 128), lambda d: (d, 0, 0)),
        scratch_shapes=[pltpu.VMEM((2 * tokens, 128), jnp.int32)],
        name="gate_and_pack",
    )(words, offsets, key_proj, value_proj, taps)


def gate_rows(query_ref, mixed_ref, rows_ref):
    tokens = query_ref.shape[1]
    for c in range(mixed_ref.shape[0]):
        lanes = slice(c * 128, (c + 1) * 128)
        for s in range(2):
            rows = slice(s * tokens, (s + 1) * tokens)
            mixed = mixed_ref[c, rows, :].astype(jnp.float32)
            rows_ref[rows, lanes] = (query_ref[s, :, lanes].astype(jnp.float32) * mixed).astype(jnp.bfloat16)


def fetch(sources, index, held, sem):
    for place, source in enumerate(sources):

        @pl.when(index == place)
        def _():
            pltpu.make_async_copy(source, held, sem).start()


def arrived(sources, held, sem):
    pltpu.make_async_copy(sources[0], held, sem).wait()


def place_of(sel_ref, pair, mine):
    kept = jnp.where(pair == 0, sel_ref[0], sel_ref[1])
    return 2 * pair + (kept if mine else 1 - kept)


def half_products(sel_ref, rows_s, sources, give_ref, keep_ref, held, give_s, keep_s, sems, before):
    home, away = sel_ref[2], 1 - sel_ref[2]
    for i, (pair, mine) in enumerate(((away, False), (home, False), (away, True))):
        fetch(sources, place_of(sel_ref, pair, mine), held.at[i], sems.at[i])
    before()
    copies = []
    for i in range(3):
        arrived(sources, held.at[i], sems.at[i])
        part = jnp.dot(rows_s[...], held[i], preferred_element_type=jnp.float32)
        if i < 2:
            give_s[i] = part.astype(jnp.bfloat16)
            copy = pltpu.make_async_copy(give_s.at[i], give_ref.at[i], sems.at[3 + i])
        else:
            keep_s[...] = part
            copy = pltpu.make_async_copy(keep_s, keep_ref, sems.at[5])
        copy.start()
        copies.append(copy)
    for copy in copies:
        copy.wait()


def line_kernel(sel_ref, query_ref, mixed_ref, *refs):
    sources, (rows_ref, give_ref, keep_ref) = refs[:4], refs[4:7]
    held, give_s, keep_s, rows_s, sems, query_s, mixed_s = refs[7:]
    query_in = pltpu.make_async_copy(query_ref, query_s, sems.at[6])
    mixed_in = pltpu.make_async_copy(mixed_ref, mixed_s, sems.at[7])
    rows_out = pltpu.make_async_copy(rows_s, rows_ref, sems.at[8])
    mixed_in.start()
    query_in.start()

    def before():
        mixed_in.wait()
        query_in.wait()
        gate_rows(query_s, mixed_s, rows_s)
        rows_out.start()

    half_products(sel_ref, rows_s, sources, give_ref, keep_ref, held, give_s, keep_s, sems, before)
    rows_out.wait()


def across_kernel(sel_ref, rows_ref, *refs):
    sources, (give_ref, keep_ref) = refs[:4], refs[4:6]
    held, give_s, keep_s, rows_s, sems = refs[6:]
    rows_in = pltpu.make_async_copy(rows_ref, rows_s, sems.at[6])
    rows_in.start()
    half_products(sel_ref, rows_s, sources, give_ref, keep_ref, held, give_s, keep_s, sems, rows_in.wait)


def dots_into(rows_ref, sources, wanted, held, sems, store):
    for i, (side, place) in enumerate(wanted):
        fetch(sources[4 * side : 4 * side + 4], place, held.at[i], sems.at[i])
    for i in range(len(wanted)):
        arrived(sources, held.at[i], sems.at[i])
        store(i, jnp.dot(rows_ref[...], held[i], preferred_element_type=jnp.float32))


def put_half(x_ref, same, block, out_ref, sem):
    width = block.shape[1]
    for place in range(2):

        @pl.when((x_ref[0] == same) == (place == 0))
        def _():
            copy = pltpu.make_async_copy(block, out_ref.at[:, place * width : (place + 1) * width], sem)
            copy.start()
            copy.wait()


def home_kernel(sel_ref, x_ref, rows_ref, given_ref, given_x_ref, here_ref, *refs):
    sources, (out_ref, part_ref, held, block, sems) = refs[:8], refs[8:]
    wanted = [(side, place_of(sel_ref, sel_ref[2], True)) for side in (0, 1)]

    def store(i, part):
        if i == 0:
            total = part + given_ref[1].astype(jnp.float32) + here_ref[...].astype(jnp.float32)
            block[...] = total.astype(jnp.bfloat16)
        else:
            part_ref[...] = part + given_x_ref[1].astype(jnp.float32)

    dots_into(rows_ref, sources, wanted, held, sems, store)
    put_half(x_ref, 0, block, out_ref, sems.at[2])


def home_products(sel, x, rows, given, given_x, here, weights):
    count, (depth, width) = rows.shape[0], weights[0].shape
    anywhere = pl.BlockSpec(memory_space=pl.ANY)
    return pl.pallas_call(
        home_kernel,
        out_shape=(
            jax.ShapeDtypeStruct((count, 2 * width), jnp.bfloat16),
            jax.ShapeDtypeStruct((count, width), jnp.float32),
        ),
        in_specs=[SMEM, SMEM] + [VMEM] * 4 + [anywhere] * 8,
        out_specs=(anywhere, VMEM),
        scratch_shapes=[
            pltpu.VMEM((2, depth, width), jnp.bfloat16),
            pltpu.VMEM((count, width), jnp.bfloat16),
            pltpu.SemaphoreType.DMA((3,)),
        ],
        compiler_params=pltpu.CompilerParams(vmem_limit_bytes=20 << 20),
        cost_estimate=pl.CostEstimate(
            flops=4 * count * depth * width, bytes_accessed=8 << 20, transcendentals=0
        ),
        name="products",
    )(sel, x, rows, given, given_x, here, *weights)


def finish_kernel(x_ref, part_ref, there_ref, so_far_ref, out_ref, block, sem):
    del so_far_ref
    block[...] = (part_ref[...] + there_ref[...].astype(jnp.float32)).astype(jnp.bfloat16)
    put_half(x_ref, 1, block, out_ref, sem)


def finish(x, part, there, so_far):
    anywhere = pl.BlockSpec(memory_space=pl.ANY)
    return pl.pallas_call(
        finish_kernel,
        out_shape=jax.ShapeDtypeStruct(so_far.shape, so_far.dtype),
        in_specs=[SMEM, VMEM, VMEM, anywhere],
        out_specs=anywhere,
        scratch_shapes=[pltpu.VMEM(there.shape, jnp.bfloat16), pltpu.SemaphoreType.DMA],
        input_output_aliases={3: 0},
        compiler_params=pltpu.CompilerParams(vmem_limit_bytes=16 << 20),
        name="finish",
    )(x, part, there, so_far)


def half_call(kernel, outs, sel, left, weights, scratch=()):
    rows, (depth, width) = outs[-1].shape[-2], weights[0].shape
    anywhere = pl.BlockSpec(memory_space=pl.ANY)
    return pl.pallas_call(
        kernel,
        out_shape=outs,
        in_specs=[SMEM] + [anywhere] * (len(left) + len(weights)),
        out_specs=(anywhere,) * len(outs),
        scratch_shapes=[
            pltpu.VMEM((3, depth, width), jnp.bfloat16),
            pltpu.VMEM((2, rows, width), jnp.bfloat16),
            pltpu.VMEM((rows, width), jnp.float32),
            pltpu.VMEM((rows, depth), jnp.bfloat16),
            pltpu.SemaphoreType.DMA((9,)),
            *scratch,
        ],
        compiler_params=pltpu.CompilerParams(vmem_limit_bytes=20 << 20),
        cost_estimate=pl.CostEstimate(
            flops=6 * rows * depth * width, bytes_accessed=8 << 20, transcendentals=0
        ),
        name="products",
    )(sel, *left, *weights)


def per_device_mesh(
    query_proj,
    key_proj,
    value_proj,
    filter_taps,
    skip_gain,
    out_weight,
    drop_seed,
    drop_step,
    offsets,
):
    group_width = query_proj.shape[2]
    ctx, ch = lax.axis_index("ctx"), lax.axis_index("ch")
    z, x, y, core = ctx // 2, ctx % 2, ch // 2, ch % 2

    def along_z(value, pairs):
        return lax.ppermute(value, "ctx", [(2 * a + k, 2 * b + k) for a, b in pairs for k in (0, 1)])

    def across_x(value):
        return lax.ppermute(value, "ctx", [(i, i ^ 1) for i in range(8)])

    def to_sibling(value):
        return lax.ppermute(value, "ch", [(j, j ^ 1) for j in range(4)])

    def across_y(value):
        return lax.ppermute(value, "ch", [(j, j ^ 2) for j in range(4)])

    own = out_weight
    near = along_z(own, [(0, 1), (1, 0), (2, 3), (3, 2)])
    middle = along_z(own, [(1, 2), (2, 1)])
    seed_word = mix_bits(drop_seed[0] * jnp.int32(-1640531535) + drop_step[0])
    words = jnp.stack([seed_word, ch * group_width])
    packed = gate_and_pack(words, offsets, key_proj, value_proj, filter_taps)
    got = lax.all_to_all(packed, "ctx", split_axis=0, concat_axis=0, tiled=True)
    own, packed = lax.optimization_barrier((own, packed))
    own_x = across_x(own)

    near, small = lax.optimization_barrier((near, small_waves()))
    far_mid = along_z(near, [(2, 1), (1, 2)])
    tabs = tables(small)
    middle, tabs = lax.optimization_barrier((middle, tabs))
    far_ends = along_z(middle, [(1, 0), (2, 3)])
    near, own_x, tabs = lax.optimization_barrier((near, own_x, tabs))
    near_x = across_x(near)
    inner = (z == 1) | (z == 2)
    third = jnp.where(inner, middle, far_ends)
    got, third, far_mid, tabs = lax.optimization_barrier((got, third, far_mid, tabs))
    three_ends = along_z(far_mid, [(1, 0), (2, 3)])
    third, near_x = lax.optimization_barrier((third, near_x))
    third_x = across_x(third)
    skip_local = lax.dynamic_slice_in_dim(skip_gain, ctx * 128, 128)
    mixed = conv(got, skip_local[None, :], tabs)
    back = lax.all_to_all(mixed, "ctx", split_axis=0, concat_axis=0, tiled=True)
    three_ends, third_x, mixed = lax.optimization_barrier((three_ends, third_x, mixed))
    fourth = jnp.where(inner, far_mid, three_ends)
    fourth_x = across_x(fourth)

    near_kept = (z + core) % 2
    sel = jnp.stack([near_kept, (near_kept + inner) % 2, (z // 2 + y) % 2]).astype(jnp.int32)
    line, line_x = (own, near, third, fourth), (own_x, near_x, third_x, fourth_x)
    row_count, half_width = 2 * query_proj.shape[1], own.shape[1]

    def out(dtype, *lead):
        return jax.ShapeDtypeStruct(lead + (row_count, half_width), dtype)

    outs = (out(jnp.bfloat16, 2), out(jnp.float32))
    rows_type = jax.ShapeDtypeStruct((row_count, group_width), jnp.bfloat16)
    scratch = (pltpu.VMEM(query_proj.shape, jnp.bfloat16), pltpu.VMEM(back.shape, jnp.bfloat16))
    rows, give, keep = half_call(line_kernel, (rows_type,) + outs, sel, (query_proj, back), line, scratch)
    given = to_sibling(give)
    here = across_y((keep + given[0].astype(jnp.float32)).astype(jnp.bfloat16))
    give, keep = half_call(across_kernel, outs, sel, (rows,), line_x)
    given_x = to_sibling(give)
    there = across_y((keep + given_x[0].astype(jnp.float32)).astype(jnp.bfloat16))
    x_word = x.astype(jnp.int32)[None]
    so_far, part = home_products(sel, x_word, rows, given, given_x, here, line + line_x)
    return finish(x_word, part, there, so_far).reshape(query_proj.shape)


def solution(mesh):
    sizes = dict(mesh.shape)

    def per_device(query_proj, *rest):
        width = query_proj.shape[2]
        length = query_proj.shape[1] * sizes["ctx"]
        fits = sizes["ctx"] == 8 and sizes["ch"] == 4 and width == 1024 and length == 2048
        return (per_device_mesh if fits else per_device_plain)(query_proj, *rest)

    return jax.shard_map(
        per_device,
        mesh=mesh,
        in_specs=(
            P(None, "ctx", "ch"),
            P(None, "ctx", "ch"),
            P(None, "ctx", "ch"),
            P("ctx", "ch"),
            P("ch"),
            P("ch", "ctx"),
            P(),
            P(),
            P(None, "ctx"),
        ),
        out_specs=P(None, "ctx", "ch"),
        check_vma=False,
    )
```
